32 devices in a mesh: clip: 4 (over z), wide: 4 (over y, core), narrow: 2 (over x).
Axes of the slice: x: 2, y: 2, z: 4, core: 2. Of those that a mesh axis runs over, the one named last changes fastest.
Arguments:
- tokens: bfloat16 [4, 1024, 1536], P('clip', ('wide', 'narrow')), may hold values from -6 to 6
- positions: int32 [4, 1024], P('clip', ('wide', 'narrow')), may hold values from 0 to 1023, each once within a row
- captions: bfloat16 [4, 256, 4096], P('clip', 'narrow'), may hold values from -6 to 6
- caption_lengths: int32 [4], replicated, may hold values from 1 to 256, 640 in all
- conditioning: bfloat16 [4, 1024], P(None, ('clip', 'wide', 'narrow')), may hold values from -6 to 6
- modulation_weight: bfloat16 [1024, 9216], P(('clip', 'wide', 'narrow')), may hold values from -0.1875 to 0.1875
- modulation_bias: float32 [9216], replicated, may hold values from -3 to 3
- attention_gain: float32 [1536], replicated, may hold values from 0.5 to 1.5
- query_weight: bfloat16 [1536, 1536], P(('clip', 'wide', 'narrow')), may hold values from -0.15625 to 0.15625
- key_weight: bfloat16 [1536, 1536], P(('clip', 'wide', 'narrow')), may hold values from -0.15625 to 0.15625
- value_weight: bfloat16 [1536, 1536], P(('clip', 'wide', 'narrow')), may hold values from -0.15625 to 0.15625
- query_gain: float32 [64], replicated, may hold values from 0.5 to 1.5
- key_gain: float32 [64], replicated, may hold values from 0.5 to 1.5
- text_weight: bfloat16 [4096, 1536], P(('clip', 'wide', 'narrow')), may hold values from -0.09375 to 0.09375
- textkey_weight: bfloat16 [1536, 1536], P(('clip', 'wide', 'narrow')), may hold values from -0.15625 to 0.15625
- textvalue_weight: bfloat16 [1536, 1536], P(('clip', 'wide', 'narrow')), may hold values from -0.15625 to 0.15625
- textkey_gain: float32 [64], replicated, may hold values from 0.5 to 1.5
- cross_gate: float32 [24], replicated, may hold values from -0.25 to 0.25
- output_weight: bfloat16 [1536, 1536], P(('clip', 'wide', 'narrow')), may hold values from -4 to 4
- feedforward_gain: float32 [1536], replicated, may hold values from 0.5 to 1.5
- gate_weight: bfloat16 [1536, 4096], P(('clip', 'wide', 'narrow')), may hold values from -0.15625 to 0.15625
- up_weight: bfloat16 [1536, 4096], P(('clip', 'wide', 'narrow')), may hold values from -0.15625 to 0.15625
- down_weight: bfloat16 [4096, 1536], P(('clip', 'wide', 'narrow')), may hold values from -0.09375 to 0.09375
- cotangent: bfloat16 [4, 1024, 1536], P('clip', ('wide', 'narrow')), may hold values from -6 to 6
Outputs:
- block_output: float32 [4, 1024, 1536], P('clip', ('wide', 'narrow'))
- tokens_grad: float32 [4, 1024, 1536], P('clip', ('wide', 'narrow'))
- captions_grad: float32 [4, 256, 4096], P('clip', 'narrow')
- conditioning_grad: float32 [4, 1024], P(None, ('clip', 'wide', 'narrow'))
- modweight_grad: float32 [1024, 9216], P(('clip', 'wide', 'narrow'))
- modbias_grad: float32 [9216], replicated
- attngain_grad: float32 [1536], replicated
- queryweight_grad: float32 [1536, 1536], P(('clip', 'wide', 'narrow'))
- keyweight_grad: float32 [1536, 1536], P(('clip', 'wide', 'narrow'))
- valueweight_grad: float32 [1536, 1536], P(('clip', 'wide', 'narrow'))
- querygain_grad: float32 [64], replicated
- keygain_grad: float32 [64], replicated
- textweight_grad: float32 [4096, 1536], P(('clip', 'wide', 'narrow'))
- textkey_grad: float32 [1536, 1536], P(('clip', 'wide', 'narrow'))
- textvalue_grad: float32 [1536, 1536], P(('clip', 'wide', 'narrow'))
- textgain_grad: float32 [64], replicated
- crossgate_grad: float32 [24], replicated
- outweight_grad: float32 [1536, 1536], P(('clip', 'wide', 'narrow'))
- feedgain_grad: float32 [1536], replicated
- gateweight_grad: float32 [1536, 4096], P(('clip', 'wide', 'narrow'))
- upweight_grad: float32 [1536, 4096], P(('clip', 'wide', 'narrow'))
- downweight_grad: float32 [4096, 1536], P(('clip', 'wide', 'narrow'))
The draws below stay inside these ranges and needn't reach their ends.
Inputs may be any that keep to these rules, and one draw needn't show every extreme that they name: Each clip's positions are a permutation of 0 to 1023. `caption_lengths`: some clip has all 256 caption slots live.
All inputs are finite; a program needn't handle non-finite values.
Results may differ from the reference program's by a relative error of at most 0.025.
Values may be sent and summed in bfloat16 or wider, within the bound.
No kernel may reach another device: no remote copies, remote signals or barrier semaphores. Data moves between devices by JAX's collectives and lax.ppermute only.
A program may use at most 384 MiB of HBM per device.

```python
import math
import jax
import jax.numpy as jnp
import numpy as np
from jax import lax

D = 1536
H = 24
HD = 64
FF = 4096
TD = 4096
CD = 1024
CAP = 256
LEN = 1024
CLIPS = 4


def level_of(key, extent, cuts, least, top_value):
    loudness, own = 1.0, jax.random.fold_in(key, 6)
    for position, shards_of in cuts:
        heights = jnp.exp(jax.random.uniform(jax.random.fold_in(own, position), (shards_of,), jnp.float32, least / len(cuts), top_value / len(cuts)))
        loudness = loudness * jnp.repeat(heights, extent[position] // shards_of).reshape([-1 if axis == position else 1 for axis in range(len(extent))])
    return loudness


def profile(amount, total, reach, lean):
    portions = [(1 << 20) // math.isqrt(rank ** lean) + 1 for rank in range(2, amount + 1)]
    rest, holding = total - reach - (amount - 1), [1] * (amount - 1)
    while rest > 0:
        candidates = [i for i in range(amount - 1) if holding[i] < reach]
        mass, left = sum([portions[i] for i in candidates]), rest
        for i in candidates:
            extra = min(reach - holding[i], max(1, left * portions[i] // mass), rest)
            holding[i] = holding[i] + extra
            rest = rest - extra
    return np.array([reach] + holding)


def uneven(key, number_of, total, most, lean):
    if number_of == 2:
        one = jax.random.randint(key, (), max(1, total - most), min(most, total - 1) + 1)
        return jnp.stack([one, total - one])
    sizes = jnp.asarray(profile(number_of, total, most, lean), jnp.int32)
    pairs = (number_of - 1) // 2
    donor, sink = sizes[1:1 + 2 * pairs:2], sizes[2:2 + 2 * pairs:2]
    margin = jnp.minimum(donor - 1, most - sink)
    shifted = jax.random.randint(jax.random.fold_in(key, 1), (pairs,), 0, 1 << 20) % (margin + 1)
    sizes = sizes.at[1:1 + 2 * pairs:2].set(donor - shifted).at[2:2 + 2 * pairs:2].set(sink + shifted)
    return sizes[jax.random.permutation(jax.random.fold_in(key, 2), number_of)]


def gaussian(stream_key, shape, deviation, reach, shards=(), kind=jnp.bfloat16):
    entries = deviation * jax.random.normal(stream_key, shape, jnp.float32)
    if shards:
        entries = entries * level_of(stream_key, shape, shards, -0.22, 0.18)
    return jnp.clip(entries, -reach, reach).astype(kind)


def setup_inputs(seed: int = 0) -> dict:
    key_of = jax.random.split(jax.random.key(seed), 25)
    return {
        "tokens": gaussian(key_of[0], (CLIPS, LEN, D), 1.0, 6.0, ((0, 4), (1, 8))),
        "positions": jax.vmap(lambda own: jax.random.permutation(own, LEN))(jax.random.split(key_of[1], CLIPS)).reshape((CLIPS, LEN)).astype(jnp.int32),
        "captions": gaussian(key_of[2], (CLIPS, CAP, TD), 1.0, 6.0, ((0, 4), (1, 2))),
        "caption_lengths": uneven(key_of[3], CLIPS, CAP * 5 // 2, CAP, 0).astype(jnp.int32),
        "conditioning": gaussian(key_of[4], (CLIPS, CD), 1.0, 6.0, ((1, 32),)),
        "modulation_weight": gaussian(key_of[5], (CD, 6 * D), CD ** -0.5, 0.1875, ((0, 32),)),
        "modulation_bias": gaussian(key_of[6], (6 * D,), 0.5, 3.0, (), jnp.float32),
        "attention_gain": jnp.clip(1.0 + 0.1 * jax.random.normal(key_of[7], (D,), jnp.float32), 0.5, 1.5),
        "query_weight": gaussian(key_of[8], (D, D), D ** -0.5, 0.15625, ((0, 32),)),
        "key_weight": gaussian(key_of[9], (D, D), D ** -0.5, 0.15625, ((0, 32),)),
        "value_weight": gaussian(key_of[10], (D, D), D ** -0.5, 0.15625, ((0, 32),)),
        "query_gain": jnp.clip(1.0 + 0.1 * jax.random.normal(key_of[11], (HD,), jnp.float32), 0.5, 1.5),
        "key_gain": jnp.clip(1.0 + 0.1 * jax.random.normal(key_of[12], (HD,), jnp.float32), 0.5, 1.5),
        "text_weight": gaussian(key_of[13], (TD, D), TD ** -0.5, 0.09375, ((0, 32),)),
        "textkey_weight": gaussian(key_of[14], (D, D), D ** -0.5, 0.15625, ((0, 32),)),
        "textvalue_weight": gaussian(key_of[15], (D, D), D ** -0.5, 0.15625, ((0, 32),)),
        "textkey_gain": jnp.clip(1.0 + 0.1 * jax.random.normal(key_of[16], (HD,), jnp.float32), 0.5, 1.5),
        "cross_gate": jnp.clip(jax.random.uniform(key_of[17], (H,), jnp.float32, -0.25, 0.25), -0.25, 0.25),
        "output_weight": gaussian(key_of[18], (D, D), 1.0, 4.0, ((0, 32),)),
        "feedforward_gain": jnp.clip(1.0 + 0.1 * jax.random.normal(key_of[19], (D,), jnp.float32), 0.5, 1.5),
        "gate_weight": gaussian(key_of[20], (D, FF), D ** -0.5, 0.15625, ((0, 32),)),
        "up_weight": gaussian(key_of[21], (D, FF), D ** -0.5, 0.15625, ((0, 32),)),
        "down_weight": gaussian(key_of[22], (FF, D), FF ** -0.5, 0.09375, ((0, 32),)),
        "cotangent": gaussian(key_of[23], (CLIPS, LEN, D), 1.0, 6.0, ((0, 4), (1, 8))),
    }


@jax.custom_vjp
def low(v):
    return lax.optimization_barrier(v.astype(jnp.bfloat16)).astype(jnp.float32)

@jax.custom_vjp
def low_back(v):
    return v

def low_keep(v):
    return (low(v), None)

def low_pass(kept, grad):
    return (grad,)

def back_keep(v):
    return (v, None)

def back_low(kept, grad):
    return (low(grad),)
low.defvjp(low_keep, low_pass)
low_back.defvjp(back_keep, back_low)
EPSILON = 1e-06
ROPE_BASE = 10000.0
HIGHEST_PRECISION = lax.Precision.HIGHEST

def matmul(left, right):
    return jnp.dot(left, right, precision=HIGHEST_PRECISION, preferred_element_type=jnp.float32)

def rms_norm(values, gain):
    return values * lax.rsqrt(lax.optimization_barrier(jnp.mean(values * values, axis=-1, keepdims=True)) + EPSILON) * gain

def rope_tables(clip_positions):
    half_size = HD // 2
    frequency = jnp.exp(-math.log(ROPE_BASE) * 2.0 * jnp.arange(half_size, dtype=jnp.float32) / HD)
    angles = clip_positions.astype(jnp.float32)[:, None] * frequency[None, :]
    return (jnp.cos(angles)[:, None, :], jnp.sin(angles)[:, None, :])

def rotate(values, cosine_table, sine_table):
    half_size = values.shape[-1] // 2
    first_half = values[..., :half_size]
    second_half = values[..., half_size:]
    return jnp.concatenate([first_half * cosine_table - second_half * sine_table, first_half * sine_table + second_half * cosine_table], axis=-1)

def attend(queries, keys_all, values_all, text_keys, text_values, keep, text_gate):
    score_scale = HD ** (-0.5)
    score_shift = 3.0 * math.sqrt(HD)
    scores = low_back(jnp.einsum('thd,khd->htk', queries, keys_all, precision=HIGHEST_PRECISION) * score_scale)
    weights = jnp.exp(scores - score_shift)
    numer = low_back(jnp.einsum('htk,khd->thd', low(weights), values_all, precision=HIGHEST_PRECISION))
    denom = lax.optimization_barrier(jnp.sum(weights, axis=-1))
    own = numer / denom.T[:, :, None]
    text_scores = low_back(jnp.einsum('thd,khd->htk', queries, text_keys, precision=HIGHEST_PRECISION) * score_scale)
    text_weights = jnp.exp(text_scores - score_shift) * keep[None, None, :]
    text_numer = low_back(jnp.einsum('htk,khd->thd', low(text_weights), text_values, precision=HIGHEST_PRECISION))
    text_denom = lax.optimization_barrier(jnp.sum(text_weights, axis=-1))
    cross = text_numer / text_denom.T[:, :, None]
    return own + text_gate[None, :, None] * cross

def block_forward(positions, caption_lengths, tokens, captions, conditioning, modulation_weight, modulation_bias, attention_gain, query_weight, key_weight, value_weight, query_gain, key_gain, text_weight, textkey_weight, textvalue_weight, textkey_gain, cross_gate, output_weight, feedforward_gain, gate_weight, up_weight, down_weight):
    modulation = matmul(jax.nn.silu(conditioning), modulation_weight) + modulation_bias
    text_gate = jnp.tanh(cross_gate)
    query_rows = min(512, LEN)

    def one_clip(clip_inputs):
        clip_tokens, clip_caption, clip_mod, clip_positions, clip_length = clip_inputs
        shift_attn, scale_attn, gate_attn, shift_feed, scale_feed, gate_feed = jnp.split(clip_mod, 6)
        mod_in = low(rms_norm(clip_tokens, attention_gain) * (1.0 + scale_attn) + shift_attn)
        cosine_table, sine_table = rope_tables(clip_positions)
        query_raw = low_back(matmul(mod_in, query_weight)).reshape(LEN, H, HD)
        queries = low(rotate(rms_norm(query_raw, query_gain), cosine_table, sine_table))
        key_raw = low_back(matmul(mod_in, key_weight)).reshape(LEN, H, HD)
        keys_all = low(rotate(rms_norm(key_raw, key_gain), cosine_table, sine_table))
        values_all = low(low_back(matmul(mod_in, value_weight))).reshape(LEN, H, HD)
        text = low(low_back(matmul(clip_caption, text_weight)))
        text_keys = low(rms_norm(low_back(matmul(text, textkey_weight)).reshape(CAP, H, HD), textkey_gain))
        text_values = low(low_back(matmul(text, textvalue_weight))).reshape(CAP, H, HD)
        keep = (jnp.arange(CAP) < clip_length).astype(jnp.float32)
        query_blocks = queries.reshape(LEN // query_rows, query_rows, H, HD)

        def block_attend(query_block):
            return attend(query_block, keys_all, values_all, text_keys, text_values, keep, text_gate)
        mixed = lax.map(jax.checkpoint(block_attend), query_blocks).reshape(LEN, D)
        attn_out = low_back(matmul(low(mixed), output_weight))
        resid = clip_tokens + gate_attn * attn_out
        mod_ff = low(rms_norm(resid, feedforward_gain) * (1.0 + scale_feed) + shift_feed)
        gate_pre = low_back(matmul(mod_ff, gate_weight))
        up_pre = low_back(matmul(mod_ff, up_weight))
        inner = low(jax.nn.silu(gate_pre) * up_pre)
        feed_out = low_back(matmul(inner, down_weight))
        return resid + gate_feed * feed_out
    return lax.map(one_clip, (tokens, captions, modulation, positions, caption_lengths))

def reference(tokens, positions, captions, caption_lengths, conditioning, modulation_weight, modulation_bias, attention_gain, query_weight, key_weight, value_weight, query_gain, key_gain, text_weight, textkey_weight, textvalue_weight, textkey_gain, cross_gate, output_weight, feedforward_gain, gate_weight, up_weight, down_weight, cotangent):

    def layer(*inputs):
        return block_forward(positions, caption_lengths, *inputs)
    block_output, pullback = jax.vjp(layer, tokens.astype(jnp.float32), captions.astype(jnp.float32), conditioning.astype(jnp.float32), modulation_weight.astype(jnp.float32), modulation_bias.astype(jnp.float32), attention_gain.astype(jnp.float32), query_weight.astype(jnp.float32), key_weight.astype(jnp.float32), value_weight.astype(jnp.float32), query_gain.astype(jnp.float32), key_gain.astype(jnp.float32), text_weight.astype(jnp.float32), textkey_weight.astype(jnp.float32), textvalue_weight.astype(jnp.float32), textkey_gain.astype(jnp.float32), cross_gate.astype(jnp.float32), output_weight.astype(jnp.float32), feedforward_gain.astype(jnp.float32), gate_weight.astype(jnp.float32), up_weight.astype(jnp.float32), down_weight.astype(jnp.float32))
    tokens_grad, captions_grad, conditioning_grad, modweight_grad, modbias_grad, attngain_grad, queryweight_grad, keyweight_grad, valueweight_grad, querygain_grad, keygain_grad, textweight_grad, textkey_grad, textvalue_grad, textgain_grad, crossgate_grad, outweight_grad, feedgain_grad, gateweight_grad, upweight_grad, downweight_grad = pullback(cotangent.astype(jnp.float32))
    return (block_output, tokens_grad, captions_grad, conditioning_grad, modweight_grad, modbias_grad, attngain_grad, queryweight_grad, keyweight_grad, valueweight_grad, querygain_grad, keygain_grad, textweight_grad, textkey_grad, textvalue_grad, textgain_grad, crossgate_grad, outweight_grad, feedgain_grad, gateweight_grad, upweight_grad, downweight_grad)
```

```python
import math

import jax
import jax.numpy as jnp
from jax import lax
from jax.sharding import PartitionSpec as P

EPSILON = 1e-06
ROPE_BASE = 10000.0
C, W, N = "clip", "wide", "narrow"
ALL = (C, W, N)
PLANE = (W, N)
BF16, F32 = jnp.bfloat16, jnp.float32
HIGHEST = lax.Precision.HIGHEST


def dot(left, right, left_dim=1, right_dim=0):
    return lax.dot_general(
        left, right, (((left_dim,), (right_dim,)), ((), ())), preferred_element_type=F32
    )


def inverse_rms(values):
    return lax.rsqrt(jnp.mean(values * values, axis=-1, keepdims=True) + EPSILON)


def norm_backward(normed, inv_scale, gain, upstream):
    gain_grad = jnp.sum((upstream * normed).reshape(-1, normed.shape[-1]), axis=0)
    scaled = upstream * gain
    values_grad = inv_scale * (scaled - normed * jnp.mean(scaled * normed, axis=-1, keepdims=True))
    return (gain_grad, values_grad)


def rope_tables(positions, head_size):
    half_size = head_size // 2
    frequency = jnp.exp(-math.log(ROPE_BASE) * 2.0 * jnp.arange(half_size, dtype=F32) / head_size)
    angles = positions.astype(F32)[:, None] * frequency[None, :]
    return (jnp.cos(angles)[:, None, :], jnp.sin(angles)[:, None, :])


def rotate(values, cosine_table, sine_table):
    half_size = values.shape[-1] // 2
    first_half = values[..., :half_size]
    second_half = values[..., half_size:]
    return jnp.concatenate(
        [
            first_half * cosine_table - second_half * sine_table,
            first_half * sine_table + second_half * cosine_table,
        ],
        axis=-1,
    )


def axes_size(axes):
    return math.prod(lax.axis_size(axis) for axis in axes)


def swap(x, axes, mask):
    return lax.ppermute(x, axes, [(i, i ^ mask) for i in range(axes_size(axes))])


def pick(x, index, axis=0):
    return lax.dynamic_index_in_dim(x, index, axis, keepdims=False)


def spread(x, axes, masks):
    fast, first, second = masks
    me = lax.axis_index(axes)
    rows = x.shape[0]
    half = rows // 2
    one = swap(x, axes, first)
    two = swap(x, axes, second)
    if half:
        far = jnp.concatenate(
            [swap(two[:half], axes, first), swap(one[half:], axes, second)], axis=0
        )
    else:
        far = swap(two, axes, first)
    held = {0: x, first: one, second: two, first ^ second: far}
    for mask in (0, first, second, first ^ second):
        held[mask ^ fast] = swap(held[mask], axes, fast)
    out = jnp.zeros((len(held),) + x.shape, x.dtype)
    for mask, piece in held.items():
        out = lax.dynamic_update_index_in_dim(out, piece, me ^ mask, 0)
    return out


def collect(parts, axes, masks):
    fast, first, second = masks
    me = lax.axis_index(axes)
    rows = parts.shape[1]
    half = rows // 2

    def low(x):
        return x.astype(BF16)

    def part(mask):
        return pick(parts, me ^ mask)

    total = {}
    for mask in (first ^ second, first, second, 0):
        got = swap(low(part(mask ^ fast)), axes, fast)
        total[mask] = part(mask).astype(F32) + got.astype(F32)
    far, one, two, own = total[first ^ second], total[first], total[second], total[0]
    to_two = swap(low(far[:half]), axes, first)
    to_one = swap(low(far[half:]), axes, second)
    one_low = swap(low(one[:half]), axes, first)
    two_high = swap(low(two[half:]), axes, second)
    two_low = swap(low(two[:half] + to_two.astype(F32)), axes, second)
    one_high = swap(low(one[half:] + to_one.astype(F32)), axes, first)
    low_rows = own[:half] + one_low.astype(F32) + two_low.astype(F32)
    high_rows = own[half:] + one_high.astype(F32) + two_high.astype(F32)
    return jnp.concatenate([low_rows, high_rows], axis=0)


def small_sum(x, axes):
    count = axes_size(axes)
    if count > 8 or count & (count - 1):
        return lax.psum(x, axes)
    total = x
    for mask in range(1, count):
        total = total + swap(x, axes, mask)
    return total


def clip_rows(x, axes):
    count = axes_size(axes)
    if count > 8 or count & (count - 1):
        return lax.psum_scatter(x, axes, scatter_dimension=0, tiled=False)
    me = lax.axis_index(axes)
    total = pick(x, me).astype(F32)
    for mask in range(1, count):
        total = total + swap(pick(x, me ^ mask), axes, mask).astype(F32)
    return total


def clip_spread(x, axes):
    count = axes_size(axes)
    if count > 8 or count & (count - 1):
        return lax.all_gather(x, axes, axis=0, tiled=False)
    me = lax.axis_index(axes)
    out = jnp.zeros((count,) + x.shape, x.dtype)
    for mask in range(count):
        piece = swap(x, axes, mask) if mask else x
        out = lax.dynamic_update_index_in_dim(out, piece, me ^ mask, 0)
    return out


def turn(x, axes):
    return lax.all_to_all(x, axes, split_axis=0, concat_axis=0, tiled=False)


def on_device(
    tokens,
    positions,
    captions,
    caption_lengths,
    conditioning,
    modulation_weight,
    modulation_bias,
    attention_gain,
    query_weight,
    key_weight,
    value_weight,
    query_gain,
    key_gain,
    text_weight,
    textkey_weight,
    textvalue_weight,
    textkey_gain,
    cross_gate,
    output_weight,
    feedforward_gain,
    gate_weight,
    up_weight,
    down_weight,
    cotangent,
):
    wide_count, narrow_count = lax.axis_size(W), lax.axis_size(N)
    clip_count = lax.axis_size(C)
    clip_index, wide_index = lax.axis_index(C), lax.axis_index(W)
    own_rows, model_width = tokens.shape[1], tokens.shape[2]
    head_size = query_gain.shape[0]
    head_count = model_width // head_size
    score_scale = head_size ** (-0.5)
    score_shift = 3.0 * math.sqrt(head_size)
    split_tokens = head_count % (wide_count * narrow_count) != 0
    tp, dp = ((N,), (C, W)) if split_tokens else (PLANE, (C,))
    tp_count, dp_count = axes_size(tp), axes_size(dp)
    tp_index = lax.axis_index(tp)
    masks = (2, 1, 4)
    group_rows = own_rows * tp_count
    local_heads = head_count // tp_count
    head_width = local_heads * head_size
    weight_rows = query_weight.shape[0]
    hidden_rows, hidden_width = down_weight.shape[0], gate_weight.shape[1]
    local_hidden = hidden_width // tp_count

    cond_float = conditioning.astype(F32)
    cond_act = jax.nn.silu(cond_float)
    weight_float = modulation_weight.astype(F32)
    partial_mod = jnp.dot(cond_act, weight_float, precision=HIGHEST, preferred_element_type=F32)
    own_mod = small_sum(clip_rows(partial_mod, (C,)), PLANE) + modulation_bias
    shift_attn, scale_attn, gate_attn, shift_feed, scale_feed, gate_feed = jnp.split(own_mod, 6)

    def head_columns(weight):
        return weight.reshape(weight_rows, tp_count, head_width).transpose(1, 0, 2)

    def hidden_columns(weight):
        split = weight.reshape(weight_rows, dp_count, tp_count, hidden_rows)
        return split.transpose(2, 0, 1, 3).reshape(tp_count, weight_rows, local_hidden)

    def gather_rows(rows):
        return lax.all_gather(rows, dp, axis=0, tiled=True)

    qkv_parts = turn(
        jnp.concatenate([head_columns(w) for w in (query_weight, key_weight, value_weight)], axis=2), tp
    )
    qkv_slice = gather_rows(qkv_parts.reshape(tp_count * weight_rows, 3 * head_width))
    text_parts = turn(
        jnp.concatenate([head_columns(w) for w in (textkey_weight, textvalue_weight)], axis=2), tp
    ).reshape(tp_count * weight_rows, 2 * head_width)
    pieces = model_width // (2 * head_width)
    mixed_rows = jnp.concatenate(
        [text_parts, output_weight.reshape(weight_rows * pieces, 2 * head_width)], axis=0
    )
    mixed_all = gather_rows(mixed_rows).reshape(dp_count, mixed_rows.shape[0], 2 * head_width)
    text_slice = mixed_all[:, : tp_count * weight_rows].reshape(model_width, 2 * head_width)
    output_rows = mixed_all[:, tp_count * weight_rows :].reshape(dp_count * weight_rows, model_width)
    output_all = spread(output_rows, tp, masks).reshape(tp_count, dp_count, weight_rows, model_width)
    output_full = output_all.transpose(1, 0, 2, 3).reshape(model_width, model_width)
    hidden_parts = turn(
        jnp.concatenate([hidden_columns(gate_weight), hidden_columns(up_weight)], axis=2), tp
    )
    hidden_slice = gather_rows(hidden_parts.reshape(tp_count * weight_rows, 2 * local_hidden))
    down_slice = gather_rows(down_weight)

    token_all = spread(tokens[0], tp, masks).reshape(group_rows, model_width)
    cotangent_all = spread(cotangent[0], tp, masks).reshape(group_rows, model_width)
    position_all = spread(positions, tp, masks).reshape(group_rows)

    token_float = tokens[0].astype(F32)
    inv_attn = inverse_rms(token_float)
    hat_attn = token_float * inv_attn
    normed_attn = hat_attn * attention_gain
    group_float = token_all.astype(F32)
    group_normed = group_float * inverse_rms(group_float) * attention_gain
    mod_in = (group_normed * (1.0 + scale_attn) + shift_attn).astype(BF16)

    caption_rows, text_width = captions.shape[1], captions.shape[2]
    text_rows = text_weight.shape[0]
    own_columns = pick(
        captions[0].reshape(caption_rows, clip_count, wide_count, narrow_count, text_rows), wide_index, 2
    )
    caption_parts = own_columns.transpose(1, 2, 0, 3).reshape(-1, caption_rows, text_rows)
    caption_columns = turn(caption_parts, (C, N)).reshape(-1, text_rows)
    slot_count = caption_rows * narrow_count
    slot_part = slot_count // tp_count
    text_partial = dot(caption_columns, text_weight).reshape(clip_count, tp_count, slot_part, model_width)
    text_group = collect(
        text_partial.transpose(1, 0, 2, 3).reshape(tp_count, clip_count * slot_part, model_width), tp, masks
    )
    if split_tokens:
        text_group = lax.psum(text_group, W)
    text_own = clip_rows(text_group.astype(BF16).reshape(clip_count, slot_part, model_width), (C,))
    text_proj = spread(text_own.astype(BF16), tp, masks).reshape(slot_count, model_width)

    heads_shape = (group_rows, local_heads, head_size)
    cosine_table, sine_table = rope_tables(position_all, head_size)
    qkv_raw = dot(mod_in, qkv_slice)
    query_raw = qkv_raw[:, :head_width].reshape(heads_shape)
    key_raw = qkv_raw[:, head_width : 2 * head_width].reshape(heads_shape)
    value_heads = qkv_raw[:, 2 * head_width :].astype(BF16).reshape(heads_shape)
    inv_query = inverse_rms(query_raw)
    hat_query = query_raw * inv_query
    query_rot = rotate(hat_query * query_gain, cosine_table, sine_table).astype(BF16)
    inv_key = inverse_rms(key_raw)
    hat_key = key_raw * inv_key
    key_rot = rotate(hat_key * key_gain, cosine_table, sine_table).astype(BF16)
    if split_tokens:
        keys_all = lax.all_gather(key_rot, W, axis=0, tiled=True)
        values_all = lax.all_gather(value_heads, W, axis=0, tiled=True)
    else:
        keys_all, values_all = key_rot, value_heads

    text_heads = (slot_count, local_heads, head_size)
    text_raw = dot(text_proj, text_slice)
    tkey_raw = text_raw[:, :head_width].reshape(text_heads)
    inv_tkey = inverse_rms(tkey_raw)
    hat_tkey = tkey_raw * inv_tkey
    text_key = (hat_tkey * textkey_gain).astype(BF16)
    text_value = text_raw[:, head_width:].astype(BF16).reshape(text_heads)
    keep_mask = (jnp.arange(slot_count) < caption_lengths[clip_index]).astype(F32)

    def scores_of(left, right):
        return jnp.einsum("thd,khd->htk", left, right, preferred_element_type=F32)

    def gather_of(weights, right):
        return jnp.einsum("htk,khd->thd", weights, right, preferred_element_type=F32)

    def scatter_of(weights, left):
        return jnp.einsum("htk,thd->khd", weights, left, preferred_element_type=F32)

    own_wts = jnp.exp(scores_of(query_rot, keys_all) * score_scale - score_shift)
    denom = jnp.sum(own_wts, axis=-1)
    own_out = gather_of(own_wts.astype(BF16), values_all) / denom.T[:, :, None]
    cross_wts = jnp.exp(scores_of(query_rot, text_key) * score_scale - score_shift) * keep_mask
    text_denom = jnp.sum(cross_wts, axis=-1)
    cross_out = gather_of(cross_wts.astype(BF16), text_value) / text_denom.T[:, :, None]
    text_gate = pick(jnp.tanh(cross_gate).reshape(tp_count, local_heads), tp_index)
    mixed = (own_out + text_gate[None, :, None] * cross_out).astype(BF16)

    mixed_parts = turn(mixed.reshape(tp_count, own_rows, head_width), tp)
    mixed_own = mixed_parts.transpose(1, 0, 2).reshape(own_rows, model_width)
    attn_out = dot(mixed_own, output_full)
    resid = token_float + gate_attn * attn_out
    inv_feed = inverse_rms(resid)
    hat_feed = resid * inv_feed
    normed_feed = hat_feed * feedforward_gain
    mod_own = (normed_feed * (1.0 + scale_feed) + shift_feed).astype(BF16)
    mod_ff = spread(mod_own, tp, masks).reshape(group_rows, model_width)

    hidden_pre = dot(mod_ff, hidden_slice)
    gate_pre, up_pre = hidden_pre[:, :local_hidden], hidden_pre[:, local_hidden:]
    sigmoid_gate = jax.nn.sigmoid(gate_pre)
    silu_gate = gate_pre * sigmoid_gate
    inner = (silu_gate * up_pre).astype(BF16)
    dfeed = (gate_feed * cotangent_all.astype(F32)).astype(BF16)
    dinner = dot(dfeed, down_slice, 1, 1)
    dgate_pre = (dinner * up_pre * (sigmoid_gate * (1.0 + gate_pre * (1.0 - sigmoid_gate)))).astype(BF16)
    dup_pre = (dinner * silu_gate).astype(BF16)
    dhidden = jnp.concatenate([dgate_pre, dup_pre], axis=1)
    dmod_parts = dot(dhidden, hidden_slice, 1, 1).reshape(tp_count, own_rows, model_width)
    dmod_ff = collect(dmod_parts, tp, masks)
    feed_parts = dot(inner, down_slice).reshape(tp_count, own_rows, model_width)
    feed_out = collect(feed_parts, tp, masks)

    def scatter_rows(grads):
        return lax.psum_scatter(grads.astype(BF16), dp, scatter_dimension=0, tiled=True)

    dhidden_rows = scatter_rows(dot(mod_ff, dhidden, 0, 0))
    downweight_grad = scatter_rows(dot(inner, dfeed, 0, 0)).astype(F32)

    block_output = resid + gate_feed * feed_out
    dout = cotangent[0].astype(F32)
    dgate_feed = jnp.sum(dout * feed_out, axis=0)
    dshift_feed = jnp.sum(dmod_ff, axis=0)
    dscale_feed = jnp.sum(dmod_ff * normed_feed, axis=0)
    dfeed_gain, dresid_norm = norm_backward(
        hat_feed, inv_feed, feedforward_gain, dmod_ff * (1.0 + scale_feed)
    )
    dresid = dout + dresid_norm
    dgate_attn = jnp.sum(dresid * attn_out, axis=0)
    dattn = (gate_attn * dresid).astype(BF16)

    dmixed_own = dot(dattn, output_full, 1, 1).astype(BF16)
    dmixed_parts = dmixed_own.reshape(own_rows, tp_count, head_width).transpose(1, 0, 2)
    dmixed = turn(dmixed_parts, tp).reshape(heads_shape).astype(F32)
    dout_parts = dot(mixed_own, dattn, 0, 0).reshape(dp_count, tp_count, weight_rows, model_width)
    dout_group = collect(
        dout_parts.transpose(1, 0, 2, 3).reshape(tp_count, dp_count * weight_rows, model_width), tp, masks
    )
    outweight_grad = clip_rows(
        dout_group.astype(BF16).reshape(dp_count, weight_rows, model_width), dp
    ).astype(F32)

    dcross_out = dmixed * text_gate[None, :, None]
    dcross_gate = jnp.sum(dmixed * cross_out, axis=(0, 2)) * (1.0 - text_gate * text_gate)
    dlevel_cross = -jnp.sum(dcross_out * cross_out, axis=-1) / text_denom.T
    dnumer_cross = (dcross_out / text_denom.T[:, :, None]).astype(BF16)
    cross_dscores = (
        cross_wts * (scores_of(dnumer_cross, text_value) + dlevel_cross.T[:, :, None])
    ).astype(BF16)
    dquery_cross = gather_of(cross_dscores, text_key)
    dtext_keys = scatter_of(cross_dscores, query_rot) * score_scale
    dtext_values = scatter_of(cross_wts.astype(BF16), dnumer_cross)
    if split_tokens:
        dtext_keys = lax.psum(dtext_keys, W)
        dtext_values = lax.psum(dtext_values, W)
    dtkey_gain, dtkey_raw = norm_backward(hat_tkey, inv_tkey, textkey_gain, dtext_keys)
    dtext_heads = jnp.concatenate(
        [
            dtkey_raw.astype(BF16).reshape(slot_count, head_width),
            dtext_values.astype(BF16).reshape(slot_count, head_width),
        ],
        axis=1,
    )
    dtext_group = collect(
        dot(dtext_heads, text_slice, 1, 1).reshape(tp_count, slot_part, model_width), tp, masks
    ).astype(BF16)
    dtext_clips = clip_spread(dtext_group, (C,)).reshape(clip_count * slot_part, model_width)
    dtext_all = (
        spread(dtext_clips, tp, masks)
        .reshape(tp_count, clip_count, slot_part, model_width)
        .transpose(1, 0, 2, 3)
        .reshape(clip_count * slot_count, model_width)
    )
    textweight_grad = dot(caption_columns, dtext_all, 0, 0)
    dcaption_parts = (
        dot(dtext_all, text_weight, 1, 1).astype(BF16).reshape(-1, caption_rows, text_rows)
    )
    dcaption_own = turn(dcaption_parts, (C, N))
    dcaption_wide = lax.all_gather(dcaption_own, W, axis=0, tiled=False)
    captions_grad = (
        dcaption_wide.reshape(wide_count, clip_count, narrow_count, caption_rows, text_rows)
        .transpose(3, 1, 0, 2, 4)
        .reshape(caption_rows, text_width)
        .astype(F32)
    )

    dlevel_self = -jnp.sum(dmixed * own_out, axis=-1) / denom.T
    dnumer_self = (dmixed / denom.T[:, :, None]).astype(BF16)
    dscores = (own_wts * (scores_of(dnumer_self, values_all) + dlevel_self.T[:, :, None])).astype(BF16)
    dquery_self = gather_of(dscores, keys_all)
    dkey = scatter_of(dscores, query_rot) * score_scale
    dvalue = scatter_of(own_wts.astype(BF16), dnumer_self)
    if split_tokens:
        dkey = lax.psum_scatter(dkey.astype(BF16), W, scatter_dimension=0, tiled=True).astype(F32)
        dvalue = lax.psum_scatter(dvalue.astype(BF16), W, scatter_dimension=0, tiled=True)
    dquery = rotate((dquery_self + dquery_cross) * score_scale, cosine_table, -sine_table)
    dquery_gain, dquery_raw = norm_backward(hat_query, inv_query, query_gain, dquery)
    dkey_gain, dkey_raw = norm_backward(hat_key, inv_key, key_gain, rotate(dkey, cosine_table, -sine_table))
    dqkv = jnp.concatenate(
        [x.astype(BF16).reshape(group_rows, head_width) for x in (dquery_raw, dkey_raw, dvalue)], axis=1
    )
    dmod_in = collect(dot(dqkv, qkv_slice, 1, 1).reshape(tp_count, own_rows, model_width), tp, masks)
    shared = 1.0 / wide_count if split_tokens else 1.0
    dhead_rows = scatter_rows(
        jnp.concatenate([dot(mod_in, dqkv, 0, 0), dot(text_proj, dtext_heads, 0, 0) * shared], axis=1)
    )

    dhead_parts = turn(dhead_rows.reshape(tp_count, weight_rows, 5 * head_width), tp)
    dhead_split = dhead_parts.reshape(tp_count, weight_rows, 5, head_width).transpose(2, 1, 0, 3)
    head_grads = dhead_split.reshape(5, weight_rows, model_width).astype(F32)
    dhidden_parts = turn(dhidden_rows.reshape(tp_count, weight_rows, 2 * local_hidden), tp)
    hidden_grads = (
        dhidden_parts.reshape(tp_count, weight_rows, 2, dp_count, hidden_rows)
        .transpose(2, 1, 3, 0, 4)
        .reshape(2, weight_rows, hidden_width)
        .astype(F32)
    )

    dshift_attn = jnp.sum(dmod_in, axis=0)
    dscale_attn = jnp.sum(dmod_in * normed_attn, axis=0)
    dattn_gain, dtokens_norm = norm_backward(
        hat_attn, inv_attn, attention_gain, dmod_in * (1.0 + scale_attn)
    )
    tokens_grad = dresid + dtokens_norm

    dgate_rows = jnp.zeros((tp_count, local_heads), F32)
    dgate_rows = lax.dynamic_update_index_in_dim(dgate_rows, dcross_gate, tp_index, 0).reshape(-1)
    pad = -head_count % head_size
    small = jnp.concatenate(
        [
            dshift_attn,
            dscale_attn,
            dgate_attn,
            dshift_feed,
            dscale_feed,
            dgate_feed,
            dattn_gain,
            dfeed_gain,
            dquery_gain,
            dkey_gain,
            dtkey_gain * shared,
            dgate_rows,
            jnp.zeros((pad,), F32),
        ]
    )
    clip_small = clip_spread(small_sum(small, PLANE), (C,))
    mod_width = 6 * model_width
    dmod_all = clip_small[:, :mod_width]
    gains = jnp.sum(clip_small[:, mod_width:], axis=0)
    attngain_grad, feedgain_grad = gains[:model_width], gains[model_width : 2 * model_width]
    rest = gains[2 * model_width :]
    querygain_grad, keygain_grad, textgain_grad = (
        rest[:head_size],
        rest[head_size : 2 * head_size],
        rest[2 * head_size : 3 * head_size],
    )
    crossgate_grad = rest[3 * head_size : 3 * head_size + head_count]
    modweight_grad = jnp.dot(cond_act.T, dmod_all, precision=HIGHEST, preferred_element_type=F32)
    dcond_act = jnp.dot(dmod_all, weight_float.T, precision=HIGHEST, preferred_element_type=F32)
    sigmoid_cond = jax.nn.sigmoid(cond_float)
    conditioning_grad = dcond_act * sigmoid_cond * (1.0 + cond_float * (1.0 - sigmoid_cond))
    modbias_grad = jnp.sum(dmod_all, axis=0)
    return (
        block_output[None],
        tokens_grad[None],
        captions_grad[None],
        conditioning_grad,
        modweight_grad,
        modbias_grad,
        attngain_grad,
        head_grads[0],
        head_grads[1],
        head_grads[2],
        querygain_grad,
        keygain_grad,
        textweight_grad,
        head_grads[3],
        head_grads[4],
        textgain_grad,
        crossgate_grad,
        outweight_grad,
        feedgain_grad,
        hidden_grads[0],
        hidden_grads[1],
        downweight_grad,
    )


def solution(mesh):
    rows, whole = P(ALL, None), P()
    tokens, captions = P(C, PLANE, None), P(C, N, None)
    columns = P(None, ALL)
    return jax.shard_map(
        on_device,
        mesh=mesh,
        in_specs=(
            tokens,
            P(C, PLANE),
            captions,
            whole,
            columns,
            rows,
            whole,
            whole,
            rows,
            rows,
            rows,
            whole,
            whole,
            rows,
            rows,
            rows,
            whole,
            whole,
            rows,
            whole,
            rows,
            rows,
            rows,
            tokens,
        ),
        out_specs=(
            tokens,
            tokens,
            captions,
            columns,
            rows,
            whole,
            whole,
            rows,
            rows,
            rows,
            whole,
            whole,
            rows,
            rows,
            rows,
            whole,
            whole,
            rows,
            whole,
            rows,
            rows,
            rows,
        ),
        check_vma=False,
    )
```

```python
import functools
import math

import jax
import jax.numpy as jnp
from jax import lax
from jax.experimental import pallas as pl
from jax.experimental.pallas import tpu as pltpu
from jax.sharding import PartitionSpec as P

EPSILON = 1e-06
ROPE_BASE = 10000.0
C, W, N = "clip", "wide", "narrow"
ALL = (C, W, N)
PLANE = (W, N)
BF16, F32 = jnp.bfloat16, jnp.float32
HIGHEST = lax.Precision.HIGHEST


def dot(left, right, left_dim=1, right_dim=0):
    return lax.dot_general(
        left, right, (((left_dim,), (right_dim,)), ((), ())), preferred_element_type=F32
    )


def inverse_rms(values):
    return lax.rsqrt(jnp.mean(values * values, axis=-1, keepdims=True) + EPSILON)


def norm_backward(normed, inv_scale, gain, upstream):
    gain_grad = jnp.sum((upstream * normed).reshape(-1, normed.shape[-1]), axis=0)
    scaled = upstream * gain
    values_grad = inv_scale * (scaled - normed * jnp.mean(scaled * normed, axis=-1, keepdims=True))
    return (gain_grad, values_grad)


def rope_tables(positions, head_size):
    half_size = head_size // 2
    frequency = jnp.exp(-math.log(ROPE_BASE) * 2.0 * jnp.arange(half_size, dtype=F32) / head_size)
    angles = positions.astype(F32)[:, None] * frequency[None, :]
    cosine, sine = jnp.cos(angles), jnp.sin(angles)
    return (jnp.concatenate([cosine, cosine], axis=1), jnp.concatenate([-sine, sine], axis=1))


def swap_halves(values):
    half_size = values.shape[1] // 2
    return jnp.concatenate([values[:, half_size:], values[:, :half_size]], axis=1)


def full_spec(shape):
    return pl.BlockSpec(shape, lambda *_: (0,) * len(shape))


def row_spec(rows, width):
    return pl.BlockSpec((rows, width), lambda i, *_: (i, 0))


def struct(shape, dtype):
    return jax.ShapeDtypeStruct(shape, dtype)


def head_parts(width, size):
    return [slice(at, at + size) for at in range(0, width, size)]


def prepare_body(raw_ref, cos_ref, sin_ref, query_gain_ref, key_gain_ref, query_ref, key_ref, value_ref):
    width, size = query_ref.shape[1], query_gain_ref.shape[1]
    raw, cosine, sine = raw_ref[...], cos_ref[...], sin_ref[...]
    for out_ref, gain, base in ((query_ref, query_gain_ref[...], 0), (key_ref, key_gain_ref[...], width)):
        heads = []
        for part in head_parts(width, size):
            head = raw[:, base + part.start : base + part.stop]
            head = head * inverse_rms(head) * gain
            heads.append(head * cosine + swap_halves(head) * sine)
        out_ref[...] = jnp.concatenate(heads, axis=1).astype(BF16)
    value_ref[...] = raw[:, 2 * width :].astype(BF16)


def prepare(raw, cosine, sine, query_gain, key_gain, width):
    rows, size = raw.shape[0], cosine.shape[1]
    block = math.gcd(rows, 256)
    return pl.pallas_call(
        prepare_body,
        grid=(rows // block,),
        in_specs=[
            row_spec(block, raw.shape[1]),
            row_spec(block, size),
            row_spec(block, size),
            full_spec((1, size)),
            full_spec((1, size)),
        ],
        out_specs=[row_spec(block, width)] * 3,
        out_shape=[struct((rows, width), BF16)] * 3,
        name="prepare",
    )(raw, cosine, sine, query_gain[None], key_gain[None])


def prepare_text_body(raw_ref, gain_ref, key_ref, value_ref):
    width, size = key_ref.shape[1], gain_ref.shape[1]
    raw, gain = raw_ref[...], gain_ref[...]
    heads = [raw[:, part] for part in head_parts(width, size)]
    heads = [head * inverse_rms(head) * gain for head in heads]
    key_ref[...] = jnp.concatenate(heads, axis=1).astype(BF16)
    value_ref[...] = raw[:, width:].astype(BF16)


def prepare_text(raw, gain, width):
    return pl.pallas_call(
        prepare_text_body, out_shape=[struct((raw.shape[0], width), BF16)] * 2, name="prepare_text"
    )(raw, gain[None])


def weights_of(left, right, factor, offset):
    scores = lax.dot_general(left, right, (((1,), (1,)), ((), ())), preferred_element_type=F32)
    return jnp.exp2(scores * factor - offset)


def attend_body(
    order_ref,
    query_ref,
    key_ref,
    value_ref,
    text_key_ref,
    text_value_ref,
    keep_ref,
    gate_ref,
    mixed_ref,
    own_ref,
    cross_ref,
    denom_ref,
    text_denom_ref,
    *,
    size,
    factor,
    offset,
):
    rows, width = query_ref.shape
    part_rows = mixed_ref.shape[1]
    keep = keep_ref[...]
    results = []
    for part in head_parts(width, size):
        query = query_ref[:, part]
        wts = weights_of(query, key_ref[:, part], factor, offset)
        denom = jnp.sum(wts, axis=1, keepdims=True)
        own = dot(wts.astype(BF16), value_ref[:, part]) / denom
        text_wts = weights_of(query, text_key_ref[:, part], factor, offset) * keep
        text_denom = jnp.sum(text_wts, axis=1, keepdims=True)
        cross = dot(text_wts.astype(BF16), text_value_ref[:, part]) / text_denom
        shape = (rows, size)
        results.append(
            (own, cross, jnp.broadcast_to(denom, shape), jnp.broadcast_to(text_denom, shape))
        )
    own, cross, denom, text_denom = (jnp.concatenate(heads, axis=1) for heads in zip(*results))
    own_ref[...], cross_ref[...], denom_ref[...], text_denom_ref[...] = own, cross, denom, text_denom
    mixed = (own + gate_ref[...] * cross).astype(BF16)
    first = pl.program_id(0) * (rows // part_rows)
    for index in range(rows // part_rows):
        mixed_ref[order_ref[first + index]] = mixed[index * part_rows : (index + 1) * part_rows]


def attend(order, query, keys, values, text_key, text_value, keep, gate, size):
    rows, width = query.shape
    slots = text_key.shape[0]
    part_rows = rows // order.shape[0]
    block = part_rows * math.gcd(order.shape[0], max(1, 256 // part_rows))
    body = functools.partial(
        attend_body, size=size, factor=size**-0.5 / math.log(2.0), offset=3.0 * size**0.5 / math.log(2.0)
    )
    return pl.pallas_call(
        body,
        grid_spec=pltpu.PrefetchScalarGridSpec(
            num_scalar_prefetch=1,
            grid=(rows // block,),
            in_specs=[
                row_spec(block, width),
                full_spec(keys.shape),
                full_spec(values.shape),
                full_spec((slots, width)),
                full_spec((slots, width)),
                full_spec((1, slots)),
                full_spec((1, width)),
            ],
            out_specs=[full_spec((order.shape[0], part_rows, width))] + [row_spec(block, width)] * 4,
        ),
        out_shape=[struct((order.shape[0], part_rows, width), BF16)] + [struct((rows, width), F32)] * 4,
        name="attend",
    )(order, query, keys, values, text_key, text_value, keep[None], gate[None])


def attend_back_body(
    order_ref, query_ref, out_ref, denom_ref, dmixed_ref, key_ref, value_ref, *refs, size, factor, offset, text
):
    if text:
        keep_ref, gate_ref, dquery_ref, dkey_ref, dvalue_ref, dgate_ref = refs
    else:
        start_ref, dquery_ref, dkey_ref, dvalue_ref = refs
    rows, width = query_ref.shape
    part_rows = dmixed_ref.shape[1]
    step = pl.program_id(0)
    first = step * (rows // part_rows)
    dmixed = jnp.concatenate(
        [dmixed_ref[order_ref[first + index]] for index in range(rows // part_rows)], axis=0
    ).astype(F32)
    out, inv = out_ref[...], 1.0 / denom_ref[...]

    @pl.when(step == 0)
    def _():
        dkey_ref[...] = jnp.zeros_like(dkey_ref)
        dvalue_ref[...] = jnp.zeros_like(dvalue_ref)
        if text:
            dgate_ref[...] = jnp.zeros_like(dgate_ref)

    if text:
        dgate_ref[...] += jnp.sum(dmixed * out, axis=0, keepdims=True)
        dmixed = dmixed * gate_ref[...]
    dnumer = (dmixed * inv).astype(BF16)
    level = -(dmixed * out * inv)
    scale = size**-0.5
    results = []
    for part in head_parts(width, size):
        query, keys, numer = query_ref[:, part], key_ref[:, part], dnumer[:, part]
        column = jnp.sum(level[:, part], axis=1, keepdims=True)
        level_row = jnp.broadcast_to(column, (rows, 128)).T[:1]
        wts = weights_of(keys, query, factor, offset)
        if text:
            wts = wts * keep_ref[...]
        dwts = lax.dot_general(
            value_ref[:, part], numer, (((1,), (1,)), ((), ())), preferred_element_type=F32
        )
        dscores = (wts * (dwts + level_row)).astype(BF16)
        dquery = (dot(keys.T, dscores) * scale).T
        results.append((dquery, dot(dscores, query) * scale, dot(wts.astype(BF16), numer)))
    dquery, dkey, dvalue = (jnp.concatenate(heads, axis=1) for heads in zip(*results))
    dquery_ref[...] = dquery if text else dquery + start_ref[...]
    dkey_ref[...] += dkey
    dvalue_ref[...] += dvalue


def attend_back(order, query, out, denom, dmixed, keys, values, size, text=None, start=None):
    rows, width = query.shape
    slots = keys.shape[0]
    part_rows = rows // order.shape[0]
    block = part_rows * math.gcd(order.shape[0], max(1, 256 // part_rows))
    body = functools.partial(
        attend_back_body,
        size=size,
        factor=size**-0.5 / math.log(2.0),
        offset=3.0 * size**0.5 / math.log(2.0),
        text=text is not None,
    )
    if text is None:
        extra, extra_specs = (start,), [row_spec(block, width)]
    else:
        extra, extra_specs = (text[0][:, None], text[1][None]), [full_spec((slots, 1)), full_spec((1, width))]
    ends = [] if text is None else [(1, width)]
    return pl.pallas_call(
        body,
        grid_spec=pltpu.PrefetchScalarGridSpec(
            num_scalar_prefetch=1,
            grid=(rows // block,),
            in_specs=[row_spec(block, width)] * 3
            + [full_spec(dmixed.shape), full_spec(keys.shape), full_spec(keys.shape)]
            + extra_specs,
            out_specs=[row_spec(block, width)]
            + [full_spec(keys.shape)] * 2
            + [full_spec(shape) for shape in ends],
        ),
        out_shape=[struct((rows, width), F32)]
        + [struct(keys.shape, F32)] * 2
        + [struct(shape, F32) for shape in ends],
        name="text_back" if text else "attend_back",
    )(order, query, out, denom, dmixed, keys, values, *extra)


def norm_heads_back(raw, upstream, gain, size):
    gain_grad, grads = 0.0, []
    for part in head_parts(raw.shape[1], size):
        head, grad = raw[:, part], upstream[part.start // size]
        inv = inverse_rms(head)
        hat = head * inv
        gain_grad = gain_grad + jnp.sum(grad * hat, axis=0, keepdims=True)
        scaled = grad * gain
        grads.append(inv * (scaled - hat * jnp.mean(scaled * hat, axis=1, keepdims=True)))
    return gain_grad, jnp.concatenate(grads, axis=1)


def finish_body(
    raw_ref, dquery_ref, dkey_ref, dvalue_ref, cos_ref, sin_ref, query_gain_ref, key_gain_ref, out_ref, gain_ref
):
    width, size = dquery_ref.shape[1], query_gain_ref.shape[1]
    cosine, sine = cos_ref[...], sin_ref[...]

    @pl.when(pl.program_id(0) == 0)
    def _():
        gain_ref[...] = jnp.zeros_like(gain_ref)

    gains, outs = [], []
    for grad_ref, gain, base in ((dquery_ref, query_gain_ref[...], 0), (dkey_ref, key_gain_ref[...], width)):
        upstream = []
        for part in head_parts(width, size):
            grad = grad_ref[:, part].astype(F32)
            upstream.append(grad * cosine - swap_halves(grad) * sine)
        gain_grad, grads = norm_heads_back(raw_ref[:, base : base + width], upstream, gain, size)
        gains.append(gain_grad)
        outs.append(grads.astype(BF16))
    out_ref[...] = jnp.concatenate(outs + [dvalue_ref[...].astype(BF16)], axis=1)
    gain_ref[...] += jnp.concatenate(gains, axis=0)


def finish(raw, dquery, dkey, dvalue, cosine, sine, query_gain, key_gain):
    rows, width = dquery.shape
    size = cosine.shape[1]
    block = math.gcd(rows, 256)
    return pl.pallas_call(
        finish_body,
        grid=(rows // block,),
        in_specs=[row_spec(block, 3 * width)]
        + [row_spec(block, width)] * 3
        + [row_spec(block, size)] * 2
        + [full_spec((1, size))] * 2,
        out_specs=[row_spec(block, 3 * width), full_spec((2, size))],
        out_shape=[struct((rows, 3 * width), BF16), struct((2, size), F32)],
        name="finish",
    )(raw, dquery, dkey, dvalue, cosine, sine, query_gain[None], key_gain[None])


def finish_text_body(raw_ref, dkey_ref, dvalue_ref, gain_in_ref, out_ref, gain_ref):
    width, size = dkey_ref.shape[1], gain_in_ref.shape[1]
    upstream = [dkey_ref[:, part] for part in head_parts(width, size)]
    gain_ref[...], grads = norm_heads_back(raw_ref[:, :width], upstream, gain_in_ref[...], size)
    out_ref[...] = jnp.concatenate([grads.astype(BF16), dvalue_ref[...].astype(BF16)], axis=1)


def finish_text(raw, dkey, dvalue, gain):
    return pl.pallas_call(
        finish_text_body,
        out_shape=[struct(raw.shape, BF16), struct((1, gain.shape[0]), F32)],
        name="finish_text",
    )(raw, dkey, dvalue, gain[None])


def join_body(parts_ref, *outs, width):
    for index, out_ref in enumerate(outs):
        for turn_index in range(parts_ref.shape[0]):
            at = turn_index * width
            out_ref[:, at : at + width] = parts_ref[turn_index, :, index * width : (index + 1) * width].astype(F32)


def join_heads(parts, width):
    count, rows, total = parts.shape
    return pl.pallas_call(
        functools.partial(join_body, width=width),
        out_shape=[struct((rows, count * width), F32)] * (total // width),
        name="join_heads",
    )(parts)


def join_hidden_body(parts_ref, gate_ref, up_ref, *, groups, width):
    count = parts_ref.shape[0]
    for index, out_ref in enumerate((gate_ref, up_ref)):
        for group in range(groups):
            for turn_index in range(count):
                at = (group * count + turn_index) * width
                source = (index * groups + group) * width
                out_ref[:, at : at + width] = parts_ref[turn_index, :, source : source + width].astype(F32)


def join_hidden(parts, groups, width):
    count, rows, _ = parts.shape
    return pl.pallas_call(
        functools.partial(join_hidden_body, groups=groups, width=width),
        out_shape=[struct((rows, groups * count * width), F32)] * 2,
        name="join_hidden",
    )(parts)


def join_captions_body(order_ref, *refs, groups, inner):
    *pieces, out_ref = refs
    width = pieces[0].shape[2]
    for at, piece in enumerate(pieces):
        for group in range(groups):
            for index in range(inner):
                column = ((group * len(pieces) + order_ref[at]) * inner + index) * width
                out_ref[:, pl.ds(pl.multiple_of(column, width), width)] = piece[group * inner + index].astype(F32)


def join_captions(pieces, order, groups, inner):
    count, rows, width = pieces[0].shape
    if width % 128:
        full = jnp.zeros((len(pieces),) + pieces[0].shape, pieces[0].dtype)
        for at, piece in enumerate(pieces):
            full = lax.dynamic_update_index_in_dim(full, piece, order[at], 0)
        full = full.reshape(len(pieces), groups, inner, rows, width).transpose(3, 1, 0, 2, 4)
        return full.reshape(rows, -1).astype(F32)
    return pl.pallas_call(
        functools.partial(join_captions_body, groups=groups, inner=inner),
        grid_spec=pltpu.PrefetchScalarGridSpec(
            num_scalar_prefetch=1,
            grid=(1,),
            in_specs=[full_spec(piece.shape) for piece in pieces],
            out_specs=full_spec((rows, len(pieces) * count * width)),
        ),
        out_shape=struct((rows, len(pieces) * count * width), F32),
        name="join_captions",
    )(order, *pieces)


def place_body(index_ref, *refs):
    *pieces, out_ref, sems = refs
    copies = [
        pltpu.make_async_copy(piece, out_ref.at[:, index_ref[at]], sems.at[at])
        for at, piece in enumerate(pieces)
    ]
    for copy in copies:
        copy.start()
    for copy in copies:
        copy.wait()


def place(pieces, order):
    groups, rows, columns = pieces[0].shape
    anywhere = pl.BlockSpec(memory_space=pl.ANY)
    return pl.pallas_call(
        place_body,
        grid_spec=pltpu.PrefetchScalarGridSpec(
            num_scalar_prefetch=1,
            grid=(),
            in_specs=[anywhere] * len(pieces),
            out_specs=anywhere,
            scratch_shapes=[pltpu.SemaphoreType.DMA((len(pieces),))],
        ),
        out_shape=struct((groups, len(pieces), rows, columns), pieces[0].dtype),
        name="place",
    )(order, *pieces)


def axes_size(axes):
    return math.prod(lax.axis_size(axis) for axis in axes)


def swap(x, axes, mask):
    return lax.ppermute(x, axes, [(i, i ^ mask) for i in range(axes_size(axes))])


def pick(x, index, axis=0):
    return lax.dynamic_index_in_dim(x, index, axis, keepdims=False)


def spread(x, axes, masks):
    first, second, fast = masks[1], masks[2], masks[4]
    half = x.shape[0] // 2
    one = swap(x, axes, first)
    two = swap(x, axes, second)
    far = jnp.concatenate([swap(two[:half], axes, first), swap(one[half:], axes, second)], axis=0)
    near = [x, one, two, far]
    return near + [swap(piece, axes, fast) for piece in near]


def collect(keep, send, axes, masks):
    first, second, fast = masks[1], masks[2], masks[4]
    half = keep.shape[2] // 2
    total = keep + swap(send, axes, fast).astype(F32)
    left, right = total[:, :, :half], total[:, :, half:]
    left_got = swap(left[1::2].astype(BF16), axes, first).astype(F32)
    right_got = swap(right[2:].astype(BF16), axes, second).astype(F32)
    left_end = swap((left[2] + left_got[1]).astype(BF16), axes, second).astype(F32)
    right_end = swap((right[1] + right_got[1]).astype(BF16), axes, first).astype(F32)
    return jnp.concatenate(
        [left[0] + left_got[0] + left_end, right[0] + right_got[0] + right_end], axis=1
    )


def collect_rows(left, right, right_dim, axes, masks):
    rows = left.shape[0] // len(masks)
    shape = (len(masks) // 2, rows, right.shape[1 - right_dim])
    middle = left.shape[0] // 2
    send = dot(left[middle:], right, 1, right_dim).astype(BF16).reshape(shape)
    keep = dot(left[:middle], right, 1, right_dim).reshape(shape)
    return collect(keep, send, axes, masks)


def turn_sum(parts, axes):
    return jnp.sum(turn(parts.astype(BF16), axes).astype(F32), axis=0)


def small_sum(x, axes):
    count = axes_size(axes)
    if count > 8 or count & (count - 1):
        return lax.psum(x, axes)
    total = x
    for mask in range(1, count):
        total = total + swap(x, axes, mask)
    return total


def clip_rows(x, axes):
    count = axes_size(axes)
    if count > 8 or count & (count - 1):
        return lax.psum_scatter(x, axes, scatter_dimension=0, tiled=False)
    me = lax.axis_index(axes)
    total = pick(x, me).astype(F32)
    for mask in range(1, count):
        total = total + swap(pick(x, me ^ mask), axes, mask).astype(F32)
    return total


def clip_spread(x, axes):
    return [swap(x, axes, mask) if mask else x for mask in range(axes_size(axes))]


def turn(x, axes):
    return lax.all_to_all(x, axes, split_axis=0, concat_axis=0, tiled=False)


def on_device(
    tokens,
    positions,
    captions,
    caption_lengths,
    conditioning,
    modulation_weight,
    modulation_bias,
    attention_gain,
    query_weight,
    key_weight,
    value_weight,
    query_gain,
    key_gain,
    text_weight,
    textkey_weight,
    textvalue_weight,
    textkey_gain,
    cross_gate,
    output_weight,
    feedforward_gain,
    gate_weight,
    up_weight,
    down_weight,
    cotangent,
):
    wide_count, narrow_count = lax.axis_size(W), lax.axis_size(N)
    clip_count = lax.axis_size(C)
    clip_index, wide_index = lax.axis_index(C), lax.axis_index(W)
    own_rows, model_width = tokens.shape[1], tokens.shape[2]
    head_size = query_gain.shape[0]
    head_count = model_width // head_size
    score_scale = head_size ** (-0.5)
    score_shift = 3.0 * math.sqrt(head_size)
    split_tokens = head_count % (wide_count * narrow_count) != 0
    tp, dp = ((N,), (C, W)) if split_tokens else (PLANE, (C,))
    tp_count, dp_count = axes_size(tp), axes_size(dp)
    tp_index = lax.axis_index(tp)
    masks = [0, 1, 4, 5, 2, 3, 6, 7]
    order = (tp_index ^ jnp.array(masks, jnp.int32)).astype(jnp.int32)
    clip_order = clip_index ^ jnp.arange(clip_count, dtype=jnp.int32)
    group_rows = own_rows * tp_count
    local_heads = head_count // tp_count
    head_width = local_heads * head_size
    weight_rows = query_weight.shape[0]
    hidden_rows, hidden_width = down_weight.shape[0], gate_weight.shape[1]
    local_hidden = hidden_width // tp_count

    def after(value, *others):
        return lax.optimization_barrier((value,) + others)[0]

    def head_columns(weight):
        return weight.reshape(weight_rows, tp_count, head_width).transpose(1, 0, 2)

    def hidden_columns(weight):
        split = weight.reshape(weight_rows, dp_count, tp_count, hidden_rows)
        return split.transpose(2, 0, 1, 3).reshape(tp_count, weight_rows, local_hidden)

    def gather_rows(rows):
        return lax.all_gather(rows, dp, axis=0, tiled=True)

    qkv_parts = turn(
        jnp.concatenate([head_columns(w) for w in (query_weight, key_weight, value_weight)], axis=2), tp
    )
    qkv_slice = gather_rows(qkv_parts.reshape(tp_count * weight_rows, 3 * head_width))

    cond_float = conditioning.astype(F32)
    cond_act = jax.nn.silu(cond_float)
    weight_float = modulation_weight.astype(F32)
    partial_mod = jnp.dot(cond_act, weight_float, precision=HIGHEST, preferred_element_type=F32)
    own_mod = small_sum(clip_rows(partial_mod, (C,)), PLANE) + modulation_bias
    shift_attn, scale_attn, gate_attn, shift_feed, scale_feed, gate_feed = jnp.split(own_mod, 6)

    place_rows = jnp.stack([positions[0] // 64, positions[0] % 64]).astype(BF16)
    place_rows = jnp.pad(place_rows, ((0, 30), (0, model_width - own_rows)))
    bundle = jnp.stack(spread(jnp.concatenate([tokens[0], cotangent[0], place_rows], axis=0), tp, masks))
    token_all = bundle[:, :own_rows].reshape(group_rows, model_width)
    cotangent_all = bundle[:, own_rows : 2 * own_rows].reshape(group_rows, model_width)
    place_all = bundle[:, 2 * own_rows : 2 * own_rows + 2, :own_rows].astype(F32)
    position_all = (place_all[:, 0] * 64.0 + place_all[:, 1]).reshape(group_rows)

    token_float = tokens[0].astype(F32)
    inv_attn = inverse_rms(token_float)
    hat_attn = token_float * inv_attn
    normed_attn = hat_attn * attention_gain
    group_float = token_all.astype(F32)
    group_normed = group_float * inverse_rms(group_float) * attention_gain
    mod_in = (group_normed * (1.0 + scale_attn) + shift_attn).astype(BF16)

    text_weights = jnp.concatenate([head_columns(w) for w in (textkey_weight, textvalue_weight)], axis=2)
    text_parts = turn(after(text_weights, qkv_parts), tp).reshape(tp_count * weight_rows, 2 * head_width)
    pieces = model_width // (2 * head_width)
    mixed_rows = jnp.concatenate(
        [text_parts, output_weight.reshape(weight_rows * pieces, 2 * head_width)], axis=0
    )
    mixed_all = gather_rows(mixed_rows).reshape(dp_count, mixed_rows.shape[0], 2 * head_width)
    text_slice = mixed_all[:, : tp_count * weight_rows].reshape(model_width, 2 * head_width)
    output_rows = mixed_all[:, tp_count * weight_rows :].reshape(dp_count * weight_rows, model_width)
    output_pieces = [
        piece.reshape(dp_count, weight_rows, model_width) for piece in spread(output_rows, tp, masks)
    ]
    output_full = place(output_pieces, order).reshape(model_width, model_width)
    hidden_weights = jnp.concatenate([hidden_columns(gate_weight), hidden_columns(up_weight)], axis=2)
    hidden_parts = turn(after(hidden_weights, text_parts), tp)
    hidden_slice = gather_rows(hidden_parts.reshape(tp_count * weight_rows, 2 * local_hidden))
    down_slice = gather_rows(after(down_weight, hidden_parts))

    caption_rows, text_width = captions.shape[1], captions.shape[2]
    text_rows = text_weight.shape[0]
    slot_count = caption_rows * narrow_count
    slot_part = slot_count // tp_count
    own_columns = pick(
        captions[0].reshape(caption_rows, clip_count, wide_count, narrow_count, text_rows), wide_index, 2
    )
    caption_parts = own_columns.transpose(1, 2, 0, 3).reshape(-1, caption_rows, text_rows)
    caption_columns = (
        turn(after(caption_parts, text_parts), (C, N))
        .reshape(clip_count, tp_count, slot_part, text_rows)
        .transpose(1, 0, 2, 3)
        .reshape(clip_count * slot_count, text_rows)
    )
    text_group = turn_sum(
        dot(caption_columns, text_weight).reshape(tp_count, clip_count * slot_part, model_width), tp
    )
    if split_tokens:
        text_group = lax.psum(text_group, W)
    text_own = clip_rows(text_group.astype(BF16).reshape(clip_count, slot_part, model_width), (C,))
    text_proj = jnp.concatenate(spread(text_own.astype(BF16), tp, masks), axis=0)
    true_slot = (order[:, None] * slot_part + jnp.arange(slot_part)).reshape(slot_count)
    keep = (true_slot < caption_lengths[clip_index]).astype(F32)

    cosine, sine = rope_tables(position_all, head_size)
    qkv_raw = dot(mod_in, qkv_slice)
    query_rot, key_rot, value_own = prepare(qkv_raw, cosine, sine, query_gain, key_gain, head_width)
    if split_tokens:
        keys_all = lax.all_gather(key_rot, W, axis=0, tiled=True)
        values_all = lax.all_gather(value_own, W, axis=0, tiled=True)
    else:
        keys_all, values_all = key_rot, value_own
    text_raw = dot(text_proj, text_slice)
    text_key, text_value = prepare_text(text_raw, textkey_gain, head_width)
    text_gate = pick(jnp.tanh(cross_gate).reshape(tp_count, local_heads), tp_index)
    gate_lanes = jnp.repeat(text_gate, head_size)
    mixed, own_out, cross_out, denom, text_denom = attend(
        order, query_rot, keys_all, values_all, text_key, text_value, keep, gate_lanes, head_size
    )

    mixed_own = turn(mixed, tp).transpose(1, 0, 2).reshape(own_rows, model_width)
    attn_out = dot(mixed_own, output_full)
    resid = token_float + gate_attn * attn_out
    inv_feed = inverse_rms(resid)
    hat_feed = resid * inv_feed
    normed_feed = hat_feed * feedforward_gain
    mod_own = (normed_feed * (1.0 + scale_feed) + shift_feed).astype(BF16)
    mod_ff = jnp.concatenate(spread(mod_own, tp, masks), axis=0)

    hidden_pre = dot(mod_ff, hidden_slice)
    gate_pre, up_pre = hidden_pre[:, :local_hidden], hidden_pre[:, local_hidden:]
    sigmoid_gate = jax.nn.sigmoid(gate_pre)
    silu_gate = gate_pre * sigmoid_gate
    inner = (silu_gate * up_pre).astype(BF16)
    dfeed = (gate_feed * cotangent_all.astype(F32)).astype(BF16)
    dinner = dot(dfeed, down_slice, 1, 1)
    dgate_pre = (dinner * up_pre * (sigmoid_gate * (1.0 + gate_pre * (1.0 - sigmoid_gate)))).astype(BF16)
    dup_pre = (dinner * silu_gate).astype(BF16)
    dhidden = jnp.concatenate([dgate_pre, dup_pre], axis=1)
    dmod_ff = collect_rows(dhidden, hidden_slice, 1, tp, masks)

    def scatter_rows(grads):
        return lax.psum_scatter(grads.astype(BF16), dp, scatter_dimension=0, tiled=True)

    dhidden_rows = scatter_rows(dot(mod_ff, dhidden, 0, 0))
    downweight_grad = scatter_rows(dot(inner, dfeed, 0, 0)).astype(F32)

    dout = cotangent[0].astype(F32)
    dshift_feed = jnp.sum(dmod_ff, axis=0)
    dscale_feed = jnp.sum(dmod_ff * normed_feed, axis=0)
    dfeed_gain, dresid_norm = norm_backward(
        hat_feed, inv_feed, feedforward_gain, dmod_ff * (1.0 + scale_feed)
    )
    dresid = dout + dresid_norm
    dgate_attn = jnp.sum(dresid * attn_out, axis=0)
    dattn = (gate_attn * dresid).astype(BF16)

    dmixed_own = dot(dattn, output_full, 1, 1).astype(BF16)
    dmixed = turn(dmixed_own.reshape(own_rows, tp_count, head_width).transpose(1, 0, 2), tp)
    dquery_text, dtext_key, dtext_value, dgate_lanes = attend_back(
        order, query_rot, cross_out, text_denom, dmixed, text_key, text_value, head_size, text=(keep, gate_lanes)
    )
    dquery, dkey, dvalue = attend_back(
        order, query_rot, own_out, denom, dmixed, keys_all, values_all, head_size, start=dquery_text
    )
    if split_tokens:
        dkey = lax.psum_scatter(dkey.astype(BF16), W, scatter_dimension=0, tiled=True)
        dvalue = lax.psum_scatter(dvalue.astype(BF16), W, scatter_dimension=0, tiled=True)
        dtext_key, dtext_value = lax.psum((dtext_key, dtext_value), W)
    dcross_gate = jnp.sum(dgate_lanes.reshape(local_heads, head_size), axis=1) * (1.0 - text_gate * text_gate)
    dqkv, gain_grads = finish(qkv_raw, dquery, dkey, dvalue, cosine, sine, query_gain, key_gain)
    dmod_in = collect_rows(dqkv, qkv_slice, 1, tp, masks)

    dtext_heads, dtkey_gain = finish_text(text_raw, dtext_key, dtext_value, textkey_gain)
    dtext_parts = dot(dtext_heads, text_slice, 1, 1).reshape(tp_count, slot_part, model_width)
    dtext_own = jnp.zeros_like(dtext_parts)
    for at in range(tp_count):
        dtext_own = lax.dynamic_update_index_in_dim(dtext_own, dtext_parts[at], order[at], 0)
    dtext_group = turn_sum(dtext_own, tp).astype(BF16)
    dtext_clips = clip_spread(dtext_group, (C,))
    dtext_rows = jnp.zeros((clip_count, slot_part, model_width), BF16)
    for at in range(clip_count):
        dtext_rows = lax.dynamic_update_index_in_dim(dtext_rows, dtext_clips[at], clip_order[at], 0)
    dtext_pieces = spread(dtext_rows.reshape(clip_count * slot_part, model_width), tp, masks)
    dtext_all = place([piece[None] for piece in dtext_pieces], order).reshape(-1, model_width)
    textweight_grad = dot(caption_columns, dtext_all, 0, 0)
    dcaption_parts = (
        dot(dtext_all, text_weight, 1, 1)
        .astype(BF16)
        .reshape(tp_count, clip_count, slot_part, text_rows)
        .transpose(1, 0, 2, 3)
        .reshape(-1, caption_rows, text_rows)
    )
    dcaption_own = turn(dcaption_parts, (C, N))
    wide_order = (wide_index ^ jnp.arange(wide_count, dtype=jnp.int32)).astype(jnp.int32)
    captions_grad = join_captions(clip_spread(dcaption_own, (W,)), wide_order, clip_count, narrow_count)

    feed_out = collect_rows(after(inner, dmod_ff), down_slice, 0, tp, masks)
    block_output = resid + gate_feed * feed_out
    dgate_feed = jnp.sum(dout * feed_out, axis=0)

    dout_parts = (
        dot(after(mixed_own, dmixed), dattn, 0, 0)
        .astype(BF16)
        .reshape(dp_count, tp_count, weight_rows, model_width)
        .transpose(1, 0, 2, 3)
        .reshape(tp_count, dp_count * weight_rows, model_width)
    )
    dout_group = turn_sum(dout_parts, tp)
    outweight_grad = clip_rows(
        dout_group.astype(BF16).reshape(dp_count, weight_rows, model_width), dp
    ).astype(F32)
    shared = 1.0 / wide_count if split_tokens else 1.0
    dhead_rows = scatter_rows(
        jnp.concatenate([dot(mod_in, dqkv, 0, 0), dot(text_proj, dtext_heads, 0, 0) * shared], axis=1)
    )
    dhidden_parts = turn(dhidden_rows.reshape(tp_count, weight_rows, 2 * local_hidden), tp)
    gateweight_grad, upweight_grad = join_hidden(dhidden_parts, dp_count, hidden_rows)
    dhead_parts = turn(dhead_rows.reshape(tp_count, weight_rows, 5 * head_width), tp)
    queryweight_grad, keyweight_grad, valueweight_grad, textkey_grad, textvalue_grad = join_heads(
        dhead_parts, head_width
    )

    dshift_attn = jnp.sum(dmod_in, axis=0)
    dscale_attn = jnp.sum(dmod_in * normed_attn, axis=0)
    dattn_gain, dtokens_norm = norm_backward(
        hat_attn, inv_attn, attention_gain, dmod_in * (1.0 + scale_attn)
    )
    tokens_grad = dresid + dtokens_norm

    head_range = jnp.arange(head_count) - tp_index * local_heads
    dgate_rows = jnp.sum(
        jnp.where(head_range[:, None] == jnp.arange(local_heads)[None, :], dcross_gate[None, :], 0.0), axis=1
    )
    pad = -head_count % head_size
    small = jnp.concatenate(
        [
            dshift_attn,
            dscale_attn,
            dgate_attn,
            dshift_feed,
            dscale_feed,
            dgate_feed,
            dattn_gain,
            dfeed_gain,
            gain_grads[0],
            gain_grads[1],
            dtkey_gain[0] * shared,
            dgate_rows,
            jnp.zeros((pad,), F32),
        ]
    )
    clip_small = jnp.stack(clip_spread(small_sum(small, PLANE), (C,)))
    mod_width = 6 * model_width
    dmod_all = clip_small[:, :mod_width]
    gains = jnp.sum(clip_small[:, mod_width:], axis=0)
    attngain_grad, feedgain_grad = gains[:model_width], gains[model_width : 2 * model_width]
    rest = gains[2 * model_width :]
    querygain_grad, keygain_grad, textgain_grad = (
        rest[:head_size],
        rest[head_size : 2 * head_size],
        rest[2 * head_size : 3 * head_size],
    )
    crossgate_grad = rest[3 * head_size : 3 * head_size + head_count]
    cond_rows = jnp.stack([pick(cond_act, clip_order[at]) for at in range(clip_count)])
    modweight_grad = jnp.dot(cond_rows.T, dmod_all, precision=HIGHEST, preferred_element_type=F32)
    dcond_rows = jnp.dot(dmod_all, weight_float.T, precision=HIGHEST, preferred_element_type=F32)
    dcond_act = jnp.stack([pick(dcond_rows, clip_order[at]) for at in range(clip_count)])
    sigmoid_cond = jax.nn.sigmoid(cond_float)
    conditioning_grad = dcond_act * sigmoid_cond * (1.0 + cond_float * (1.0 - sigmoid_cond))
    modbias_grad = jnp.sum(dmod_all, axis=0)
    return (
        block_output[None],
        tokens_grad[None],
        captions_grad[None],
        conditioning_grad,
        modweight_grad,
        modbias_grad,
        attngain_grad,
        queryweight_grad,
        keyweight_grad,
        valueweight_grad,
        querygain_grad,
        keygain_grad,
        textweight_grad,
        textkey_grad,
        textvalue_grad,
        textgain_grad,
        crossgate_grad,
        outweight_grad,
        feedgain_grad,
        gateweight_grad,
        upweight_grad,
        downweight_grad,
    )


def solution(mesh):
    rows, whole = P(ALL, None), P()
    tokens, captions = P(C, PLANE, None), P(C, N, None)
    columns = P(None, ALL)
    return jax.shard_map(
        on_device,
        mesh=mesh,
        in_specs=(
            tokens,
            P(C, PLANE),
            captions,
            whole,
            columns,
            rows,
            whole,
            whole,
            rows,
            rows,
            rows,
            whole,
            whole,
            rows,
            rows,
            rows,
            whole,
            whole,
            rows,
            whole,
            rows,
            rows,
            rows,
            tokens,
        ),
        out_specs=(
            tokens,
            tokens,
            captions,
            columns,
            rows,
            whole,
            whole,
            rows,
            rows,
            rows,
            whole,
            whole,
            rows,
            rows,
            rows,
            whole,
            whole,
            rows,
            whole,
            rows,
            rows,
            rows,
        ),
        check_vma=False,
    )
```

```python
import functools
import math

import jax
import jax.numpy as jnp
import numpy as np
from jax import lax
from jax.experimental import pallas as pl
from jax.experimental.pallas import tpu as pltpu
from jax.sharding import PartitionSpec as P

EPSILON = 1e-06
ROPE_BASE = 10000.0
C, W, N = "clip", "wide", "narrow"
ALL = (C, W, N)
PLANE = (W, N)
BF16, F32 = jnp.bfloat16, jnp.float32
HIGHEST = lax.Precision.HIGHEST


def dot(left, right, left_dim=1, right_dim=0):
    return lax.dot_general(
        left, right, (((left_dim,), (right_dim,)), ((), ())), preferred_element_type=F32
    )


def inverse_rms(values):
    return lax.rsqrt(jnp.mean(values * values, axis=-1, keepdims=True) + EPSILON)


def norm_backward(normed, inv_scale, gain, upstream):
    gain_grad = jnp.sum((upstream * normed).reshape(-1, normed.shape[-1]), axis=0)
    scaled = upstream * gain
    values_grad = inv_scale * (scaled - normed * jnp.mean(scaled * normed, axis=-1, keepdims=True))
    return (gain_grad, values_grad)


def rope_tables(positions, head_size, width):
    half_size = head_size // 2
    frequency = jnp.exp(-math.log(ROPE_BASE) * 2.0 * jnp.arange(half_size, dtype=F32) / head_size)
    angles = positions.astype(F32)[:, None] * jnp.tile(frequency, width // half_size)[None, :]
    sign = jnp.where(jnp.arange(width) % head_size < half_size, -1.0, 1.0)
    return (jnp.cos(angles), jnp.sin(angles) * sign[None, :])


def exact_dot(left, right):
    high = left.astype(BF16)
    low = (left - high.astype(F32)).astype(BF16)
    return dot(high, right) + dot(low, right)


def head_means(width, size):
    at = np.arange(width)
    return jnp.asarray((at[:, None] // size == at[None, :] // size) / size, BF16)


def half_swaps(width, size):
    at = np.arange(width)
    other = np.where(at % size < size // 2, at + size // 2, at - size // 2)
    return jnp.asarray(at[:, None] == other[None, :], BF16)


def widen(table, width):
    return jnp.concatenate([table] * (width // table.shape[1]), axis=1)


def full_spec(shape):
    return pl.BlockSpec(shape, lambda *_: (0,) * len(shape))


def row_spec(rows, width):
    return pl.BlockSpec((rows, width), lambda i, *_: (i, 0))


def struct(shape, dtype):
    return jax.ShapeDtypeStruct(shape, dtype)


def head_parts(width, size):
    return [slice(at, at + size) for at in range(0, width, size)]


def prepare_body(raw_ref, cos_ref, sin_ref, gain_ref, means_ref, swaps_ref, out_ref, value_ref):
    width = out_ref.shape[1]
    raw = raw_ref[:, :width]
    inv = lax.rsqrt(exact_dot(raw * raw, means_ref[...]) + EPSILON)
    normed = raw * inv * gain_ref[...]
    swapped = exact_dot(normed, swaps_ref[...])
    cosine, sine = widen(cos_ref[...], width), widen(sin_ref[...], width)
    out_ref[...] = (normed * cosine + swapped * sine).astype(BF16)
    value_ref[...] = raw_ref[:, width:].astype(BF16)


def prepare(raw, cosine, sine, gain, size):
    rows, width = raw.shape[0], gain.shape[0]
    block = math.gcd(rows, 256)
    return pl.pallas_call(
        prepare_body,
        grid=(rows // block,),
        in_specs=[
            row_spec(block, raw.shape[1]),
            row_spec(block, cosine.shape[1]),
            row_spec(block, cosine.shape[1]),
            full_spec((1, width)),
            full_spec((width, width)),
            full_spec((width, width)),
        ],
        out_specs=[row_spec(block, width), row_spec(block, raw.shape[1] - width)],
        out_shape=[struct((rows, width), BF16), struct((rows, raw.shape[1] - width), BF16)],
        name="prepare",
    )(raw, cosine, sine, gain[None], head_means(width, size), half_swaps(width, size))


def prepare_text_body(raw_ref, gain_ref, key_ref, value_ref):
    width, size = key_ref.shape[1], gain_ref.shape[1]
    raw, gain = raw_ref[...], gain_ref[...]
    heads = [raw[:, part] for part in head_parts(width, size)]
    heads = [head * inverse_rms(head) * gain for head in heads]
    key_ref[...] = jnp.concatenate(heads, axis=1).astype(BF16)
    value_ref[...] = raw[:, width:].astype(BF16)


def prepare_text(raw, gain, width):
    return pl.pallas_call(
        prepare_text_body, out_shape=[struct((raw.shape[0], width), BF16)] * 2, name="prepare_text"
    )(raw, gain[None])


def weights_of(left, right, factor, offset):
    scores = lax.dot_general(left, right, (((1,), (1,)), ((), ())), preferred_element_type=F32)
    return jnp.exp2(scores * factor - offset)


def attend_body(query_ref, key_ref, value_ref, out_ref, denom_ref, *, size, base, factor, offset):
    rows, width = out_ref.shape
    outs, denoms = [], []
    for part in head_parts(width, size):
        keys = key_ref[:, base + part.start : base + part.stop]
        wts = weights_of(query_ref[:, part], keys, factor, offset)
        denom = jnp.sum(wts, axis=1, keepdims=True)
        outs.append(dot(wts.astype(BF16), value_ref[:, part]) / denom)
        denoms.append(jnp.broadcast_to(denom, (rows, size)))
    out_ref[...] = jnp.concatenate(outs, axis=1)
    denom_ref[...] = jnp.concatenate(denoms, axis=1)


def score_constants(size):
    return {"factor": size**-0.5 / math.log(2.0), "offset": 3.0 * size**0.5 / math.log(2.0)}


def attend(query, keys, base, values, size):
    rows, width = query.shape[0], values.shape[1]
    block = math.gcd(rows, 256)
    return pl.pallas_call(
        functools.partial(attend_body, size=size, base=base, **score_constants(size)),
        grid=(rows // block,),
        in_specs=[row_spec(block, query.shape[1]), full_spec(keys.shape), full_spec(values.shape)],
        out_specs=[row_spec(block, width)] * 2,
        out_shape=[struct((rows, width), F32)] * 2,
        name="attend",
    )(query, keys, values)


def attend_text_body(
    order_ref,
    query_ref,
    key_ref,
    value_ref,
    keep_ref,
    gate_ref,
    own_ref,
    mixed_ref,
    cross_ref,
    denom_ref,
    *,
    size,
    factor,
    offset,
):
    rows, width = cross_ref.shape
    part_rows = mixed_ref.shape[1]
    keep = keep_ref[...]
    outs, denoms = [], []
    for part in head_parts(width, size):
        wts = weights_of(query_ref[:, part], key_ref[:, part], factor, offset) * keep
        denom = jnp.sum(wts, axis=1, keepdims=True)
        outs.append(dot(wts.astype(BF16), value_ref[:, part]) / denom)
        denoms.append(jnp.broadcast_to(denom, (rows, size)))
    cross = jnp.concatenate(outs, axis=1)
    cross_ref[...], denom_ref[...] = cross, jnp.concatenate(denoms, axis=1)
    mixed = (own_ref[...] + gate_ref[...] * cross).astype(BF16)
    first = pl.program_id(0) * (rows // part_rows)
    for index in range(rows // part_rows):
        mixed_ref[order_ref[first + index]] = mixed[index * part_rows : (index + 1) * part_rows]


def attend_text(order, query, text_key, text_value, keep, gate, own, size):
    rows, width = own.shape
    slots, count = text_key.shape[0], order.shape[0]
    part_rows = rows // count
    block = part_rows * math.gcd(count, max(1, 512 // part_rows))
    return pl.pallas_call(
        functools.partial(attend_text_body, size=size, **score_constants(size)),
        grid_spec=pltpu.PrefetchScalarGridSpec(
            num_scalar_prefetch=1,
            grid=(rows // block,),
            in_specs=[
                row_spec(block, query.shape[1]),
                full_spec((slots, width)),
                full_spec((slots, width)),
                full_spec((1, slots)),
                full_spec((1, width)),
                row_spec(block, width),
            ],
            out_specs=[full_spec((count, part_rows, width))] + [row_spec(block, width)] * 2,
        ),
        out_shape=[struct((count, part_rows, width), BF16)] + [struct((rows, width), F32)] * 2,
        name="attend_text",
    )(order, query, text_key, text_value, keep[None], gate[None], own)


def attend_back_body(
    order_ref, query_ref, out_ref, denom_ref, dmixed_ref, key_ref, value_ref, *refs, size, base, factor, offset, text
):
    if text:
        keep_ref, gate_ref, dquery_ref, dkey_ref, dvalue_ref, dgate_ref = refs
    else:
        start_ref, dquery_ref, dkey_ref, dvalue_ref = refs
    rows, width = out_ref.shape
    part_rows = dmixed_ref.shape[1]
    step = pl.program_id(0)
    first = step * (rows // part_rows)
    dmixed = jnp.concatenate(
        [dmixed_ref[order_ref[first + index]] for index in range(rows // part_rows)], axis=0
    ).astype(F32)
    out, inv = out_ref[...], 1.0 / denom_ref[...]

    @pl.when(step == 0)
    def _():
        dkey_ref[...] = jnp.zeros_like(dkey_ref)
        dvalue_ref[...] = jnp.zeros_like(dvalue_ref)
        if text:
            dgate_ref[...] = jnp.zeros_like(dgate_ref)

    if text:
        dgate_ref[...] += jnp.sum(dmixed * out, axis=0, keepdims=True)
        dmixed = dmixed * gate_ref[...]
    dnumer = (dmixed * inv).astype(BF16)
    level = -(dmixed * out * inv)
    scale = size**-0.5
    results = []
    for part in head_parts(width, size):
        query, numer = query_ref[:, part], dnumer[:, part]
        keys = key_ref[:, base + part.start : base + part.stop]
        column = jnp.sum(level[:, part], axis=1, keepdims=True)
        level_row = jnp.broadcast_to(column, (rows, 128)).T[:1]
        wts = weights_of(keys, query, factor, offset)
        if text:
            wts = wts * keep_ref[...]
        dwts = lax.dot_general(
            value_ref[:, part], numer, (((1,), (1,)), ((), ())), preferred_element_type=F32
        )
        dscores = (wts * (dwts + level_row)).astype(BF16)
        dquery = (dot(keys.T, dscores) * scale).T
        results.append((dquery, dot(dscores, query) * scale, dot(wts.astype(BF16), numer)))
    dquery, dkey, dvalue = (jnp.concatenate(heads, axis=1) for heads in zip(*results))
    dquery_ref[...] = dquery if text else dquery + start_ref[...]
    dkey_ref[...] += dkey
    dvalue_ref[...] += dvalue


def attend_back(order, query, out, denom, dmixed, keys, base, values, size, text=None, start=None):
    rows, width = out.shape
    slots = keys.shape[0]
    part_rows = rows // order.shape[0]
    block = part_rows * math.gcd(order.shape[0], max(1, (256 if text is None else 512) // part_rows))
    if text is None:
        extra, extra_specs, ends = (start,), [row_spec(block, width)], []
    else:
        extra, ends = (text[0][:, None], text[1][None]), [(1, width)]
        extra_specs = [full_spec((slots, 1)), full_spec((1, width))]
    return pl.pallas_call(
        functools.partial(
            attend_back_body, size=size, base=base, text=text is not None, **score_constants(size)
        ),
        grid_spec=pltpu.PrefetchScalarGridSpec(
            num_scalar_prefetch=1,
            grid=(rows // block,),
            in_specs=[row_spec(block, query.shape[1]), row_spec(block, width), row_spec(block, width)]
            + [full_spec(dmixed.shape), full_spec(keys.shape), full_spec(values.shape)]
            + extra_specs,
            out_specs=[row_spec(block, width)]
            + [full_spec(values.shape)] * 2
            + [full_spec(shape) for shape in ends],
        ),
        out_shape=[struct((rows, width), F32)]
        + [struct(values.shape, F32)] * 2
        + [struct(shape, F32) for shape in ends],
        name="text_back" if text else "attend_back",
    )(order, query, out, denom, dmixed, keys, values, *extra)


def norm_heads_back(raw, upstream, gain, size):
    gain_grad, grads = 0.0, []
    for part in head_parts(raw.shape[1], size):
        head, grad = raw[:, part], upstream[part.start // size]
        inv = inverse_rms(head)
        hat = head * inv
        gain_grad = gain_grad + jnp.sum(grad * hat, axis=0, keepdims=True)
        scaled = grad * gain
        grads.append(inv * (scaled - hat * jnp.mean(scaled * hat, axis=1, keepdims=True)))
    return gain_grad, jnp.concatenate(grads, axis=1)


def finish_body(
    raw_ref, dquery_ref, dkey_ref, dvalue_ref, cos_ref, sin_ref, gain_ref, means_ref, swaps_ref, out_ref, dgain_ref
):
    width = gain_ref.shape[1]

    @pl.when(pl.program_id(0) == 0)
    def _():
        dgain_ref[...] = jnp.zeros_like(dgain_ref)

    raw, means = raw_ref[:, :width], means_ref[...]
    inv = lax.rsqrt(exact_dot(raw * raw, means) + EPSILON)
    hat = raw * inv
    grad = jnp.concatenate([dquery_ref[...], dkey_ref[...].astype(F32)], axis=1)
    swapped = exact_dot(grad, swaps_ref[...])
    grad = grad * widen(cos_ref[...], width) - swapped * widen(sin_ref[...], width)
    dgain_ref[...] += jnp.sum(grad * hat, axis=0, keepdims=True)
    scaled = grad * gain_ref[...]
    out = inv * (scaled - hat * exact_dot(scaled * hat, means))
    out_ref[...] = jnp.concatenate([out.astype(BF16), dvalue_ref[...].astype(BF16)], axis=1)


def finish(raw, dquery, dkey, dvalue, cosine, sine, gain, size):
    rows, width = raw.shape[0], gain.shape[0]
    block = math.gcd(rows, 256)
    return pl.pallas_call(
        finish_body,
        grid=(rows // block,),
        in_specs=[row_spec(block, raw.shape[1])]
        + [row_spec(block, width // 2)] * 3
        + [row_spec(block, cosine.shape[1])] * 2
        + [full_spec((1, width)), full_spec((width, width)), full_spec((width, width))],
        out_specs=[row_spec(block, raw.shape[1]), full_spec((1, width))],
        out_shape=[struct(raw.shape, BF16), struct((1, width), F32)],
        name="finish",
    )(raw, dquery, dkey, dvalue, cosine, sine, gain[None], head_means(width, size), half_swaps(width, size))


def finish_text_body(raw_ref, dkey_ref, dvalue_ref, gain_in_ref, out_ref, gain_ref):
    width, size = dkey_ref.shape[1], gain_in_ref.shape[1]
    upstream = [dkey_ref[:, part] for part in head_parts(width, size)]
    gain_ref[...], grads = norm_heads_back(raw_ref[:, :width], upstream, gain_in_ref[...], size)
    out_ref[...] = jnp.concatenate([grads.astype(BF16), dvalue_ref[...].astype(BF16)], axis=1)


def finish_text(raw, dkey, dvalue, gain):
    return pl.pallas_call(
        finish_text_body,
        out_shape=[struct(raw.shape, BF16), struct((1, gain.shape[0]), F32)],
        name="finish_text",
    )(raw, dkey, dvalue, gain[None])


def join_body(parts_ref, *outs, width):
    for index, out_ref in enumerate(outs):
        for turn_index in range(parts_ref.shape[0]):
            at = turn_index * width
            out_ref[:, at : at + width] = parts_ref[turn_index, :, index * width : (index + 1) * width].astype(F32)


def join_heads(parts, width):
    count, rows, total = parts.shape
    return pl.pallas_call(
        functools.partial(join_body, width=width),
        out_shape=[struct((rows, count * width), F32)] * (total // width),
        name="join_heads",
    )(parts)


def join_groups_body(parts_ref, *outs, groups, width):
    count = parts_ref.shape[0]
    for index, out_ref in enumerate(outs):
        for group in range(groups):
            for turn_index in range(count):
                at = (group * count + turn_index) * width
                source = (index * groups + group) * width
                out_ref[:, at : at + width] = parts_ref[turn_index, :, source : source + width].astype(F32)


def join_groups(parts, groups, width, kinds):
    count, rows, _ = parts.shape
    return pl.pallas_call(
        functools.partial(join_groups_body, groups=groups, width=width),
        out_shape=[struct((rows, groups * count * width), F32)] * kinds,
        name="join_groups",
    )(parts)


def split_heads_body(*refs, width):
    *ins, out_ref = refs
    for index, in_ref in enumerate(ins):
        for device in range(out_ref.shape[0]):
            at = device * width
            out_ref[device, :, index * width : (index + 1) * width] = in_ref[:, at : at + width]


def split_heads(weights, count):
    rows, columns = weights[0].shape
    width = columns // count
    return pl.pallas_call(
        functools.partial(split_heads_body, width=width),
        out_shape=struct((count, rows, len(weights) * width), BF16),
        name="split_heads",
    )(*weights)


def split_groups_body(*refs, groups, width):
    *ins, out_ref = refs
    count = out_ref.shape[0]
    for index, in_ref in enumerate(ins):
        for group in range(groups):
            for device in range(count):
                at, to = (group * count + device) * width, (index * groups + group) * width
                out_ref[device, :, to : to + width] = in_ref[:, at : at + width]


def split_groups(weights, count, groups, width):
    rows = weights[0].shape[0]
    return pl.pallas_call(
        functools.partial(split_groups_body, groups=groups, width=width),
        out_shape=struct((count, rows, len(weights) * groups * width), BF16),
        name="split_groups",
    )(*weights)


def take_columns_body(order_ref, in_ref, *outs, groups, count, width):
    for index, out_ref in enumerate(outs):
        for group in range(groups):
            at = pl.multiple_of((group * count + order_ref[index]) * width, width)
            out_ref[:, group * width : (group + 1) * width] = in_ref[:, pl.ds(at, width)]


def take_columns(values, order, takers, groups, count, width):
    rows = values.shape[0]
    if width % 128:
        split = values.reshape(rows, groups, count, width)
        return [pick(split, order[at], 2).reshape(rows, groups * width) for at in range(takers)]
    return pl.pallas_call(
        functools.partial(take_columns_body, groups=groups, count=count, width=width),
        grid_spec=pltpu.PrefetchScalarGridSpec(
            num_scalar_prefetch=1,
            grid=(1,),
            in_specs=[full_spec(values.shape)],
            out_specs=[full_spec((rows, groups * width))] * takers,
        ),
        out_shape=[struct((rows, groups * width), values.dtype)] * takers,
        name="take_columns",
    )(order, values)


def head_grads_body(text_ref, dtext_ref, mod_ref, dqkv_ref, out_ref, *, factor):
    text = dot(text_ref[...], dtext_ref[...], 0, 0) * factor
    out_ref[:, : text.shape[1]] = text.astype(BF16)
    out_ref[:, text.shape[1] :] = dot(mod_ref[...], dqkv_ref[...], 0, 0).astype(BF16)


def head_grads(text, dtext, mod, dqkv, factor):
    width, total = text.shape[1], dtext.shape[1] + dqkv.shape[1]
    block = math.gcd(width, 256)
    return pl.pallas_call(
        functools.partial(head_grads_body, factor=factor),
        grid=(width // block,),
        in_specs=[
            pl.BlockSpec((text.shape[0], block), lambda i: (0, i)),
            full_spec(dtext.shape),
            pl.BlockSpec((mod.shape[0], block), lambda i: (0, i)),
            full_spec(dqkv.shape),
        ],
        out_specs=row_spec(block, total),
        out_shape=struct((width, total), BF16),
        name="head_grads",
    )(text, dtext, mod, dqkv)


def feed_body(*refs, count, steps):
    pieces = refs[:count]
    weight_ref, down_ref, dfeed_ref, mod_ref, inner_ref, dhidden_ref, buffer, sems = refs[count:]
    step, per = pl.program_id(0), count // steps
    rows, hidden = pieces[0].shape[0], inner_ref.shape[1]

    def fetch(at):
        for index in range(per):
            pltpu.make_async_copy(
                pieces[at * per + index], buffer.at[at % 2, pl.ds(index * rows, rows)], sems.at[at % 2, index]
            ).start()

    @pl.when(step == 0)
    def _():
        fetch(0)

    for at in range(steps - 1):

        @pl.when(step == at)
        def _(at=at):
            fetch(at + 1)

    slot = step % 2
    for index in range(per):
        pltpu.make_async_copy(
            pieces[0], buffer.at[slot, pl.ds(index * rows, rows)], sems.at[slot, index]
        ).wait()
    mod = buffer[slot]
    mod_ref[...] = mod
    gate = dot(mod, weight_ref[:, :hidden])
    up = dot(mod, weight_ref[:, hidden:])
    sigmoid = 1.0 / (1.0 + jnp.exp(-gate))
    silu = gate * sigmoid
    inner = (silu * up).astype(BF16)
    inner_ref[...] = inner
    dinner = dot(dfeed_ref[...], down_ref[...], 1, 1)
    dhidden_ref[:, :hidden] = (dinner * up * (sigmoid * (1.0 + gate * (1.0 - sigmoid)))).astype(BF16)
    dhidden_ref[:, hidden:] = (dinner * silu).astype(BF16)


def feed(pieces, weight, down, dfeed):
    count = len(pieces)
    rows, width = pieces[0].shape
    hidden = down.shape[0]
    steps = count // 2
    block = rows * 2
    return pl.pallas_call(
        functools.partial(feed_body, count=count, steps=steps),
        grid=(steps,),
        in_specs=[pl.BlockSpec(memory_space=pl.ANY)] * count
        + [
            full_spec(weight.shape),
            full_spec(down.shape),
            row_spec(block, width),
        ],
        out_specs=[
            row_spec(block, width),
            row_spec(block, hidden),
            row_spec(block, 2 * hidden),
        ],
        out_shape=[
            struct((count * rows, width), BF16),
            struct((count * rows, hidden), BF16),
            struct((count * rows, 2 * hidden), BF16),
        ],
        scratch_shapes=[pltpu.VMEM((2, block, width), BF16), pltpu.SemaphoreType.DMA((2, 2))],
        name="feed",
    )(*pieces, weight, down, dfeed)


def place_body(order_ref, *refs):
    *pieces, out_ref = refs
    for at, piece in enumerate(pieces):
        out_ref[:, order_ref[at]] = piece[...]


def place(pieces, order):
    groups, rows, columns = pieces[0].shape
    return pl.pallas_call(
        place_body,
        grid_spec=pltpu.PrefetchScalarGridSpec(
            num_scalar_prefetch=1,
            grid=(groups,),
            in_specs=[pl.BlockSpec((1, rows, columns), lambda i, *_: (i, 0, 0))] * len(pieces),
            out_specs=pl.BlockSpec((1, len(pieces), rows, columns), lambda i, *_: (i, 0, 0, 0)),
        ),
        out_shape=struct((groups, len(pieces), rows, columns), pieces[0].dtype),
        name="place",
    )(order, *pieces)


def modulate_body(*refs, count, own_rows):
    pieces = refs[:count]
    scale_ref, shift_ref, gate_ref, mod_ref, dfeed_ref, tail_ref, buffer, sems = refs[count:]
    step = pl.program_id(0)

    def fetch(at):
        pltpu.make_async_copy(pieces[at], buffer.at[at % 2], sems.at[at % 2]).start()

    @pl.when(step == 0)
    def _():
        fetch(0)

    for at in range(count - 1):

        @pl.when(step == at)
        def _(at=at):
            fetch(at + 1)

    slot = step % 2
    pltpu.make_async_copy(pieces[0], buffer.at[slot], sems.at[slot]).wait()
    tokens = buffer[slot, :own_rows].astype(F32)
    mod_ref[...] = (tokens * inverse_rms(tokens) * scale_ref[...] + shift_ref[...]).astype(BF16)
    dfeed_ref[...] = (buffer[slot, own_rows : 2 * own_rows].astype(F32) * gate_ref[...]).astype(BF16)
    tail_ref[0] = buffer[slot, 2 * own_rows :, : tail_ref.shape[2]]


def modulate(pieces, scale, shift, gate, own_rows, tail_width):
    count = len(pieces)
    rows, width = pieces[0].shape
    tail = (1, rows - 2 * own_rows, tail_width)
    return pl.pallas_call(
        functools.partial(modulate_body, count=count, own_rows=own_rows),
        grid=(count,),
        in_specs=[pl.BlockSpec(memory_space=pl.ANY)] * count + [full_spec((1, width))] * 3,
        out_specs=[row_spec(own_rows, width)] * 2 + [pl.BlockSpec(tail, lambda i: (i, 0, 0))],
        out_shape=[struct((count * own_rows, width), BF16)] * 2 + [struct((count,) + tail[1:], BF16)],
        scratch_shapes=[pltpu.VMEM((2, rows, width), BF16), pltpu.SemaphoreType.DMA((2,))],
        name="modulate",
    )(*pieces, scale[None], shift[None], gate[None])


def outer_body(order_ref, left_ref, right_ref, out_ref):
    groups, _, rows, inner = left_ref.shape
    product = dot(left_ref[...].reshape(groups * rows, inner), right_ref[...]).astype(BF16)
    out_ref[0] = product.reshape(out_ref.shape[1:])


def outer(left, right, order):
    groups, count, rows, inner = left.shape
    columns = right.shape[1]
    return pl.pallas_call(
        outer_body,
        grid_spec=pltpu.PrefetchScalarGridSpec(
            num_scalar_prefetch=1,
            grid=(count,),
            in_specs=[
                pl.BlockSpec((groups, 1, rows, inner), lambda i, order_ref: (0, order_ref[i], 0, 0)),
                full_spec((inner, columns)),
            ],
            out_specs=pl.BlockSpec((1, groups, rows, columns), lambda i, order_ref: (i, 0, 0, 0)),
        ),
        out_shape=struct((count, groups, rows, columns), BF16),
        name="outer",
    )(order, left, right)


def axes_size(axes):
    return math.prod(lax.axis_size(axis) for axis in axes)


def swap(x, axes, mask):
    return lax.ppermute(x, axes, [(i, i ^ mask) for i in range(axes_size(axes))])


def pick(x, index, axis=0):
    return lax.dynamic_index_in_dim(x, index, axis, keepdims=False)


def spread(x, axes, masks):
    first, second, fast = masks[1], masks[2], masks[4]
    half = x.shape[0] // 2
    one = swap(x, axes, first)
    two = swap(x, axes, second)
    far = jnp.concatenate([swap(two[:half], axes, first), swap(one[half:], axes, second)], axis=0)
    near = [x, one, two, far]
    return near + [swap(piece, axes, fast) for piece in near]


class Collect:
    def __init__(self, keep, send, axes, masks):
        self.axes, self.masks, self.keep = axes, masks, keep
        self.got = swap(send, axes, masks[4])

    def exchange(self, x, index):
        return swap(x.astype(BF16), self.axes, self.masks[index])

    def part(self, slots, columns):
        return self.keep[slots, :, columns].astype(F32) + self.got[slots, :, columns].astype(F32)

    def first(self):
        half = self.keep.shape[2] // 2
        left, right = slice(0, half), slice(half, 2 * half)
        self.left_got = self.exchange(self.part(slice(1, 4, 2), left), 1)
        self.right_got = self.exchange(self.part(slice(2, 4), right), 2)
        self.left = [self.part(0, left), self.part(2, left)]
        self.right = [self.part(0, right), self.part(1, right)]

    def second(self):
        left_got, right_got = self.left_got.astype(F32), self.right_got.astype(F32)
        self.left_end = self.exchange(self.left[1] + left_got[1], 2)
        self.right_end = self.exchange(self.right[1] + right_got[1], 1)

    def end(self):
        left = self.left[0] + self.left_got[0].astype(F32) + self.left_end.astype(F32)
        right = self.right[0] + self.right_got[0].astype(F32) + self.right_end.astype(F32)
        return jnp.concatenate([left, right], axis=1)

    def tie_first(self, *others):
        self.got, *rest = tie(self.got, *others)
        self.first()
        return rest

    def tie_second(self, *others):
        self.left_got, self.right_got, *rest = tie(self.left_got, self.right_got, *others)
        self.second()
        return rest

    def tie_end(self, *others):
        self.left_end, self.right_end, *rest = tie(self.left_end, self.right_end, *others)
        return [self.end()] + rest


def tie(*values):
    return lax.optimization_barrier(values)


def halves_product(left, right, right_dim, count):
    middle = left.shape[0] // 2
    shape = (count // 2, left.shape[0] // count, right.shape[1 - right_dim])
    send = dot(left[middle:], right, 1, right_dim).astype(BF16).reshape(shape)
    send, first = tie(send, left[:middle])
    return dot(first, right, 1, right_dim).astype(BF16).reshape(shape), send


def small_sum(x, axes):
    count = axes_size(axes)
    if count > 8 or count & (count - 1):
        return lax.psum(x, axes)
    total = x
    for mask in range(1, count):
        total = total + swap(x, axes, mask)
    return total


def partner_sum(parts, axes):
    total = parts[0].astype(F32)
    for mask in range(1, len(parts)):
        total = total + swap(parts[mask], axes, mask).astype(F32)
    return total


def partner_spread(x, axes):
    return [swap(x, axes, mask) if mask else x for mask in range(axes_size(axes))]


def turn_spread(x, axes):
    return turn(jnp.broadcast_to(x, (axes_size(axes),) + x.shape), axes)


def turn_sum(parts, axes):
    return jnp.sum(turn(parts, axes).astype(F32), axis=0)


def turn(x, axes):
    return lax.all_to_all(x, axes, split_axis=0, concat_axis=0, tiled=False)


def on_device(
    tokens,
    positions,
    captions,
    caption_lengths,
    conditioning,
    modulation_weight,
    modulation_bias,
    attention_gain,
    query_weight,
    key_weight,
    value_weight,
    query_gain,
    key_gain,
    text_weight,
    textkey_weight,
    textvalue_weight,
    textkey_gain,
    cross_gate,
    output_weight,
    feedforward_gain,
    gate_weight,
    up_weight,
    down_weight,
    cotangent,
):
    wide_count, narrow_count = lax.axis_size(W), lax.axis_size(N)
    clip_count = lax.axis_size(C)
    clip_index, wide_index = lax.axis_index(C), lax.axis_index(W)
    own_rows, model_width = tokens.shape[1], tokens.shape[2]
    head_size = query_gain.shape[0]
    head_count = model_width // head_size
    score_scale = head_size ** (-0.5)
    score_shift = 3.0 * math.sqrt(head_size)
    split_tokens = head_count % (wide_count * narrow_count) != 0
    tp, dp = ((N,), (C, W)) if split_tokens else (PLANE, (C,))
    tp_count, dp_count = axes_size(tp), axes_size(dp)
    tp_index = lax.axis_index(tp)
    masks = [0, 1, 4, 5, 2, 3, 6, 7]
    order = (tp_index ^ jnp.array(masks, jnp.int32)).astype(jnp.int32)
    clip_order = (clip_index ^ jnp.arange(clip_count, dtype=jnp.int32)).astype(jnp.int32)
    group_rows = own_rows * tp_count
    local_heads = head_count // tp_count
    head_width = local_heads * head_size
    weight_rows = query_weight.shape[0]
    hidden_rows, hidden_width = down_weight.shape[0], gate_weight.shape[1]
    local_hidden = hidden_width // tp_count

    text_rows, caption_rows = text_weight.shape[0], captions.shape[1]
    slot_count = caption_rows * narrow_count
    slot_part = slot_count // tp_count

    def gather_rows(rows):
        return lax.all_gather(rows, dp, axis=0, tiled=True)

    def scatter_rows(grads):
        return lax.psum_scatter(grads, dp, scatter_dimension=0, tiled=True)

    row_stack = gather_rows(jnp.concatenate([output_weight, text_weight], axis=0))
    row_stack = row_stack.reshape(dp_count, weight_rows + text_rows, model_width)

    head_parts_in = split_heads((textkey_weight, textvalue_weight, query_weight, key_weight, value_weight), tp_count)
    place_rows = jnp.stack([positions[0] // 64, positions[0] % 64]).astype(BF16)
    place_rows = jnp.pad(place_rows, ((0, 30), (0, model_width - own_rows)))
    bundle = jnp.concatenate([tokens[0], cotangent[0], place_rows], axis=0)
    head_parts_got = turn(head_parts_in, tp)
    head_slice = gather_rows(head_parts_got.reshape(tp_count * weight_rows, 5 * head_width))
    text_slice, qkv_slice = head_slice[:, : 2 * head_width], head_slice[:, 2 * head_width :]

    cond_float = conditioning.astype(F32)
    cond_act = jax.nn.silu(cond_float)
    cond_rows = jnp.stack([pick(cond_act, clip_order[at]) for at in range(clip_count)])
    weight_float = modulation_weight.astype(F32)
    partial_mod = jnp.dot(cond_rows, weight_float, precision=HIGHEST, preferred_element_type=F32)
    clip_mod = partner_sum([partial_mod[at] for at in range(clip_count)], (C,))
    own_mod = small_sum(clip_mod, PLANE) + modulation_bias
    own_mod, bundle = tie(own_mod, bundle)
    pieces = spread(bundle, tp, masks)
    shift_attn, scale_attn, gate_attn, shift_feed, scale_feed, gate_feed = jnp.split(own_mod, 6)

    hidden_in = split_groups((gate_weight, up_weight), tp_count, dp_count, hidden_rows)
    pieces[3], hidden_in = tie(pieces[3], hidden_in)
    hidden_parts, down_rows = tie(turn(hidden_in, tp), down_weight)
    hidden_slice = gather_rows(hidden_parts.reshape(tp_count * weight_rows, 2 * local_hidden))
    down_slice = gather_rows(down_rows)

    caption_sent = take_columns(captions[0], tp_index ^ jnp.arange(narrow_count), narrow_count, dp_count, tp_count, text_rows)
    caption_got = [swap(part, (N,), at) if at else part for at, part in enumerate(caption_sent)]
    narrow_order = (lax.axis_index(N) ^ jnp.arange(narrow_count, dtype=jnp.int32)).astype(jnp.int32)
    caption_columns = place([part[None] for part in caption_got], narrow_order).reshape(slot_count, -1)

    mod_in, dfeed, tails = modulate(
        pieces, attention_gain * (1.0 + scale_attn), shift_attn, gate_feed, own_rows, own_rows
    )
    position_all = (tails[:, 0].astype(F32) * 64.0 + tails[:, 1].astype(F32)).reshape(group_rows)
    cosine, sine = rope_tables(position_all, head_size, 2 * head_size)
    head_gain = jnp.concatenate([jnp.tile(query_gain, local_heads), jnp.tile(key_gain, local_heads)])

    output_rows = row_stack[:, :weight_rows].reshape(dp_count * weight_rows, model_width)
    text_own_rows = row_stack[:, weight_rows:].reshape(-1, model_width)
    text_parts = dot(caption_columns, text_own_rows).astype(BF16).reshape(tp_count, slot_part, model_width)
    text_own = turn_sum(text_parts, tp).astype(BF16)
    text_proj = turn_spread(text_own, tp).reshape(slot_count, model_width)
    output_pieces = [
        piece.reshape(dp_count, weight_rows, model_width) for piece in spread(output_rows, tp, masks)
    ]
    output_full = place(output_pieces, order).reshape(model_width, model_width)

    qkv_raw = dot(mod_in, qkv_slice)
    heads, value_own = prepare(qkv_raw, cosine, sine, head_gain, head_size)
    if split_tokens:
        keys_all, key_base = lax.all_gather(heads[:, head_width:], W, axis=0, tiled=True), 0
        values_all = lax.all_gather(value_own, W, axis=0, tiled=True)
    else:
        keys_all, values_all, key_base = heads, value_own, head_width
    own_out, denom = attend(heads, keys_all, key_base, values_all, head_size)
    keep = (jnp.arange(slot_count) < caption_lengths[clip_index]).astype(F32)
    text_raw = dot(text_proj, text_slice)
    text_key, text_value = prepare_text(text_raw, textkey_gain, head_width)
    text_gate = pick(jnp.tanh(cross_gate).reshape(tp_count, local_heads), tp_index)
    gate_lanes = jnp.repeat(text_gate, head_size)
    mixed, cross_out, text_denom = attend_text(
        order, heads, text_key, text_value, keep, gate_lanes, own_out, head_size
    )

    token_float = tokens[0].astype(F32)
    inv_attn = inverse_rms(token_float)
    hat_attn = token_float * inv_attn
    normed_attn = hat_attn * attention_gain
    mixed_own = turn(mixed, tp).transpose(1, 0, 2).reshape(own_rows, model_width)
    attn_out = dot(mixed_own, output_full)
    resid = token_float + gate_attn * attn_out
    inv_feed = inverse_rms(resid)
    hat_feed = resid * inv_feed
    normed_feed = hat_feed * feedforward_gain
    mod_own = (normed_feed * (1.0 + scale_feed) + shift_feed).astype(BF16)

    mod_ff, inner, dhidden = feed(spread(mod_own, tp, masks), hidden_slice, down_slice, dfeed)
    dmod_sum = Collect(*halves_product(dhidden, hidden_slice, 1, tp_count), tp, masks)
    dmod_sum.keep, mod_ff, dhidden = tie(dmod_sum.keep, mod_ff, dhidden)
    dmod_sum.first()
    dhidden_grads = dot(mod_ff, dhidden, 0, 0).astype(BF16)
    (dhidden_grads,) = dmod_sum.tie_second(dhidden_grads)
    ddown_grads = dot(inner, dfeed, 0, 0).astype(BF16)
    dmod_ff, ddown_grads = dmod_sum.tie_end(ddown_grads)
    dhidden_rows = scatter_rows(dhidden_grads)
    downweight_grad = scatter_rows(ddown_grads).astype(F32)

    dout = cotangent[0].astype(F32)
    dshift_feed = jnp.sum(dmod_ff, axis=0)
    dscale_feed = jnp.sum(dmod_ff * normed_feed, axis=0)
    dfeed_gain, dresid_norm = norm_backward(
        hat_feed, inv_feed, feedforward_gain, dmod_ff * (1.0 + scale_feed)
    )
    dresid = dout + dresid_norm
    dgate_attn = jnp.sum(dresid * attn_out, axis=0)
    dattn = (gate_attn * dresid).astype(BF16)

    dmixed_own = dot(dattn, output_full, 1, 1).astype(BF16)
    dmixed_own, inner, mixed_own = tie(dmixed_own, inner, mixed_own)
    dmixed = turn(dmixed_own.reshape(own_rows, tp_count, head_width).transpose(1, 0, 2), tp)
    feed_sum = Collect(*halves_product(inner, down_slice, 0, tp_count), tp, masks)
    feed_sum.keep, mixed_own = tie(feed_sum.keep, mixed_own)
    dout_parts = outer(
        mixed_own.T.reshape(dp_count, tp_count, weight_rows, own_rows), dattn, order
    ).reshape(tp_count, dp_count * weight_rows, model_width)
    dmixed, dout_parts = tie(dmixed, dout_parts)
    out_sum = Collect(dout_parts[: tp_count // 2], dout_parts[tp_count // 2 :], tp, masks)
    (dmixed,) = feed_sum.tie_first(dmixed)
    dquery_text, dtext_key, dtext_value, dgate_lanes = attend_back(
        order, heads, cross_out, text_denom, dmixed, text_key, 0, text_value, head_size, text=(keep, gate_lanes)
    )
    if split_tokens:
        dtext_key, dtext_value = lax.psum((dtext_key, dtext_value), W)
    dtext_heads, dtkey_gain = finish_text(text_raw, dtext_key, dtext_value, textkey_gain)
    dtext_parts = dot(dtext_heads, text_slice, 1, 1).astype(BF16).reshape(tp_count, slot_part, model_width)
    dtext_parts, dquery_text = tie(dtext_parts, dquery_text)
    dtext_turned = turn(dtext_parts, tp)
    (dquery_text,) = feed_sum.tie_second(dquery_text)
    shared = 1.0 / wide_count if split_tokens else 1.0
    dquery, dkey, dvalue = attend_back(
        order, heads, own_out, denom, dmixed, keys_all, key_base, values_all, head_size, start=dquery_text
    )
    dtext_turned, dquery = tie(dtext_turned, dquery)
    dtext_own = jnp.sum(dtext_turned.astype(F32), axis=0).astype(BF16)
    dtext_all = turn_spread(dtext_own, tp).reshape(slot_count, model_width)
    if split_tokens:
        dkey = lax.psum_scatter(dkey.astype(BF16), W, scatter_dimension=0, tiled=True)
        dvalue = lax.psum_scatter(dvalue.astype(BF16), W, scatter_dimension=0, tiled=True)
    dcross_gate = jnp.sum(dgate_lanes.reshape(local_heads, head_size), axis=1) * (1.0 - text_gate * text_gate)
    (dquery,) = out_sum.tie_first(dquery)
    dqkv, dhead_gain = finish(qkv_raw, dquery, dkey, dvalue, cosine, sine, head_gain, head_size)
    (dqkv,) = out_sum.tie_second(dqkv)

    middle = group_rows // 2
    shape = (tp_count // 2, own_rows, model_width)
    din_send = dot(dqkv[middle:], qkv_slice, 1, 1).astype(BF16).reshape(shape)
    dhidden_parts = turn(dhidden_rows.reshape(tp_count, weight_rows, 2 * local_hidden), tp)
    din_send, dqkv, dhidden_parts = tie(din_send, dqkv, dhidden_parts)
    dhead_grads = head_grads(text_proj, dtext_heads, mod_in, dqkv, shared)
    dhead_grads, dqkv = tie(dhead_grads, dqkv)
    dhead_rows = scatter_rows(dhead_grads)
    din_sum = Collect(dot(dqkv[:middle], qkv_slice, 1, 1).astype(BF16).reshape(shape), din_send, tp, masks)
    din_sum.first()
    feed_out, dtext_all = feed_sum.tie_end(dtext_all)
    dtext_grads = (dot(caption_columns, dtext_all, 0, 0) * shared).astype(BF16)
    textweight_grad = scatter_rows(dtext_grads).astype(F32)
    dcaption = dot(dtext_all, text_own_rows, 1, 1).astype(BF16).reshape(narrow_count, caption_rows, -1)
    (dcaption,) = din_sum.tie_second(dcaption)
    dmod_in = din_sum.end()

    dshift_attn = jnp.sum(dmod_in, axis=0)
    dscale_attn = jnp.sum(dmod_in * normed_attn, axis=0)
    dattn_gain, dtokens_norm = norm_backward(
        hat_attn, inv_attn, attention_gain, dmod_in * (1.0 + scale_attn)
    )
    tokens_grad = dresid + dtokens_norm
    block_output = resid + gate_feed * feed_out
    dgate_feed = jnp.sum(dout * feed_out, axis=0)
    head_range = jnp.arange(head_count) - tp_index * local_heads
    dgate_rows = jnp.sum(
        jnp.where(head_range[:, None] == jnp.arange(local_heads)[None, :], dcross_gate[None, :], 0.0), axis=1
    )
    dgains = jnp.sum(dhead_gain.reshape(2, local_heads, head_size), axis=1)
    pad = -head_count % head_size
    small = jnp.concatenate(
        [
            dshift_attn,
            dscale_attn,
            dgate_attn,
            dshift_feed,
            dscale_feed,
            dgate_feed,
            dattn_gain,
            dfeed_gain,
            dgains[0],
            dgains[1],
            dtkey_gain[0] * shared,
            dgate_rows,
            jnp.zeros((pad,), F32),
        ]
    )
    clip_small = jnp.stack(partner_spread(small_sum(small, PLANE), (C,)))
    mod_width = 6 * model_width
    dmod_all = clip_small[:, :mod_width]
    gains = jnp.sum(clip_small[:, mod_width:], axis=0)
    attngain_grad, feedgain_grad = gains[:model_width], gains[model_width : 2 * model_width]
    rest = gains[2 * model_width :]
    querygain_grad, keygain_grad, textgain_grad = (
        rest[:head_size],
        rest[head_size : 2 * head_size],
        rest[2 * head_size : 3 * head_size],
    )
    crossgate_grad = rest[3 * head_size : 3 * head_size + head_count]
    modweight_grad = jnp.dot(cond_rows.T, dmod_all, precision=HIGHEST, preferred_element_type=F32)
    dcond_rows = jnp.dot(dmod_all, weight_float.T, precision=HIGHEST, preferred_element_type=F32)
    dcond_act = jnp.stack([pick(dcond_rows, clip_order[at]) for at in range(clip_count)])
    sigmoid_cond = jax.nn.sigmoid(cond_float)
    conditioning_grad = dcond_act * sigmoid_cond * (1.0 + cond_float * (1.0 - sigmoid_cond))
    modbias_grad = jnp.sum(dmod_all, axis=0)

    dcaption_sent = jnp.broadcast_to(dcaption, (tp_count // narrow_count,) + dcaption.shape)
    dcaption_got = turn(dcaption_sent.reshape(tp_count, caption_rows, -1), tp)
    (captions_grad,) = join_groups(dcaption_got, dp_count, text_rows, 1)

    dout_group = out_sum.end().astype(BF16).reshape(dp_count, weight_rows, model_width)
    if split_tokens:
        outweight_grad = lax.psum_scatter(dout_group, dp, scatter_dimension=0, tiled=False).astype(F32)
    else:
        outweight_grad = partner_sum([pick(dout_group, clip_order[at]) for at in range(dp_count)], dp)
    gateweight_grad, upweight_grad = join_groups(dhidden_parts, dp_count, hidden_rows, 2)
    dhead_parts = turn(dhead_rows.reshape(tp_count, weight_rows, 5 * head_width), tp)
    textkey_grad, textvalue_grad, queryweight_grad, keyweight_grad, valueweight_grad = join_heads(
        dhead_parts, head_width
    )
    return (
        block_output[None],
        tokens_grad[None],
        captions_grad[None],
        conditioning_grad,
        modweight_grad,
        modbias_grad,
        attngain_grad,
        queryweight_grad,
        keyweight_grad,
        valueweight_grad,
        querygain_grad,
        keygain_grad,
        textweight_grad,
        textkey_grad,
        textvalue_grad,
        textgain_grad,
        crossgate_grad,
        outweight_grad,
        feedgain_grad,
        gateweight_grad,
        upweight_grad,
        downweight_grad,
    )


def solution(mesh):
    rows, whole = P(ALL, None), P()
    tokens, captions = P(C, PLANE, None), P(C, N, None)
    columns = P(None, ALL)
    return jax.shard_map(
        on_device,
        mesh=mesh,
        in_specs=(
            tokens,
            P(C, PLANE),
            captions,
            whole,
            columns,
            rows,
            whole,
            whole,
            rows,
            rows,
            rows,
            whole,
            whole,
            rows,
            rows,
            rows,
            whole,
            whole,
            rows,
            whole,
            rows,
            rows,
            rows,
            tokens,
        ),
        out_specs=(
            tokens,
            tokens,
            captions,
            columns,
            rows,
            whole,
            whole,
            rows,
            rows,
            rows,
            whole,
            whole,
            rows,
            rows,
            rows,
            whole,
            whole,
            rows,
            whole,
            rows,
            rows,
            rows,
        ),
        check_vma=False,
    )
```

```python
import functools
import math

import jax
import jax.numpy as jnp
import numpy as np
from jax import lax
from jax.experimental import pallas as pl
from jax.experimental.pallas import tpu as pltpu
from jax.sharding import PartitionSpec as P

EPSILON = 1e-06
ROPE_BASE = 10000.0
BLOCK = 512
C, W, N = "clip", "wide", "narrow"
ALL = (C, W, N)
PLANE = (W, N)
BF16, F32 = jnp.bfloat16, jnp.float32
HIGHEST = lax.Precision.HIGHEST


def dot(left, right, left_dim=1, right_dim=0):
    return lax.dot_general(
        left, right, (((left_dim,), (right_dim,)), ((), ())), preferred_element_type=F32
    )


def inverse_rms(values):
    return lax.rsqrt(jnp.mean(values * values, axis=-1, keepdims=True) + EPSILON)


def norm_backward(normed, inv_scale, gain, upstream):
    gain_grad = jnp.sum((upstream * normed).reshape(-1, normed.shape[-1]), axis=0)
    scaled = upstream * gain
    values_grad = inv_scale * (scaled - normed * jnp.mean(scaled * normed, axis=-1, keepdims=True))
    return (gain_grad, values_grad)


def rope_tables(positions, head_size, width):
    half_size = head_size // 2
    frequency = jnp.exp(-math.log(ROPE_BASE) * 2.0 * jnp.arange(half_size, dtype=F32) / head_size)
    angles = positions.astype(F32)[:, None] * jnp.tile(frequency, width // half_size)[None, :]
    sign = jnp.where(jnp.arange(width) % head_size < half_size, -1.0, 1.0)
    return (jnp.cos(angles), jnp.sin(angles) * sign[None, :])


def exact_dot(left, right):
    high = left.astype(BF16)
    low = (left - high.astype(F32)).astype(BF16)
    return dot(high, right) + dot(low, right)


def head_means(width, size):
    at = np.arange(width)
    return jnp.asarray((at[:, None] // size == at[None, :] // size) / size, BF16)


def half_swaps(width, size):
    at = np.arange(width)
    other = np.where(at % size < size // 2, at + size // 2, at - size // 2)
    return jnp.asarray(at[:, None] == other[None, :], BF16)


def widen(table, width):
    return jnp.concatenate([table] * (width // table.shape[1]), axis=1)


def full_spec(shape):
    return pl.BlockSpec(shape, lambda *_: (0,) * len(shape))


def row_spec(rows, width):
    return pl.BlockSpec((rows, width), lambda i, *_: (i, 0))


def struct(shape, dtype):
    return jax.ShapeDtypeStruct(shape, dtype)


def head_parts(width, size):
    return [slice(at, at + size) for at in range(0, width, size)]


def prepare_body(raw_ref, cos_ref, sin_ref, gain_ref, means_ref, swaps_ref, out_ref, value_ref):
    width = out_ref.shape[1]
    raw = raw_ref[:, :width]
    inv = lax.rsqrt(exact_dot(raw * raw, means_ref[...]) + EPSILON)
    normed = raw * inv * gain_ref[...]
    swapped = exact_dot(normed, swaps_ref[...])
    cosine, sine = widen(cos_ref[...], width), widen(sin_ref[...], width)
    out_ref[...] = (normed * cosine + swapped * sine).astype(BF16)
    value_ref[...] = raw_ref[:, width:].astype(BF16)


def prepare(raw, cosine, sine, gain, size):
    rows, width = raw.shape[0], gain.shape[0]
    block = math.gcd(rows, 256)
    return pl.pallas_call(
        prepare_body,
        grid=(rows // block,),
        in_specs=[
            row_spec(block, raw.shape[1]),
            row_spec(block, cosine.shape[1]),
            row_spec(block, cosine.shape[1]),
            full_spec((1, width)),
            full_spec((width, width)),
            full_spec((width, width)),
        ],
        out_specs=[row_spec(block, width), row_spec(block, raw.shape[1] - width)],
        out_shape=[struct((rows, width), BF16), struct((rows, raw.shape[1] - width), BF16)],
        name="prepare",
    )(raw, cosine, sine, gain[None], head_means(width, size), half_swaps(width, size))


def prepare_text_body(raw_ref, gain_ref, key_ref, value_ref):
    width, size = key_ref.shape[1], gain_ref.shape[1]
    raw, gain = raw_ref[...], gain_ref[...]
    heads = [raw[:, part] for part in head_parts(width, size)]
    heads = [head * inverse_rms(head) * gain for head in heads]
    key_ref[...] = jnp.concatenate(heads, axis=1).astype(BF16)
    value_ref[...] = raw[:, width:].astype(BF16)


def prepare_text(raw, gain, width):
    return pl.pallas_call(
        prepare_text_body, out_shape=[struct((raw.shape[0], width), BF16)] * 2, name="prepare_text"
    )(raw, gain[None])


def weights_of(left, right, factor, offset):
    scores = lax.dot_general(left, right, (((1,), (1,)), ((), ())), preferred_element_type=F32)
    return jnp.exp2(scores * factor - offset)


def attend_body(query_ref, key_ref, value_ref, out_ref, denom_ref, *, size, base, factor, offset):
    rows, width = out_ref.shape
    outs, denoms = [], []
    for part in head_parts(width, size):
        keys = key_ref[:, base + part.start : base + part.stop]
        wts = weights_of(query_ref[:, part], keys, factor, offset)
        denom = jnp.sum(wts, axis=1, keepdims=True)
        outs.append(dot(wts.astype(BF16), value_ref[:, part]) / denom)
        denoms.append(jnp.broadcast_to(denom, (rows, size)))
    out_ref[...] = jnp.concatenate(outs, axis=1)
    denom_ref[...] = jnp.concatenate(denoms, axis=1)


def score_constants(size):
    return {"factor": size**-0.5 / math.log(2.0), "offset": 3.0 * size**0.5 / math.log(2.0)}


def attend(query, keys, base, values, size):
    rows, width = query.shape[0], values.shape[1]
    block = math.gcd(rows, 256)
    return pl.pallas_call(
        functools.partial(attend_body, size=size, base=base, **score_constants(size)),
        grid=(rows // block,),
        in_specs=[row_spec(block, query.shape[1]), full_spec(keys.shape), full_spec(values.shape)],
        out_specs=[row_spec(block, width)] * 2,
        out_shape=[struct((rows, width), F32)] * 2,
        name="attend",
    )(query, keys, values)


def attend_text_body(
    order_ref,
    query_ref,
    key_ref,
    value_ref,
    keep_ref,
    gate_ref,
    own_ref,
    mixed_ref,
    cross_ref,
    denom_ref,
    *,
    size,
    factor,
    offset,
):
    rows, width = cross_ref.shape
    part_rows = mixed_ref.shape[2]
    keep = keep_ref[...]
    outs, denoms = [], []
    for part in head_parts(width, size):
        wts = weights_of(query_ref[:, part], key_ref[:, part], factor, offset) * keep
        denom = jnp.sum(wts, axis=1, keepdims=True)
        outs.append(dot(wts.astype(BF16), value_ref[:, part]) / denom)
        denoms.append(jnp.broadcast_to(denom, (rows, size)))
    cross = jnp.concatenate(outs, axis=1)
    cross_ref[...], denom_ref[...] = cross, jnp.concatenate(denoms, axis=1)
    mixed = (own_ref[...] + gate_ref[...] * cross).astype(BF16)
    first = pl.program_id(0) * (rows // part_rows)
    for index in range(rows // part_rows):
        mixed_ref[order_ref[first + index]] = mixed[index * part_rows : (index + 1) * part_rows].T


def attend_text(order, query, text_key, text_value, keep, gate, own, size):
    rows, width = own.shape
    slots, count = text_key.shape[0], order.shape[0]
    part_rows = rows // count
    block = part_rows * math.gcd(count, max(1, 512 // part_rows))
    return pl.pallas_call(
        functools.partial(attend_text_body, size=size, **score_constants(size)),
        grid_spec=pltpu.PrefetchScalarGridSpec(
            num_scalar_prefetch=1,
            grid=(rows // block,),
            in_specs=[
                row_spec(block, query.shape[1]),
                full_spec((slots, width)),
                full_spec((slots, width)),
                full_spec((1, slots)),
                full_spec((1, width)),
                row_spec(block, width),
            ],
            out_specs=[full_spec((count, width, part_rows))] + [row_spec(block, width)] * 2,
        ),
        out_shape=[struct((count, width, part_rows), BF16)] + [struct((rows, width), F32)] * 2,
        name="attend_text",
    )(order, query, text_key, text_value, keep[None], gate[None], own)


def attend_back_body(
    order_ref, query_ref, out_ref, denom_ref, dmixed_ref, key_ref, value_ref, *refs, size, base, factor, offset, text
):
    if text:
        keep_ref, gate_ref, dquery_ref, dkey_ref, dvalue_ref, dgate_ref = refs
    else:
        start_ref, dquery_ref, dkey_ref, dvalue_ref = refs
    rows, width = out_ref.shape
    part_rows = dmixed_ref.shape[2]
    step = pl.program_id(0)
    first = step * (rows // part_rows)
    dmixed = jnp.concatenate(
        [dmixed_ref[order_ref[first + index]].astype(F32).T for index in range(rows // part_rows)], axis=0
    )
    out, inv = out_ref[...], 1.0 / denom_ref[...]

    @pl.when(step == 0)
    def _():
        dkey_ref[...] = jnp.zeros_like(dkey_ref)
        dvalue_ref[...] = jnp.zeros_like(dvalue_ref)
        if text:
            dgate_ref[...] = jnp.zeros_like(dgate_ref)

    if text:
        dgate_ref[...] += jnp.sum(dmixed * out, axis=0, keepdims=True)
        dmixed = dmixed * gate_ref[...]
    dnumer = (dmixed * inv).astype(BF16)
    level = -(dmixed * out * inv)
    scale = size**-0.5
    results = []
    for part in head_parts(width, size):
        query, numer = query_ref[:, part], dnumer[:, part]
        keys = key_ref[:, base + part.start : base + part.stop]
        column = jnp.sum(level[:, part], axis=1, keepdims=True)
        level_row = jnp.broadcast_to(column, (rows, 128)).T[:1]
        wts = weights_of(keys, query, factor, offset)
        if text:
            wts = wts * jnp.broadcast_to(keep_ref[...], (128, wts.shape[0])).T[:, :1]
        dwts = lax.dot_general(
            value_ref[:, part], numer, (((1,), (1,)), ((), ())), preferred_element_type=F32
        )
        dscores = (wts * (dwts + level_row)).astype(BF16)
        dquery = (dot(keys.T, dscores) * scale).T
        results.append((dquery, dot(dscores, query) * scale, dot(wts.astype(BF16), numer)))
    dquery, dkey, dvalue = (jnp.concatenate(heads, axis=1) for heads in zip(*results))
    dquery_ref[...] = dquery if text else dquery + start_ref[...]
    dkey_ref[...] += dkey
    dvalue_ref[...] += dvalue


def attend_back(order, query, out, denom, dmixed, keys, base, values, size, text=None, start=None):
    rows, width = out.shape
    slots = keys.shape[0]
    part_rows = rows // order.shape[0]
    block = part_rows * math.gcd(order.shape[0], max(1, (256 if text is None else 512) // part_rows))
    if text is None:
        extra, extra_specs, ends = (start,), [row_spec(block, width)], []
    else:
        extra, ends = (text[0][None], text[1][None]), [(1, width)]
        extra_specs = [full_spec((1, slots)), full_spec((1, width))]
    return pl.pallas_call(
        functools.partial(
            attend_back_body, size=size, base=base, text=text is not None, **score_constants(size)
        ),
        grid_spec=pltpu.PrefetchScalarGridSpec(
            num_scalar_prefetch=1,
            grid=(rows // block,),
            in_specs=[row_spec(block, query.shape[1]), row_spec(block, width), row_spec(block, width)]
            + [full_spec(dmixed.shape), full_spec(keys.shape), full_spec(values.shape)]
            + extra_specs,
            out_specs=[row_spec(block, width)]
            + [full_spec(values.shape)] * 2
            + [full_spec(shape) for shape in ends],
        ),
        out_shape=[struct((rows, width), F32)]
        + [struct(values.shape, F32)] * 2
        + [struct(shape, F32) for shape in ends],
        name="text_back" if text else "attend_back",
    )(order, query, out, denom, dmixed, keys, values, *extra)


def norm_heads_back(raw, upstream, gain, size):
    gain_grad, grads = 0.0, []
    for part in head_parts(raw.shape[1], size):
        head, grad = raw[:, part], upstream[part.start // size]
        inv = inverse_rms(head)
        hat = head * inv
        gain_grad = gain_grad + jnp.sum(grad * hat, axis=0, keepdims=True)
        scaled = grad * gain
        grads.append(inv * (scaled - hat * jnp.mean(scaled * hat, axis=1, keepdims=True)))
    return gain_grad, jnp.concatenate(grads, axis=1)


def finish_body(
    raw_ref, dquery_ref, dkey_ref, dvalue_ref, cos_ref, sin_ref, gain_ref, means_ref, swaps_ref, out_ref, dgain_ref
):
    width = gain_ref.shape[1]

    @pl.when(pl.program_id(0) == 0)
    def _():
        dgain_ref[...] = jnp.zeros_like(dgain_ref)

    raw, means = raw_ref[:, :width], means_ref[...]
    inv = lax.rsqrt(exact_dot(raw * raw, means) + EPSILON)
    hat = raw * inv
    grad = jnp.concatenate([dquery_ref[...], dkey_ref[...].astype(F32)], axis=1)
    swapped = exact_dot(grad, swaps_ref[...])
    grad = grad * widen(cos_ref[...], width) - swapped * widen(sin_ref[...], width)
    dgain_ref[...] += jnp.sum(grad * hat, axis=0, keepdims=True)
    scaled = grad * gain_ref[...]
    out = inv * (scaled - hat * exact_dot(scaled * hat, means))
    out_ref[...] = jnp.concatenate([out.astype(BF16), dvalue_ref[...].astype(BF16)], axis=1)


def finish(raw, dquery, dkey, dvalue, cosine, sine, gain, size):
    rows, width = raw.shape[0], gain.shape[0]
    block = math.gcd(rows, 256)
    return pl.pallas_call(
        finish_body,
        grid=(rows // block,),
        in_specs=[row_spec(block, raw.shape[1])]
        + [row_spec(block, width // 2)] * 3
        + [row_spec(block, cosine.shape[1])] * 2
        + [full_spec((1, width)), full_spec((width, width)), full_spec((width, width))],
        out_specs=[row_spec(block, raw.shape[1]), full_spec((1, width))],
        out_shape=[struct(raw.shape, BF16), struct((1, width), F32)],
        name="finish",
    )(raw, dquery, dkey, dvalue, cosine, sine, gain[None], head_means(width, size), half_swaps(width, size))


def finish_text_body(raw_ref, dkey_ref, dvalue_ref, gain_in_ref, out_ref, gain_ref):
    width, size = dkey_ref.shape[1], gain_in_ref.shape[1]
    upstream = [dkey_ref[:, part] for part in head_parts(width, size)]
    gain_ref[...], grads = norm_heads_back(raw_ref[:, :width], upstream, gain_in_ref[...], size)
    out_ref[...] = jnp.concatenate([grads.astype(BF16), dvalue_ref[...].astype(BF16)], axis=1)


def finish_text(raw, dkey, dvalue, gain):
    return pl.pallas_call(
        finish_text_body,
        out_shape=[struct(raw.shape, BF16), struct((1, gain.shape[0]), F32)],
        name="finish_text",
    )(raw, dkey, dvalue, gain[None])


def join_body(parts_ref, *outs, width):
    for index, out_ref in enumerate(outs):
        for turn_index in range(parts_ref.shape[0]):
            at = turn_index * width
            out_ref[:, at : at + width] = parts_ref[turn_index, :, index * width : (index + 1) * width].astype(F32)


def join_heads(parts, width):
    count, rows, total = parts.shape
    return pl.pallas_call(
        functools.partial(join_body, width=width),
        out_shape=[struct((rows, count * width), F32)] * (total // width),
        name="join_heads",
    )(parts)


def join_groups_body(parts_ref, *outs, groups, width):
    count = parts_ref.shape[0]
    for index, out_ref in enumerate(outs):
        for group in range(groups):
            for turn_index in range(count):
                at = (group * count + turn_index) * width
                source = (index * groups + group) * width
                out_ref[:, at : at + width] = parts_ref[turn_index, :, source : source + width].astype(F32)


def join_groups(parts, groups, width, kinds):
    count, rows, _ = parts.shape
    return pl.pallas_call(
        functools.partial(join_groups_body, groups=groups, width=width),
        out_shape=[struct((rows, groups * count * width), F32)] * kinds,
        name="join_groups",
    )(parts)


def join_captions_body(wide_ref, narrow_ref, *refs, groups, wides):
    *pieces, out_ref = refs
    inner, _, total = pieces[0].shape
    width = total // groups
    for wide, piece in enumerate(pieces):
        for narrow in range(inner):
            for group in range(groups):
                device = wide_ref[wide] * inner + narrow_ref[narrow]
                to = pl.multiple_of((group * wides * inner + device) * width, width)
                part = piece[narrow, :, group * width : (group + 1) * width]
                out_ref[:, pl.ds(to, width)] = part.astype(F32)


def join_captions(pieces, wide_order, narrow_order, groups, wides):
    inner, rows, total = pieces[0].shape
    return pl.pallas_call(
        functools.partial(join_captions_body, groups=groups, wides=wides),
        grid_spec=pltpu.PrefetchScalarGridSpec(
            num_scalar_prefetch=2,
            grid=(1,),
            in_specs=[full_spec(pieces[0].shape)] * len(pieces),
            out_specs=full_spec((rows, len(pieces) * inner * total)),
        ),
        out_shape=struct((rows, len(pieces) * inner * total), F32),
        name="join_captions",
    )(wide_order, narrow_order, *pieces)


def split_heads_body(*refs, width):
    *ins, out_ref = refs
    for index, in_ref in enumerate(ins):
        for device in range(out_ref.shape[0]):
            at = device * width
            out_ref[device, :, index * width : (index + 1) * width] = in_ref[:, at : at + width]


def split_heads(weights, count):
    rows, columns = weights[0].shape
    width = columns // count
    return pl.pallas_call(
        functools.partial(split_heads_body, width=width),
        out_shape=struct((count, rows, len(weights) * width), BF16),
        name="split_heads",
    )(*weights)


def split_groups_body(*refs, groups, width):
    *ins, out_ref = refs
    count = out_ref.shape[0]
    for index, in_ref in enumerate(ins):
        for group in range(groups):
            for device in range(count):
                at, to = (group * count + device) * width, (index * groups + group) * width
                out_ref[device, :, to : to + width] = in_ref[:, at : at + width]


def split_groups(weights, count, groups, width):
    rows = weights[0].shape[0]
    return pl.pallas_call(
        functools.partial(split_groups_body, groups=groups, width=width),
        out_shape=struct((count, rows, len(weights) * groups * width), BF16),
        name="split_groups",
    )(*weights)


def take_columns_body(order_ref, in_ref, *outs, groups, count, width):
    for index, out_ref in enumerate(outs):
        for group in range(groups):
            at = pl.multiple_of((group * count + order_ref[index]) * width, width)
            out_ref[:, group * width : (group + 1) * width] = in_ref[:, pl.ds(at, width)]


def take_columns(values, order, takers, groups, count, width):
    rows = values.shape[0]
    if width % 128:
        split = values.reshape(rows, groups, count, width)
        return [pick(split, order[at], 2).reshape(rows, groups * width) for at in range(takers)]
    return pl.pallas_call(
        functools.partial(take_columns_body, groups=groups, count=count, width=width),
        grid_spec=pltpu.PrefetchScalarGridSpec(
            num_scalar_prefetch=1,
            grid=(1,),
            in_specs=[full_spec(values.shape)],
            out_specs=[full_spec((rows, groups * width))] * takers,
        ),
        out_shape=[struct((rows, groups * width), values.dtype)] * takers,
        name="take_columns",
    )(order, values)


def head_grads_body(text_ref, dtext_ref, mod_ref, dqkv_ref, out_ref, *, factor):
    text = dot(text_ref[...], dtext_ref[...], 0, 0) * factor
    out_ref[:, : text.shape[1]] = text.astype(BF16)
    out_ref[:, text.shape[1] :] = dot(mod_ref[...], dqkv_ref[...], 0, 0).astype(BF16)


def head_grads(text, dtext, mod, dqkv, factor):
    width, total = text.shape[1], dtext.shape[1] + dqkv.shape[1]
    block = math.gcd(width, 256)
    return pl.pallas_call(
        functools.partial(head_grads_body, factor=factor),
        grid=(width // block,),
        in_specs=[
            pl.BlockSpec((text.shape[0], block), lambda i: (0, i)),
            full_spec(dtext.shape),
            pl.BlockSpec((mod.shape[0], block), lambda i: (0, i)),
            full_spec(dqkv.shape),
        ],
        out_specs=row_spec(block, total),
        out_shape=struct((width, total), BF16),
        name="head_grads",
    )(text, dtext, mod, dqkv)


def feed_body(*refs, count, steps):
    pieces = refs[:count]
    stack_ref, dfeed_ref, mod_ref, inner_ref, dhidden_ref, weight_ref, down_ref, buffer, sems = refs[count:]
    step, per = pl.program_id(0), count // steps
    rows, hidden = pieces[0].shape[0], inner_ref.shape[1]

    def fetch(at):
        for index in range(per):
            pltpu.make_async_copy(
                pieces[at * per + index], buffer.at[at % 2, pl.ds(index * rows, rows)], sems.at[at % 2, index]
            ).start()

    @pl.when(step == 0)
    def _():
        fetch(0)
        groups = stack_ref.shape[0]
        rows_in, rows_down = weight_ref.shape[0] // groups, down_ref.shape[0] // groups
        for group in range(groups):
            at = 0
            for ref, size in ((weight_ref, rows_in), (down_ref, rows_down)):
                for column in range(0, ref.shape[1], BLOCK):
                    ref[group * size : (group + 1) * size, column : column + BLOCK] = stack_ref[group, at : at + size]
                    at += size

    for at in range(steps - 1):

        @pl.when(step == at)
        def _(at=at):
            fetch(at + 1)

    slot = step % 2
    for index in range(per):
        pltpu.make_async_copy(
            pieces[0], buffer.at[slot, pl.ds(index * rows, rows)], sems.at[slot, index]
        ).wait()
    mod = buffer[slot]
    mod_ref[...] = mod
    gate = dot(mod, weight_ref[:, :hidden])
    up = dot(mod, weight_ref[:, hidden:])
    sigmoid = 1.0 / (1.0 + jnp.exp(-gate))
    silu = gate * sigmoid
    inner = (silu * up).astype(BF16)
    inner_ref[...] = inner
    dinner = dot(dfeed_ref[...], down_ref[...], 1, 1)
    dhidden_ref[:, :hidden] = (dinner * up * (sigmoid * (1.0 + gate * (1.0 - sigmoid)))).astype(BF16)
    dhidden_ref[:, hidden:] = (dinner * silu).astype(BF16)


def stack_columns(values):
    rows, width = values.shape
    return values.reshape(rows, width // BLOCK, BLOCK).transpose(1, 0, 2).reshape(-1, BLOCK)


def feed(pieces, stack, hidden, dfeed):
    count = len(pieces)
    rows, width = pieces[0].shape
    steps = count // 2
    block = rows * 2
    return pl.pallas_call(
        functools.partial(feed_body, count=count, steps=steps),
        grid=(steps,),
        in_specs=[pl.BlockSpec(memory_space=pl.ANY)] * count
        + [full_spec(stack.shape), row_spec(block, width)],
        out_specs=[
            row_spec(block, width),
            row_spec(block, hidden),
            row_spec(block, 2 * hidden),
            full_spec((width, 2 * hidden)),
            full_spec((hidden, width)),
        ],
        out_shape=[
            struct((count * rows, width), BF16),
            struct((count * rows, hidden), BF16),
            struct((count * rows, 2 * hidden), BF16),
            struct((width, 2 * hidden), BF16),
            struct((hidden, width), BF16),
        ],
        scratch_shapes=[pltpu.VMEM((2, block, width), BF16), pltpu.SemaphoreType.DMA((2, 2))],
        name="feed",
    )(*pieces, stack, dfeed)


def place_body(order_ref, *refs):
    *pieces, out_ref = refs
    for at, piece in enumerate(pieces):
        out_ref[:, order_ref[at]] = piece[...]


def place(pieces, order):
    groups, rows, columns = pieces[0].shape
    return pl.pallas_call(
        place_body,
        grid_spec=pltpu.PrefetchScalarGridSpec(
            num_scalar_prefetch=1,
            grid=(groups,),
            in_specs=[pl.BlockSpec((1, rows, columns), lambda i, *_: (i, 0, 0))] * len(pieces),
            out_specs=pl.BlockSpec((1, len(pieces), rows, columns), lambda i, *_: (i, 0, 0, 0)),
        ),
        out_shape=struct((groups, len(pieces), rows, columns), pieces[0].dtype),
        name="place",
    )(order, *pieces)


def modulate_body(*refs, count, own_rows):
    pieces = refs[:count]
    scale_ref, shift_ref, gate_ref, mod_ref, dfeed_ref, tail_ref, buffer, sems = refs[count:]
    step = pl.program_id(0)

    def fetch(at):
        pltpu.make_async_copy(pieces[at], buffer.at[at % 2], sems.at[at % 2]).start()

    @pl.when(step == 0)
    def _():
        fetch(0)

    for at in range(count - 1):

        @pl.when(step == at)
        def _(at=at):
            fetch(at + 1)

    slot = step % 2
    pltpu.make_async_copy(pieces[0], buffer.at[slot], sems.at[slot]).wait()
    tokens = buffer[slot, :own_rows].astype(F32)
    mod_ref[...] = (tokens * inverse_rms(tokens) * scale_ref[...] + shift_ref[...]).astype(BF16)
    dfeed_ref[...] = (buffer[slot, own_rows : 2 * own_rows].astype(F32) * gate_ref[...]).astype(BF16)
    tail_ref[0] = buffer[slot, 2 * own_rows :, : tail_ref.shape[2]]


def modulate(pieces, scale, shift, gate, own_rows, tail_width):
    count = len(pieces)
    rows, width = pieces[0].shape
    tail = (1, rows - 2 * own_rows, tail_width)
    return pl.pallas_call(
        functools.partial(modulate_body, count=count, own_rows=own_rows),
        grid=(count,),
        in_specs=[pl.BlockSpec(memory_space=pl.ANY)] * count + [full_spec((1, width))] * 3,
        out_specs=[row_spec(own_rows, width)] * 2 + [pl.BlockSpec(tail, lambda i: (i, 0, 0))],
        out_shape=[struct((count * own_rows, width), BF16)] * 2 + [struct((count,) + tail[1:], BF16)],
        scratch_shapes=[pltpu.VMEM((2, rows, width), BF16), pltpu.SemaphoreType.DMA((2,))],
        name="modulate",
    )(*pieces, scale[None], shift[None], gate[None])


def late_body(order_ref, inner_ref, down_ref, first_ref, second_ref, dattn_ref, keep_ref, send_ref):
    groups, _, rows, tokens = first_ref.shape
    part_rows = inner_ref.shape[0] // 2
    feed = dot(inner_ref[...], down_ref[...]).astype(BF16)
    kept = pl.program_id(0) >= pl.num_programs(0) // 2
    for index, left_ref in enumerate((first_ref, second_ref)):
        outer = dot(left_ref[...].reshape(groups * rows, tokens), dattn_ref[...]).astype(BF16)
        part = feed[index * part_rows : (index + 1) * part_rows]

        @pl.when(kept)
        def _(index=index, outer=outer, part=part):
            keep_ref[index, :part_rows] = part
            keep_ref[index, part_rows:] = outer

        @pl.when(jnp.logical_not(kept))
        def _(index=index, outer=outer, part=part):
            send_ref[index, :part_rows] = part
            send_ref[index, part_rows:] = outer


def late_parts(inner, down, mixed, dattn, order):
    groups, count, rows, tokens = mixed.shape
    columns, half = down.shape[1], count // 2
    block = 2 * (inner.shape[0] // count)
    shape = (half, block // 2 + groups * rows, columns)

    def left(which):
        return pl.BlockSpec(
            (groups, 1, rows, tokens), lambda i, order_ref: (0, order_ref[(2 * i + which + half) % count], 0, 0)
        )

    return pl.pallas_call(
        late_body,
        grid_spec=pltpu.PrefetchScalarGridSpec(
            num_scalar_prefetch=1,
            grid=(half,),
            in_specs=[
                pl.BlockSpec((block, inner.shape[1]), lambda i, order_ref: ((i + half // 2) % half, 0)),
                full_spec(down.shape),
                left(0),
                left(1),
                full_spec(dattn.shape),
            ],
            out_specs=[
                pl.BlockSpec((2,) + shape[1:], lambda i, order_ref: (jnp.maximum(i - half // 2, 0), 0, 0)),
                pl.BlockSpec((2,) + shape[1:], lambda i, order_ref: (jnp.minimum(i, half // 2 - 1), 0, 0)),
            ],
        ),
        out_shape=[struct(shape, BF16)] * 2,
        name="late_parts",
    )(order, inner, down, mixed, mixed, dattn)


def axes_size(axes):
    return math.prod(lax.axis_size(axis) for axis in axes)


def swap(x, axes, mask):
    return lax.ppermute(x, axes, [(i, i ^ mask) for i in range(axes_size(axes))])


def pick(x, index, axis=0):
    return lax.dynamic_index_in_dim(x, index, axis, keepdims=False)


def spread(x, axes, masks, hold=None):
    first, second, fast = masks[1], masks[2], masks[4]
    half = x.shape[0] // 2
    one = swap(x, axes, first)
    two = swap(x, axes, second)
    if hold is not None:
        one, two, hold = tie(one, two, hold)
    far = jnp.concatenate([swap(two[:half], axes, first), swap(one[half:], axes, second)], axis=0)
    near = [x, one, two, far]
    pieces = near + [swap(piece, axes, fast) for piece in near]
    return pieces if hold is None else (pieces, hold)


class Collect:
    def __init__(self, keep, send, axes, masks):
        self.axes, self.masks, self.keep = axes, masks, keep
        self.got = swap(send, axes, masks[4])

    def exchange(self, x, index):
        return swap(x.astype(BF16), self.axes, self.masks[index])

    def part(self, slots, columns):
        return self.keep[slots, :, columns].astype(F32) + self.got[slots, :, columns].astype(F32)

    def first(self):
        half = self.keep.shape[2] // 2
        left, right = slice(0, half), slice(half, 2 * half)
        self.left_got = self.exchange(self.part(slice(1, 4, 2), left), 1)
        self.right_got = self.exchange(self.part(slice(2, 4), right), 2)
        self.left = [self.part(0, left), self.part(2, left)]
        self.right = [self.part(0, right), self.part(1, right)]

    def second(self):
        left_got, right_got = self.left_got.astype(F32), self.right_got.astype(F32)
        self.left_end = self.exchange(self.left[1] + left_got[1], 2)
        self.right_end = self.exchange(self.right[1] + right_got[1], 1)

    def end(self):
        left = self.left[0] + self.left_got[0].astype(F32) + self.left_end.astype(F32)
        right = self.right[0] + self.right_got[0].astype(F32) + self.right_end.astype(F32)
        return jnp.concatenate([left, right], axis=1)

    def tie_first(self, *others):
        self.got, *rest = tie(self.got, *others)
        self.first()
        return rest

    def tie_second(self, *others):
        self.left_got, self.right_got, *rest = tie(self.left_got, self.right_got, *others)
        self.second()
        return rest

    def tie_end(self, *others):
        self.left_end, self.right_end, *rest = tie(self.left_end, self.right_end, *others)
        return [self.end()] + rest


def tie(*values):
    return lax.optimization_barrier(values)


def halves_product(left, right, right_dim, count):
    middle = left.shape[0] // 2
    shape = (count // 2, left.shape[0] // count, right.shape[1 - right_dim])
    send = dot(left[middle:], right, 1, right_dim).astype(BF16).reshape(shape)
    send, first = tie(send, left[:middle])
    return dot(first, right, 1, right_dim).astype(BF16).reshape(shape), send


def small_sum(x, axes):
    count = axes_size(axes)
    if count > 8 or count & (count - 1):
        return lax.psum(x, axes)
    total = x
    for mask in range(1, count):
        total = total + swap(x, axes, mask)
    return total


def partner_sum(parts, axes):
    total = parts[0].astype(F32)
    for mask in range(1, len(parts)):
        total = total + swap(parts[mask], axes, mask).astype(F32)
    return total


def partner_spread(x, axes):
    return [swap(x, axes, mask) if mask else x for mask in range(axes_size(axes))]


def turn_spread(x, axes):
    return turn(jnp.broadcast_to(x, (axes_size(axes),) + x.shape), axes)


def turn_sum(parts, axes):
    return jnp.sum(turn(parts, axes).astype(F32), axis=0)


def turn(x, axes):
    return lax.all_to_all(x, axes, split_axis=0, concat_axis=0, tiled=False)


def on_device(
    tokens,
    positions,
    captions,
    caption_lengths,
    conditioning,
    modulation_weight,
    modulation_bias,
    attention_gain,
    query_weight,
    key_weight,
    value_weight,
    query_gain,
    key_gain,
    text_weight,
    textkey_weight,
    textvalue_weight,
    textkey_gain,
    cross_gate,
    output_weight,
    feedforward_gain,
    gate_weight,
    up_weight,
    down_weight,
    cotangent,
):
    wide_count, narrow_count = lax.axis_size(W), lax.axis_size(N)
    clip_count = lax.axis_size(C)
    clip_index, wide_index = lax.axis_index(C), lax.axis_index(W)
    own_rows, model_width = tokens.shape[1], tokens.shape[2]
    head_size = query_gain.shape[0]
    head_count = model_width // head_size
    score_scale = head_size ** (-0.5)
    score_shift = 3.0 * math.sqrt(head_size)
    split_tokens = head_count % (wide_count * narrow_count) != 0
    tp, dp = ((N,), (C, W)) if split_tokens else (PLANE, (C,))
    tp_count, dp_count = axes_size(tp), axes_size(dp)
    tp_index = lax.axis_index(tp)
    masks = [0, 1, 4, 5, 2, 3, 6, 7]
    order = (tp_index ^ jnp.array(masks, jnp.int32)).astype(jnp.int32)
    group_rows = own_rows * tp_count
    local_heads = head_count // tp_count
    head_width = local_heads * head_size
    weight_rows = query_weight.shape[0]
    hidden_rows, hidden_width = down_weight.shape[0], gate_weight.shape[1]
    local_hidden = hidden_width // tp_count

    text_rows, caption_rows = text_weight.shape[0], captions.shape[1]
    slot_count = caption_rows * narrow_count
    slot_part = slot_count // tp_count

    def gather_rows(rows):
        return lax.all_gather(rows, dp, axis=0, tiled=True)

    def scatter_rows(grads):
        return lax.psum_scatter(grads, dp, scatter_dimension=0, tiled=True)

    row_stack = gather_rows(jnp.concatenate([output_weight, text_weight], axis=0))
    row_stack = row_stack.reshape(dp_count, weight_rows + text_rows, model_width)

    cond_float = conditioning.astype(F32)
    cond_act = jax.nn.silu(cond_float)
    cond_rows = jnp.stack([pick(cond_act, clip_index ^ at) for at in range(clip_count)])
    weight_float = modulation_weight.astype(F32)
    partial_mod = jnp.dot(cond_rows, weight_float, precision=HIGHEST, preferred_element_type=F32)
    clip_mod = partner_sum([partial_mod[at] for at in range(clip_count)], (C,))

    head_parts_in = split_heads((textkey_weight, textvalue_weight, query_weight, key_weight, value_weight), tp_count)
    place_rows = jnp.stack([positions[0] // 64, positions[0] % 64]).astype(BF16)
    place_rows = jnp.pad(place_rows, ((0, 30), (0, model_width - own_rows)))
    bundle = jnp.concatenate([tokens[0], cotangent[0], place_rows], axis=0)
    head_parts_got, bundle = tie(turn(head_parts_in, tp), bundle)
    pieces, clip_mod = spread(bundle, tp, masks, clip_mod)
    hidden_in = split_groups((gate_weight, up_weight), tp_count, dp_count, hidden_rows)
    own_mod = small_sum(clip_mod, PLANE) + modulation_bias
    pieces[3], hidden_in, own_mod = tie(pieces[3], hidden_in, own_mod)
    shift_attn, scale_attn, gate_attn, shift_feed, scale_feed, gate_feed = jnp.split(own_mod, 6)
    hidden_parts = turn(hidden_in, tp)
    head_slice = gather_rows(head_parts_got.reshape(tp_count * weight_rows, 5 * head_width))
    text_slice, qkv_slice = head_slice[:, : 2 * head_width], head_slice[:, 2 * head_width :]

    caption_sent = take_columns(captions[0], tp_index ^ jnp.arange(narrow_count), narrow_count, dp_count, tp_count, text_rows)
    caption_got = [swap(part, (N,), at) if at else part for at, part in enumerate(caption_sent)]
    narrow_order = (lax.axis_index(N) ^ jnp.arange(narrow_count, dtype=jnp.int32)).astype(jnp.int32)
    caption_columns = place([part[None] for part in caption_got], narrow_order).reshape(slot_count, -1)

    mod_in, dfeed, tails = modulate(
        pieces, attention_gain * (1.0 + scale_attn), shift_attn, gate_feed, own_rows, own_rows
    )
    hidden_parts, mod_in = tie(hidden_parts, mod_in)
    feed_rows = [hidden_parts.reshape(tp_count * weight_rows, 2 * local_hidden), down_weight]
    feed_stack = gather_rows(jnp.concatenate([stack_columns(rows) for rows in feed_rows], axis=0))
    feed_stack = feed_stack.reshape(dp_count, -1, BLOCK)
    position_all = (tails[:, 0].astype(F32) * 64.0 + tails[:, 1].astype(F32)).reshape(group_rows)
    cosine, sine = rope_tables(position_all, head_size, 2 * head_size)
    head_gain = jnp.concatenate([jnp.tile(query_gain, local_heads), jnp.tile(key_gain, local_heads)])

    output_rows = row_stack[:, :weight_rows].reshape(dp_count * weight_rows, model_width)
    text_own_rows = row_stack[:, weight_rows:].reshape(-1, model_width)
    text_parts = dot(caption_columns, text_own_rows).astype(BF16).reshape(tp_count, slot_part, model_width)
    text_turned = turn(text_parts, tp)
    output_pieces = [
        piece.reshape(dp_count, weight_rows, model_width) for piece in spread(output_rows, tp, masks)
    ]
    output_full = place(output_pieces, order).reshape(model_width, model_width)

    qkv_raw = dot(mod_in, qkv_slice)
    text_turned, qkv_raw = tie(text_turned, qkv_raw)
    text_own = jnp.sum(text_turned.astype(F32), axis=0).astype(BF16)
    text_proj = turn_spread(text_own, tp).reshape(slot_count, model_width)
    heads, value_own = prepare(qkv_raw, cosine, sine, head_gain, head_size)
    if split_tokens:
        keys_all, key_base = lax.all_gather(heads[:, head_width:], W, axis=0, tiled=True), 0
        values_all = lax.all_gather(value_own, W, axis=0, tiled=True)
    else:
        keys_all, values_all, key_base = heads, value_own, head_width
    own_out, denom = attend(heads, keys_all, key_base, values_all, head_size)
    keep = (jnp.arange(slot_count) < caption_lengths[clip_index]).astype(F32)
    text_raw = dot(text_proj, text_slice)
    text_key, text_value = prepare_text(text_raw, textkey_gain, head_width)
    text_gate = pick(jnp.tanh(cross_gate).reshape(tp_count, local_heads), tp_index)
    gate_lanes = jnp.repeat(text_gate, head_size)
    mixed, cross_out, text_denom = attend_text(
        order, heads, text_key, text_value, keep, gate_lanes, own_out, head_size
    )

    token_float = tokens[0].astype(F32)
    inv_attn = inverse_rms(token_float)
    hat_attn = token_float * inv_attn
    normed_attn = hat_attn * attention_gain
    mixed_own = turn(mixed, tp).reshape(model_width, own_rows)
    attn_out = dot(mixed_own, output_full, 0, 0)
    resid = token_float + gate_attn * attn_out
    inv_feed = inverse_rms(resid)
    hat_feed = resid * inv_feed
    normed_feed = hat_feed * feedforward_gain
    mod_own = (normed_feed * (1.0 + scale_feed) + shift_feed).astype(BF16)

    mod_ff, inner, dhidden, hidden_slice, down_slice = feed(
        spread(mod_own, tp, masks), feed_stack, local_hidden, dfeed
    )
    dmod_sum = Collect(*halves_product(dhidden, hidden_slice, 1, tp_count), tp, masks)
    dmod_sum.keep, mod_ff, dhidden = tie(dmod_sum.keep, mod_ff, dhidden)
    dmod_sum.first()
    dhidden_grads = dot(mod_ff, dhidden, 0, 0).astype(BF16)
    (dhidden_grads,) = dmod_sum.tie_second(dhidden_grads)
    ddown_grads = dot(inner, dfeed, 0, 0).astype(BF16)
    dmod_ff, ddown_grads = dmod_sum.tie_end(ddown_grads)
    dhidden_rows = scatter_rows(dhidden_grads)
    down_rows = scatter_rows(ddown_grads)

    dout = cotangent[0].astype(F32)
    dshift_feed = jnp.sum(dmod_ff, axis=0)
    dscale_feed = jnp.sum(dmod_ff * normed_feed, axis=0)
    dfeed_gain, dresid_norm = norm_backward(
        hat_feed, inv_feed, feedforward_gain, dmod_ff * (1.0 + scale_feed)
    )
    dresid = dout + dresid_norm
    dgate_attn = jnp.sum(dresid * attn_out, axis=0)
    dattn = (gate_attn * dresid).astype(BF16)

    dmixed_own = dot(output_full, dattn, 1, 1).astype(BF16)
    dmixed_own, inner, mixed_own = tie(dmixed_own, inner, mixed_own)
    dmixed = turn(dmixed_own.reshape(tp_count, head_width, own_rows), tp)
    late_keep, late_send = late_parts(
        inner, down_slice, mixed_own.reshape(dp_count, tp_count, weight_rows, own_rows), dattn, order
    )
    dmixed, late_send = tie(dmixed, late_send)
    late_sum = Collect(late_keep, late_send, tp, masks)
    dquery_text, dtext_key, dtext_value, dgate_lanes = attend_back(
        order, heads, cross_out, text_denom, dmixed, text_key, 0, text_value, head_size, text=(keep, gate_lanes)
    )
    if split_tokens:
        dtext_key, dtext_value = lax.psum((dtext_key, dtext_value), W)
    dtext_heads, dtkey_gain = finish_text(text_raw, dtext_key, dtext_value, textkey_gain)
    dtext_heads, dquery_text = tie(dtext_heads, dquery_text)
    (dquery_text,) = late_sum.tie_first(dquery_text)
    late_sum.left[1], dquery_text = tie(late_sum.left[1], dquery_text)
    dquery, dkey, dvalue = attend_back(
        order, heads, own_out, denom, dmixed, keys_all, key_base, values_all, head_size, start=dquery_text
    )
    dhidden_rows, dquery = tie(dhidden_rows, dquery)
    dhidden_parts = turn(dhidden_rows.reshape(tp_count, weight_rows, 2 * local_hidden), tp)
    (dquery,) = late_sum.tie_second(dquery)
    if split_tokens:
        dkey = lax.psum_scatter(dkey.astype(BF16), W, scatter_dimension=0, tiled=True)
        dvalue = lax.psum_scatter(dvalue.astype(BF16), W, scatter_dimension=0, tiled=True)
    dcross_gate = jnp.sum(dgate_lanes.reshape(local_heads, head_size), axis=1) * (1.0 - text_gate * text_gate)
    dqkv, dhead_gain = finish(qkv_raw, dquery, dkey, dvalue, cosine, sine, head_gain, head_size)
    shared = 1.0 / wide_count if split_tokens else 1.0
    dhead_grads = head_grads(text_proj, dtext_heads, mod_in, dqkv, shared)
    dhead_grads, dqkv, dtext_heads, dhidden_parts = tie(dhead_grads, dqkv, dtext_heads, dhidden_parts)
    dhead_rows = scatter_rows(dhead_grads)

    dtext_parts = dot(dtext_heads, text_slice, 1, 1).astype(BF16).reshape(tp_count, slot_part, model_width)
    dtext_parts, dqkv = tie(dtext_parts, dqkv)
    dtext_turned = turn(dtext_parts, tp)
    middle = group_rows // 2
    shape = (tp_count // 2, own_rows, model_width)
    din_send = dot(dqkv[middle:], qkv_slice, 1, 1).astype(BF16).reshape(shape)
    din_send, dqkv = tie(din_send, dqkv)
    din_sum = Collect(dot(dqkv[:middle], qkv_slice, 1, 1).astype(BF16).reshape(shape), din_send, tp, masks)
    din_sum.first()
    dtext_turned, din_sum.left[1] = tie(dtext_turned, din_sum.left[1])
    dtext_own = jnp.sum(dtext_turned.astype(F32), axis=0).astype(BF16)
    late_own, dtext_own = late_sum.tie_end(dtext_own)
    dtext_all = turn_spread(dtext_own, tp).reshape(slot_count, model_width)
    feed_out, dout_group = late_own[:own_rows], late_own[own_rows:].astype(BF16)
    block_output = resid + gate_feed * feed_out
    dgate_feed = jnp.sum(dout * feed_out, axis=0)
    (dgate_feed,) = din_sum.tie_second(dgate_feed)
    dtext_grads = (dot(caption_columns, dtext_all, 0, 0) * shared).astype(BF16)
    dcaption = dot(dtext_all, text_own_rows, 1, 1).astype(BF16)
    dmod_in, dtext_grads, dcaption, down_rows = din_sum.tie_end(dtext_grads, dcaption, down_rows)
    dtext_rows = scatter_rows(dtext_grads)
    downweight_grad = down_rows.astype(F32)

    dshift_attn = jnp.sum(dmod_in, axis=0)
    dscale_attn = jnp.sum(dmod_in * normed_attn, axis=0)
    dattn_gain, dtokens_norm = norm_backward(
        hat_attn, inv_attn, attention_gain, dmod_in * (1.0 + scale_attn)
    )
    tokens_grad = dresid + dtokens_norm
    block_output = resid + gate_feed * feed_out
    dgate_feed = jnp.sum(dout * feed_out, axis=0)
    head_range = jnp.arange(head_count) - tp_index * local_heads
    dgate_rows = jnp.sum(
        jnp.where(head_range[:, None] == jnp.arange(local_heads)[None, :], dcross_gate[None, :], 0.0), axis=1
    )
    dgains = jnp.sum(dhead_gain.reshape(2, local_heads, head_size), axis=1)
    pad = -head_count % head_size
    small = jnp.concatenate(
        [
            dshift_attn,
            dscale_attn,
            dgate_attn,
            dshift_feed,
            dscale_feed,
            dgate_feed,
            dattn_gain,
            dfeed_gain,
            dgains[0],
            dgains[1],
            dtkey_gain[0] * shared,
            dgate_rows,
            jnp.zeros((pad,), F32),
        ]
    )
    dcaption = dcaption.reshape(narrow_count, caption_rows, -1)
    if not split_tokens:
        narrow_index = lax.axis_index(N)
        own_parts = [pick(dcaption, narrow_index ^ at) for at in range(narrow_count)]
        dcaption = jnp.stack([swap(part, (N,), at) if at else part for at, part in enumerate(own_parts)])
    plane_small, dcaption, dhead_rows = tie(small_sum(small, PLANE), dcaption, dhead_rows)
    dhead_parts = turn(dhead_rows.reshape(tp_count, weight_rows, 5 * head_width), tp)
    clip_small = jnp.stack(partner_spread(plane_small, (C,)))
    dout_group = dout_group.reshape(dp_count, weight_rows, model_width)
    if split_tokens:
        outweight_grad = lax.psum_scatter(dout_group, dp, scatter_dimension=0, tiled=False).astype(F32)
    else:
        outs = [pick(dout_group, clip_index ^ at) for at in range(dp_count)]
        outs = [outs[0]] + [swap(outs[at], dp, at) for at in range(1, dp_count)]
        *outs, clip_small = tie(*outs, clip_small)
        outweight_grad = functools.reduce(jnp.add, [out.astype(F32) for out in outs])
    mod_width = 6 * model_width
    dmod_all = clip_small[:, :mod_width]
    gains = jnp.sum(clip_small[:, mod_width:], axis=0)
    attngain_grad, feedgain_grad = gains[:model_width], gains[model_width : 2 * model_width]
    rest = gains[2 * model_width :]
    querygain_grad, keygain_grad, textgain_grad = (
        rest[:head_size],
        rest[head_size : 2 * head_size],
        rest[2 * head_size : 3 * head_size],
    )
    crossgate_grad = rest[3 * head_size : 3 * head_size + head_count]
    modweight_grad = jnp.dot(cond_rows.T, dmod_all, precision=HIGHEST, preferred_element_type=F32)
    dcond_rows = jnp.dot(dmod_all, weight_float.T, precision=HIGHEST, preferred_element_type=F32)
    dcond_act = jnp.stack([pick(dcond_rows, clip_index ^ at) for at in range(clip_count)])
    sigmoid_cond = jax.nn.sigmoid(cond_float)
    conditioning_grad = dcond_act * sigmoid_cond * (1.0 + cond_float * (1.0 - sigmoid_cond))
    modbias_grad = jnp.sum(dmod_all, axis=0)

    if split_tokens:
        captions_grad = join_groups(turn(dcaption, tp), dp_count, text_rows, 1)[0]
    else:
        far_parts = swap(dcaption, (W,), 2)
        wide_parts = [dcaption, far_parts, swap(dcaption, (W,), 1), swap(far_parts, (W,), 1)]
        wide_order = wide_index ^ jnp.array([0, 2, 1, 3], jnp.int32)
        captions_grad = join_captions(wide_parts, wide_order.astype(jnp.int32), narrow_order, dp_count, wide_count)

    gateweight_grad, upweight_grad = join_groups(dhidden_parts, dp_count, hidden_rows, 2)
    head_results = join_heads(dhead_parts, head_width)
    textvalue_grad, dtext_rows = tie(head_results[1], dtext_rows)
    textkey_grad, _, queryweight_grad, keyweight_grad, valueweight_grad = head_results
    textweight_grad = dtext_rows.astype(F32)
    return (
        block_output[None],
        tokens_grad[None],
        captions_grad[None],
        conditioning_grad,
        modweight_grad,
        modbias_grad,
        attngain_grad,
        queryweight_grad,
        keyweight_grad,
        valueweight_grad,
        querygain_grad,
        keygain_grad,
        textweight_grad,
        textkey_grad,
        textvalue_grad,
        textgain_grad,
        crossgate_grad,
        outweight_grad,
        feedgain_grad,
        gateweight_grad,
        upweight_grad,
        downweight_grad,
    )


def solution(mesh):
    rows, whole = P(ALL, None), P()
    tokens, captions = P(C, PLANE, None), P(C, N, None)
    columns = P(None, ALL)
    return jax.shard_map(
        on_device,
        mesh=mesh,
        in_specs=(
            tokens,
            P(C, PLANE),
            captions,
            whole,
            columns,
            rows,
            whole,
            whole,
            rows,
            rows,
            rows,
            whole,
            whole,
            rows,
            rows,
            rows,
            whole,
            whole,
            rows,
            whole,
            rows,
            rows,
            rows,
            tokens,
        ),
        out_specs=(
            tokens,
            tokens,
            captions,
            columns,
            rows,
            whole,
            whole,
            rows,
            rows,
            rows,
            whole,
            whole,
            rows,
            rows,
            rows,
            whole,
            whole,
            rows,
            whole,
            rows,
            rows,
            rows,
        ),
        check_vma=False,
    )
```

```python
import functools
import math

import jax
import jax.numpy as jnp
import numpy as np
from jax import lax
from jax.experimental import pallas as pl
from jax.experimental.pallas import tpu as pltpu
from jax.sharding import PartitionSpec as P

EPSILON = 1e-06
ROPE_BASE = 10000.0
BLOCK = 512
C, W, N = "clip", "wide", "narrow"
ALL = (C, W, N)
PLANE = (W, N)
BF16, F32 = jnp.bfloat16, jnp.float32
HIGHEST = lax.Precision.HIGHEST


def dot(left, right, left_dim=1, right_dim=0):
    return lax.dot_general(
        left, right, (((left_dim,), (right_dim,)), ((), ())), preferred_element_type=F32
    )


def inverse_rms(values):
    return lax.rsqrt(jnp.mean(values * values, axis=-1, keepdims=True) + EPSILON)


def norm_backward(normed, inv_scale, gain, upstream):
    gain_grad = jnp.sum((upstream * normed).reshape(-1, normed.shape[-1]), axis=0)
    scaled = upstream * gain
    values_grad = inv_scale * (scaled - normed * jnp.mean(scaled * normed, axis=-1, keepdims=True))
    return (gain_grad, values_grad)


def rope_tables(positions, head_size, width):
    half_size = head_size // 2
    frequency = jnp.exp(-math.log(ROPE_BASE) * 2.0 * jnp.arange(half_size, dtype=F32) / head_size)
    angles = positions.astype(F32)[:, None] * jnp.tile(frequency, width // half_size)[None, :]
    sign = jnp.where(jnp.arange(width) % head_size < half_size, -1.0, 1.0)
    return (jnp.cos(angles), jnp.sin(angles) * sign[None, :])


def exact_dot(left, right):
    high = left.astype(BF16)
    low = (left - high.astype(F32)).astype(BF16)
    return dot(high, right) + dot(low, right)


def head_means(width, size):
    at = np.arange(width)
    return jnp.asarray((at[:, None] // size == at[None, :] // size) / size, BF16)


def half_swaps(width, size):
    at = np.arange(width)
    other = np.where(at % size < size // 2, at + size // 2, at - size // 2)
    return jnp.asarray(at[:, None] == other[None, :], BF16)


def widen(table, width):
    return jnp.concatenate([table] * (width // table.shape[1]), axis=1)


def full_spec(shape):
    return pl.BlockSpec(shape, lambda *_: (0,) * len(shape))


def row_spec(rows, width):
    return pl.BlockSpec((rows, width), lambda i, *_: (i, 0))


def struct(shape, dtype):
    return jax.ShapeDtypeStruct(shape, dtype)


def head_parts(width, size):
    return [slice(at, at + size) for at in range(0, width, size)]


def prepare_body(raw_ref, cos_ref, sin_ref, gain_ref, means_ref, swaps_ref, out_ref, value_ref):
    width = out_ref.shape[1]
    raw = raw_ref[:, :width]
    inv = lax.rsqrt(exact_dot(raw * raw, means_ref[...]) + EPSILON)
    normed = raw * inv * gain_ref[...]
    swapped = exact_dot(normed, swaps_ref[...])
    cosine, sine = widen(cos_ref[...], width), widen(sin_ref[...], width)
    out_ref[...] = (normed * cosine + swapped * sine).astype(BF16)
    value_ref[...] = raw_ref[:, width:].astype(BF16)


def prepare(raw, cosine, sine, gain, size):
    rows, width = raw.shape[0], gain.shape[0]
    block = math.gcd(rows, 512)
    return pl.pallas_call(
        prepare_body,
        grid=(rows // block,),
        in_specs=[
            row_spec(block, raw.shape[1]),
            row_spec(block, cosine.shape[1]),
            row_spec(block, cosine.shape[1]),
            full_spec((1, width)),
            full_spec((width, width)),
            full_spec((width, width)),
        ],
        out_specs=[row_spec(block, width), row_spec(block, raw.shape[1] - width)],
        out_shape=[struct((rows, width), BF16), struct((rows, raw.shape[1] - width), BF16)],
        name="prepare",
    )(raw, cosine, sine, gain[None], head_means(width, size), half_swaps(width, size))


def prepare_text_body(raw_ref, gain_ref, key_ref, value_ref):
    width, size = key_ref.shape[1], gain_ref.shape[1]
    raw, gain = raw_ref[...], gain_ref[...]
    heads = [raw[:, part] for part in head_parts(width, size)]
    heads = [head * inverse_rms(head) * gain for head in heads]
    key_ref[...] = jnp.concatenate(heads, axis=1).astype(BF16)
    value_ref[...] = raw[:, width:].astype(BF16)


def prepare_text(raw, gain, width):
    return pl.pallas_call(
        prepare_text_body, out_shape=[struct((raw.shape[0], width), BF16)] * 2, name="prepare_text"
    )(raw, gain[None])


def weights_of(left, right, factor, offset):
    scores = lax.dot_general(left, right, (((1,), (1,)), ((), ())), preferred_element_type=F32)
    return jnp.exp2(scores * factor - offset)


def attend_body(query_ref, key_ref, value_ref, out_ref, denom_ref, *, size, base, factor, offset):
    rows, width = out_ref.shape
    outs, denoms = [], []
    for part in head_parts(width, size):
        keys = key_ref[:, base + part.start : base + part.stop]
        wts = weights_of(query_ref[:, part], keys, factor, offset)
        denom = jnp.sum(wts, axis=1, keepdims=True)
        outs.append(dot(wts.astype(BF16), value_ref[:, part]) / denom)
        denoms.append(jnp.broadcast_to(denom, (rows, size)))
    out_ref[...] = jnp.concatenate(outs, axis=1)
    denom_ref[...] = jnp.concatenate(denoms, axis=1)


def score_constants(size):
    return {"factor": size**-0.5 / math.log(2.0), "offset": 3.0 * size**0.5 / math.log(2.0)}


def attend(query, keys, base, values, size):
    rows, width = query.shape[0], values.shape[1]
    block = math.gcd(rows, 512)
    return pl.pallas_call(
        functools.partial(attend_body, size=size, base=base, **score_constants(size)),
        grid=(rows // block,),
        in_specs=[row_spec(block, query.shape[1]), full_spec(keys.shape), full_spec(values.shape)],
        out_specs=[row_spec(block, width)] * 2,
        out_shape=[struct((rows, width), F32)] * 2,
        name="attend",
    )(query, keys, values)


def attend_text_body(
    order_ref,
    query_ref,
    key_ref,
    value_ref,
    keep_ref,
    gate_ref,
    own_ref,
    mixed_ref,
    cross_ref,
    denom_ref,
    *,
    size,
    factor,
    offset,
):
    rows, width = cross_ref.shape
    part_rows = mixed_ref.shape[2]
    keep = keep_ref[...]
    outs, denoms = [], []
    for part in head_parts(width, size):
        wts = weights_of(query_ref[:, part], key_ref[:, part], factor, offset) * keep
        denom = jnp.sum(wts, axis=1, keepdims=True)
        outs.append(dot(wts.astype(BF16), value_ref[:, part]) / denom)
        denoms.append(jnp.broadcast_to(denom, (rows, size)))
    cross = jnp.concatenate(outs, axis=1)
    cross_ref[...], denom_ref[...] = cross, jnp.concatenate(denoms, axis=1)
    mixed = (own_ref[...] + gate_ref[...] * cross).astype(BF16)
    first = pl.program_id(0) * (rows // part_rows)
    for index in range(rows // part_rows):
        mixed_ref[order_ref[first + index]] = mixed[index * part_rows : (index + 1) * part_rows].T


def attend_text(order, query, text_key, text_value, keep, gate, own, size):
    rows, width = own.shape
    slots, count = text_key.shape[0], order.shape[0]
    part_rows = rows // count
    block = part_rows * math.gcd(count, max(1, 512 // part_rows))
    return pl.pallas_call(
        functools.partial(attend_text_body, size=size, **score_constants(size)),
        grid_spec=pltpu.PrefetchScalarGridSpec(
            num_scalar_prefetch=1,
            grid=(rows // block,),
            in_specs=[
                row_spec(block, query.shape[1]),
                full_spec((slots, width)),
                full_spec((slots, width)),
                full_spec((1, slots)),
                full_spec((1, width)),
                row_spec(block, width),
            ],
            out_specs=[full_spec((count, width, part_rows))] + [row_spec(block, width)] * 2,
        ),
        out_shape=[struct((count, width, part_rows), BF16)] + [struct((rows, width), F32)] * 2,
        name="attend_text",
    )(order, query, text_key, text_value, keep[None], gate[None], own)


def attend_back_body(
    order_ref,
    query_ref,
    own_ref,
    denom_ref,
    cross_ref,
    text_denom_ref,
    dmixed_ref,
    key_ref,
    value_ref,
    text_key_ref,
    text_value_ref,
    keep_ref,
    gate_ref,
    dquery_ref,
    dkey_ref,
    dvalue_ref,
    dtext_key_ref,
    dtext_value_ref,
    dgate_ref,
    *,
    size,
    base,
    factor,
    offset,
):
    rows, width = own_ref.shape
    part_rows = dmixed_ref.shape[2]
    step = pl.program_id(0)
    first = step * (rows // part_rows)
    dmixed = jnp.concatenate(
        [dmixed_ref[order_ref[first + index]].astype(F32).T for index in range(rows // part_rows)], axis=0
    )
    own, cross = own_ref[...], cross_ref[...]
    inv, text_inv = 1.0 / denom_ref[...], 1.0 / text_denom_ref[...]

    @pl.when(step == 0)
    def _():
        for ref in (dkey_ref, dvalue_ref, dtext_key_ref, dtext_value_ref, dgate_ref):
            ref[...] = jnp.zeros_like(ref)

    dgate_ref[...] += jnp.sum(dmixed * cross, axis=0, keepdims=True)
    dcross = dmixed * gate_ref[...]
    numer, text_numer = (dmixed * inv).astype(BF16), (dcross * text_inv).astype(BF16)
    level, text_level = -(dmixed * own * inv), -(dcross * cross * text_inv)
    keep = jnp.broadcast_to(keep_ref[...], (128, keep_ref.shape[1])).T[:, :1]
    scale = size**-0.5

    def back(query, keys, values, dnumer, levels, mask):
        column = jnp.sum(levels, axis=1, keepdims=True)
        level_row = jnp.broadcast_to(column, (rows, 128)).T[:1]
        wts = weights_of(keys, query, factor, offset)
        if mask is not None:
            wts = wts * mask
        dwts = lax.dot_general(values, dnumer, (((1,), (1,)), ((), ())), preferred_element_type=F32)
        dscores = (wts * (dwts + level_row)).astype(BF16)
        return dot(keys.T, dscores), dot(dscores, query) * scale, dot(wts.astype(BF16), dnumer)

    results = []
    for part in head_parts(width, size):
        query, keys = query_ref[:, part], key_ref[:, base + part.start : base + part.stop]
        dquery, dkey, dvalue = back(query, keys, value_ref[:, part], numer[:, part], level[:, part], None)
        text = back(
            query, text_key_ref[:, part], text_value_ref[:, part], text_numer[:, part], text_level[:, part], keep
        )
        results.append((((dquery + text[0]) * scale).T, dkey, dvalue, text[1], text[2]))
    dquery, dkey, dvalue, dtext_key, dtext_value = (
        jnp.concatenate(heads, axis=1) for heads in zip(*results)
    )
    dquery_ref[...] = dquery
    dkey_ref[...] += dkey
    dvalue_ref[...] += dvalue
    dtext_key_ref[...] += dtext_key
    dtext_value_ref[...] += dtext_value


def attend_back(order, query, saved, dmixed, keys, base, values, text_key, text_value, keep, gate, size):
    rows, width = saved[0].shape
    slots = text_key.shape[0]
    part_rows = rows // order.shape[0]
    block = part_rows * math.gcd(order.shape[0], max(1, 512 // part_rows))
    return pl.pallas_call(
        functools.partial(attend_back_body, size=size, base=base, **score_constants(size)),
        grid_spec=pltpu.PrefetchScalarGridSpec(
            num_scalar_prefetch=1,
            grid=(rows // block,),
            in_specs=[row_spec(block, query.shape[1])]
            + [row_spec(block, width)] * 4
            + [full_spec(x.shape) for x in (dmixed, keys, values, text_key, text_value)]
            + [full_spec((1, slots)), full_spec((1, width))],
            out_specs=[row_spec(block, width)]
            + [full_spec(x.shape) for x in (values, values, text_value, text_value)]
            + [full_spec((1, width))],
        ),
        out_shape=[struct((rows, width), F32)]
        + [struct(x.shape, F32) for x in (values, values, text_value, text_value)]
        + [struct((1, width), F32)],
        name="attend_back",
    )(order, query, *saved, dmixed, keys, values, text_key, text_value, keep[None], gate[None])


def norm_heads_back(raw, upstream, gain, size):
    gain_grad, grads = 0.0, []
    for part in head_parts(raw.shape[1], size):
        head, grad = raw[:, part], upstream[part.start // size]
        inv = inverse_rms(head)
        hat = head * inv
        gain_grad = gain_grad + jnp.sum(grad * hat, axis=0, keepdims=True)
        scaled = grad * gain
        grads.append(inv * (scaled - hat * jnp.mean(scaled * hat, axis=1, keepdims=True)))
    return gain_grad, jnp.concatenate(grads, axis=1)


def finish_body(
    raw_ref,
    dquery_ref,
    dkey_ref,
    dvalue_ref,
    cos_ref,
    sin_ref,
    gain_ref,
    means_ref,
    swaps_ref,
    text_raw_ref,
    dtext_key_ref,
    dtext_value_ref,
    text_gain_ref,
    out_ref,
    dgain_ref,
    dtext_ref,
    dtext_gain_ref,
):
    width = gain_ref.shape[1]

    @pl.when(pl.program_id(0) == 0)
    def _():
        dgain_ref[...] = jnp.zeros_like(dgain_ref)
        text_width, size = dtext_key_ref.shape[1], text_gain_ref.shape[1]
        upstream = [dtext_key_ref[:, part] for part in head_parts(text_width, size)]
        dtext_gain_ref[...], grads = norm_heads_back(
            text_raw_ref[:, :text_width], upstream, text_gain_ref[...], size
        )
        dtext_ref[...] = jnp.concatenate([grads.astype(BF16), dtext_value_ref[...].astype(BF16)], axis=1)

    raw, means = raw_ref[:, :width], means_ref[...]
    inv = lax.rsqrt(exact_dot(raw * raw, means) + EPSILON)
    hat = raw * inv
    grad = jnp.concatenate([dquery_ref[...], dkey_ref[...].astype(F32)], axis=1)
    swapped = exact_dot(grad, swaps_ref[...])
    grad = grad * widen(cos_ref[...], width) - swapped * widen(sin_ref[...], width)
    dgain_ref[...] += jnp.sum(grad * hat, axis=0, keepdims=True)
    scaled = grad * gain_ref[...]
    out = inv * (scaled - hat * exact_dot(scaled * hat, means))
    out_ref[...] = jnp.concatenate([out.astype(BF16), dvalue_ref[...].astype(BF16)], axis=1)


def finish(raw, dquery, dkey, dvalue, cosine, sine, gain, text_raw, dtext_key, dtext_value, text_gain):
    rows, width, size = raw.shape[0], gain.shape[0], text_gain.shape[0]
    block = math.gcd(rows, 512)
    return pl.pallas_call(
        finish_body,
        grid=(rows // block,),
        in_specs=[row_spec(block, raw.shape[1])]
        + [row_spec(block, width // 2)] * 3
        + [row_spec(block, cosine.shape[1])] * 2
        + [full_spec((1, width)), full_spec((width, width)), full_spec((width, width))]
        + [full_spec(x.shape) for x in (text_raw, dtext_key, dtext_value)]
        + [full_spec((1, size))],
        out_specs=[
            row_spec(block, raw.shape[1]),
            full_spec((1, width)),
            full_spec(text_raw.shape),
            full_spec((1, size)),
        ],
        out_shape=[
            struct(raw.shape, BF16),
            struct((1, width), F32),
            struct(text_raw.shape, BF16),
            struct((1, size), F32),
        ],
        name="finish",
    )(
        raw,
        dquery,
        dkey,
        dvalue,
        cosine,
        sine,
        gain[None],
        head_means(width, size),
        half_swaps(width, size),
        text_raw,
        dtext_key,
        dtext_value,
        text_gain[None],
    )


def join_body(parts_ref, *outs, width):
    for index, out_ref in enumerate(outs):
        for turn_index in range(parts_ref.shape[0]):
            at = turn_index * width
            out_ref[:, at : at + width] = parts_ref[turn_index, :, index * width : (index + 1) * width].astype(F32)


def join_heads(parts, width):
    count, rows, total = parts.shape
    return pl.pallas_call(
        functools.partial(join_body, width=width),
        out_shape=[struct((rows, count * width), F32)] * (total // width),
        name="join_heads",
    )(parts)


def join_groups_body(parts_ref, *outs, groups, width):
    count = parts_ref.shape[0]
    for index, out_ref in enumerate(outs):
        for group in range(groups):
            for turn_index in range(count):
                at = (group * count + turn_index) * width
                source = (index * groups + group) * width
                out_ref[:, at : at + width] = parts_ref[turn_index, :, source : source + width].astype(F32)


def join_groups(parts, groups, width, kinds):
    count, rows, _ = parts.shape
    return pl.pallas_call(
        functools.partial(join_groups_body, groups=groups, width=width),
        out_shape=[struct((rows, groups * count * width), F32)] * kinds,
        name="join_groups",
    )(parts)


def join_captions_body(wide_ref, narrow_ref, *refs, groups, wides):
    *pieces, out_ref = refs
    inner, _, total = pieces[0].shape
    width = total // groups
    for wide, piece in enumerate(pieces):
        for narrow in range(inner):
            for group in range(groups):
                device = wide_ref[wide] * inner + narrow_ref[narrow]
                to = pl.multiple_of((group * wides * inner + device) * width, width)
                part = piece[narrow, :, group * width : (group + 1) * width]
                out_ref[:, pl.ds(to, width)] = part.astype(F32)


def join_captions(pieces, wide_order, narrow_order, groups, wides):
    inner, rows, total = pieces[0].shape
    return pl.pallas_call(
        functools.partial(join_captions_body, groups=groups, wides=wides),
        grid_spec=pltpu.PrefetchScalarGridSpec(
            num_scalar_prefetch=2,
            grid=(1,),
            in_specs=[full_spec(pieces[0].shape)] * len(pieces),
            out_specs=full_spec((rows, len(pieces) * inner * total)),
        ),
        out_shape=struct((rows, len(pieces) * inner * total), F32),
        name="join_captions",
    )(wide_order, narrow_order, *pieces)


def split_heads_body(*refs, width):
    *ins, out_ref = refs
    for index, in_ref in enumerate(ins):
        for device in range(out_ref.shape[0]):
            at = device * width
            out_ref[device, :, index * width : (index + 1) * width] = in_ref[:, at : at + width]


def split_heads(weights, count):
    rows, columns = weights[0].shape
    width = columns // count
    return pl.pallas_call(
        functools.partial(split_heads_body, width=width),
        out_shape=struct((count, rows, len(weights) * width), BF16),
        name="split_heads",
    )(*weights)


def split_groups_body(*refs, groups, width):
    *ins, out_ref = refs
    count = out_ref.shape[0]
    for index, in_ref in enumerate(ins):
        for group in range(groups):
            for device in range(count):
                at, to = (group * count + device) * width, (index * groups + group) * width
                out_ref[device, :, to : to + width] = in_ref[:, at : at + width]


def split_groups(weights, count, groups, width):
    rows = weights[0].shape[0]
    return pl.pallas_call(
        functools.partial(split_groups_body, groups=groups, width=width),
        out_shape=struct((count, rows, len(weights) * groups * width), BF16),
        name="split_groups",
    )(*weights)


def take_columns_body(order_ref, in_ref, *outs, groups, count, width):
    for index, out_ref in enumerate(outs):
        for group in range(groups):
            at = pl.multiple_of((group * count + order_ref[index]) * width, width)
            out_ref[:, group * width : (group + 1) * width] = in_ref[:, pl.ds(at, width)]


def take_columns(values, order, takers, groups, count, width):
    rows = values.shape[0]
    if width % 128:
        split = values.reshape(rows, groups, count, width)
        return [pick(split, order[at], 2).reshape(rows, groups * width) for at in range(takers)]
    return pl.pallas_call(
        functools.partial(take_columns_body, groups=groups, count=count, width=width),
        grid_spec=pltpu.PrefetchScalarGridSpec(
            num_scalar_prefetch=1,
            grid=(1,),
            in_specs=[full_spec(values.shape)],
            out_specs=[full_spec((rows, groups * width))] * takers,
        ),
        out_shape=[struct((rows, groups * width), values.dtype)] * takers,
        name="take_columns",
    )(order, values)


def head_grads_body(text_ref, dtext_ref, mod_ref, dqkv_ref, out_ref, *, factor):
    text = dot(text_ref[...], dtext_ref[...], 0, 0) * factor
    out_ref[:, : text.shape[1]] = text.astype(BF16)
    out_ref[:, text.shape[1] :] = dot(mod_ref[...], dqkv_ref[...], 0, 0).astype(BF16)


def head_grads(text, dtext, mod, dqkv, factor):
    width, total = text.shape[1], dtext.shape[1] + dqkv.shape[1]
    block = math.gcd(width, 768)
    return pl.pallas_call(
        functools.partial(head_grads_body, factor=factor),
        grid=(width // block,),
        in_specs=[
            pl.BlockSpec((text.shape[0], block), lambda i: (0, i)),
            full_spec(dtext.shape),
            pl.BlockSpec((mod.shape[0], block), lambda i: (0, i)),
            full_spec(dqkv.shape),
        ],
        out_specs=row_spec(block, total),
        out_shape=struct((width, total), BF16),
        name="head_grads",
    )(text, dtext, mod, dqkv)


def feed_body(*refs, count, steps):
    pieces = refs[:count]
    stack_ref, dfeed_ref, mod_ref, inner_ref, dhidden_ref, weight_ref, down_ref, buffer, sems = refs[count:]
    step, per = pl.program_id(0), count // steps
    rows, hidden = pieces[0].shape[0], inner_ref.shape[1]

    def fetch(at):
        for index in range(per):
            pltpu.make_async_copy(
                pieces[at * per + index], buffer.at[at % 2, pl.ds(index * rows, rows)], sems.at[at % 2, index]
            ).start()

    @pl.when(step == 0)
    def _():
        fetch(0)
        groups = stack_ref.shape[0]
        rows_in, rows_down = weight_ref.shape[0] // groups, down_ref.shape[0] // groups
        for group in range(groups):
            at = 0
            for ref, size in ((weight_ref, rows_in), (down_ref, rows_down)):
                for column in range(0, ref.shape[1], BLOCK):
                    ref[group * size : (group + 1) * size, column : column + BLOCK] = stack_ref[group, at : at + size]
                    at += size

    for at in range(steps - 1):

        @pl.when(step == at)
        def _(at=at):
            fetch(at + 1)

    slot = step % 2
    for index in range(per):
        pltpu.make_async_copy(
            pieces[0], buffer.at[slot, pl.ds(index * rows, rows)], sems.at[slot, index]
        ).wait()
    mod = buffer[slot]
    mod_ref[...] = mod
    gate = dot(mod, weight_ref[:, :hidden])
    up = dot(mod, weight_ref[:, hidden:])
    sigmoid = 1.0 / (1.0 + jnp.exp(-gate))
    silu = gate * sigmoid
    inner = (silu * up).astype(BF16)
    inner_ref[...] = inner
    dinner = dot(dfeed_ref[...], down_ref[...], 1, 1)
    dhidden_ref[:, :hidden] = (dinner * up * (sigmoid * (1.0 + gate * (1.0 - sigmoid)))).astype(BF16)
    dhidden_ref[:, hidden:] = (dinner * silu).astype(BF16)


def stack_columns(values):
    rows, width = values.shape
    return values.reshape(rows, width // BLOCK, BLOCK).transpose(1, 0, 2).reshape(-1, BLOCK)


def feed(pieces, stack, hidden, dfeed):
    count = len(pieces)
    rows, width = pieces[0].shape
    steps = count // 2
    block = rows * 2
    return pl.pallas_call(
        functools.partial(feed_body, count=count, steps=steps),
        grid=(steps,),
        in_specs=[pl.BlockSpec(memory_space=pl.ANY)] * count
        + [full_spec(stack.shape), row_spec(block, width)],
        out_specs=[
            row_spec(block, width),
            row_spec(block, hidden),
            row_spec(block, 2 * hidden),
            full_spec((width, 2 * hidden)),
            full_spec((hidden, width)),
        ],
        out_shape=[
            struct((count * rows, width), BF16),
            struct((count * rows, hidden), BF16),
            struct((count * rows, 2 * hidden), BF16),
            struct((width, 2 * hidden), BF16),
            struct((hidden, width), BF16),
        ],
        scratch_shapes=[pltpu.VMEM((2, block, width), BF16), pltpu.SemaphoreType.DMA((2, 2))],
        name="feed",
    )(*pieces, stack, dfeed)


def place_body(order_ref, *refs):
    *pieces, out_ref = refs
    for at, piece in enumerate(pieces):
        out_ref[:, order_ref[at]] = piece[...]


def place(pieces, order):
    groups, rows, columns = pieces[0].shape
    return pl.pallas_call(
        place_body,
        grid_spec=pltpu.PrefetchScalarGridSpec(
            num_scalar_prefetch=1,
            grid=(groups,),
            in_specs=[pl.BlockSpec((1, rows, columns), lambda i, *_: (i, 0, 0))] * len(pieces),
            out_specs=pl.BlockSpec((1, len(pieces), rows, columns), lambda i, *_: (i, 0, 0, 0)),
        ),
        out_shape=struct((groups, len(pieces), rows, columns), pieces[0].dtype),
        name="place",
    )(order, *pieces)


def modulate_body(*refs, count, own_rows):
    pieces = refs[:count]
    scale_ref, shift_ref, gate_ref, mod_ref, dfeed_ref, tail_ref, buffer, sems = refs[count:]
    step = pl.program_id(0)

    @pl.when(step == 0)
    def _():
        for at, piece in enumerate(pieces):
            pltpu.make_async_copy(piece, buffer.at[at], sems.at[at]).start()

    pltpu.make_async_copy(pieces[0], buffer.at[step], sems.at[step]).wait()
    tokens = buffer[step, :own_rows].astype(F32)
    mod_ref[...] = (tokens * inverse_rms(tokens) * scale_ref[...] + shift_ref[...]).astype(BF16)
    dfeed_ref[...] = (buffer[step, own_rows : 2 * own_rows].astype(F32) * gate_ref[...]).astype(BF16)
    tail_ref[0] = buffer[step, 2 * own_rows :, : tail_ref.shape[2]]


def modulate(pieces, scale, shift, gate, own_rows, tail_width):
    count = len(pieces)
    rows, width = pieces[0].shape
    tail = (1, rows - 2 * own_rows, tail_width)
    return pl.pallas_call(
        functools.partial(modulate_body, count=count, own_rows=own_rows),
        grid=(count,),
        in_specs=[pl.BlockSpec(memory_space=pl.ANY)] * count + [full_spec((1, width))] * 3,
        out_specs=[row_spec(own_rows, width)] * 2 + [pl.BlockSpec(tail, lambda i: (i, 0, 0))],
        out_shape=[struct((count * own_rows, width), BF16)] * 2 + [struct((count,) + tail[1:], BF16)],
        scratch_shapes=[pltpu.VMEM((count, rows, width), BF16), pltpu.SemaphoreType.DMA((count,))],
        name="modulate",
    )(*pieces, scale[None], shift[None], gate[None])


def late_body(order_ref, inner_ref, down_ref, first_ref, second_ref, dattn_ref, keep_ref, send_ref):
    groups, _, rows, tokens = first_ref.shape
    part_rows = inner_ref.shape[0] // 2
    feed = dot(inner_ref[...], down_ref[...]).astype(BF16)
    kept = pl.program_id(0) >= pl.num_programs(0) // 2
    for index, left_ref in enumerate((first_ref, second_ref)):
        outer = dot(left_ref[...].reshape(groups * rows, tokens), dattn_ref[...]).astype(BF16)
        part = feed[index * part_rows : (index + 1) * part_rows]

        @pl.when(kept)
        def _(index=index, outer=outer, part=part):
            keep_ref[index, :part_rows] = part
            keep_ref[index, part_rows:] = outer

        @pl.when(jnp.logical_not(kept))
        def _(index=index, outer=outer, part=part):
            send_ref[index, :part_rows] = part
            send_ref[index, part_rows:] = outer


def late_parts(inner, down, mixed, dattn, order):
    groups, count, rows, tokens = mixed.shape
    columns, half = down.shape[1], count // 2
    block = 2 * (inner.shape[0] // count)
    shape = (half, block // 2 + groups * rows, columns)

    def left(which):
        return pl.BlockSpec(
            (groups, 1, rows, tokens), lambda i, order_ref: (0, order_ref[(2 * i + which + half) % count], 0, 0)
        )

    return pl.pallas_call(
        late_body,
        grid_spec=pltpu.PrefetchScalarGridSpec(
            num_scalar_prefetch=1,
            grid=(half,),
            in_specs=[
                pl.BlockSpec((block, inner.shape[1]), lambda i, order_ref: ((i + half // 2) % half, 0)),
                full_spec(down.shape),
                left(0),
                left(1),
                full_spec(dattn.shape),
            ],
            out_specs=[
                pl.BlockSpec((2,) + shape[1:], lambda i, order_ref: (jnp.maximum(i - half // 2, 0), 0, 0)),
                pl.BlockSpec((2,) + shape[1:], lambda i, order_ref: (jnp.minimum(i, half // 2 - 1), 0, 0)),
            ],
        ),
        out_shape=[struct(shape, BF16)] * 2,
        name="late_parts",
    )(order, inner, down, mixed, mixed, dattn)


def axes_size(axes):
    return math.prod(lax.axis_size(axis) for axis in axes)


def swap(x, axes, mask):
    return lax.ppermute(x, axes, [(i, i ^ mask) for i in range(axes_size(axes))])


def pick(x, index, axis=0):
    return lax.dynamic_index_in_dim(x, index, axis, keepdims=False)


def spread(x, axes, masks, hold=None):
    first, second, fast = masks[1], masks[2], masks[4]
    half = x.shape[0] // 2
    one = swap(x, axes, first)
    two = swap(x, axes, second)
    if hold is not None:
        one, two, hold = tie(one, two, hold)
    far = jnp.concatenate([swap(two[:half], axes, first), swap(one[half:], axes, second)], axis=0)
    near = [x, one, two, far]
    pieces = near + [swap(piece, axes, fast) for piece in near]
    return pieces if hold is None else (pieces, hold)


class Collect:
    def __init__(self, keep, send, axes, masks):
        self.axes, self.masks, self.keep = axes, masks, keep
        self.got = swap(send, axes, masks[4])

    def exchange(self, x, index):
        return swap(x.astype(BF16), self.axes, self.masks[index])

    def part(self, slots, columns):
        return self.keep[slots, :, columns].astype(F32) + self.got[slots, :, columns].astype(F32)

    def first(self):
        half = self.keep.shape[2] // 2
        left, right = slice(0, half), slice(half, 2 * half)
        self.left_got = self.exchange(self.part(slice(1, 4, 2), left), 1)
        self.right_got = self.exchange(self.part(slice(2, 4), right), 2)
        self.left = [self.part(0, left), self.part(2, left)]
        self.right = [self.part(0, right), self.part(1, right)]

    def second(self):
        left_got, right_got = self.left_got.astype(F32), self.right_got.astype(F32)
        self.left_end = self.exchange(self.left[1] + left_got[1], 2)
        self.right_end = self.exchange(self.right[1] + right_got[1], 1)

    def end(self):
        left = self.left[0] + self.left_got[0].astype(F32) + self.left_end.astype(F32)
        right = self.right[0] + self.right_got[0].astype(F32) + self.right_end.astype(F32)
        return jnp.concatenate([left, right], axis=1)

    def tie_first(self, *others):
        self.got, *rest = tie(self.got, *others)
        self.first()
        return rest

    def tie_second(self, *others):
        self.left_got, self.right_got, *rest = tie(self.left_got, self.right_got, *others)
        self.second()
        return rest

    def tie_end(self, *others):
        self.left_end, self.right_end, *rest = tie(self.left_end, self.right_end, *others)
        return [self.end()] + rest


def tie(*values):
    return lax.optimization_barrier(values)


def halves_product(left, right, right_dim, count):
    middle = left.shape[0] // 2
    shape = (count // 2, left.shape[0] // count, right.shape[1 - right_dim])
    send = dot(left[middle:], right, 1, right_dim).astype(BF16).reshape(shape)
    send, first = tie(send, left[:middle])
    return dot(first, right, 1, right_dim).astype(BF16).reshape(shape), send


def small_sum(x, axes):
    count = axes_size(axes)
    if count > 8 or count & (count - 1):
        return lax.psum(x, axes)
    total = x
    for mask in range(1, count):
        total = total + swap(x, axes, mask)
    return total


def partner_sum(parts, axes):
    total = parts[0].astype(F32)
    for mask in range(1, len(parts)):
        total = total + swap(parts[mask], axes, mask).astype(F32)
    return total


def partner_spread(x, axes):
    return [swap(x, axes, mask) if mask else x for mask in range(axes_size(axes))]


def turn_spread(x, axes):
    return turn(jnp.broadcast_to(x, (axes_size(axes),) + x.shape), axes)


def turn_sum(parts, axes):
    return jnp.sum(turn(parts, axes).astype(F32), axis=0)


def turn(x, axes):
    return lax.all_to_all(x, axes, split_axis=0, concat_axis=0, tiled=False)


def on_device(
    tokens,
    positions,
    captions,
    caption_lengths,
    conditioning,
    modulation_weight,
    modulation_bias,
    attention_gain,
    query_weight,
    key_weight,
    value_weight,
    query_gain,
    key_gain,
    text_weight,
    textkey_weight,
    textvalue_weight,
    textkey_gain,
    cross_gate,
    output_weight,
    feedforward_gain,
    gate_weight,
    up_weight,
    down_weight,
    cotangent,
):
    wide_count, narrow_count = lax.axis_size(W), lax.axis_size(N)
    clip_count = lax.axis_size(C)
    clip_index, wide_index = lax.axis_index(C), lax.axis_index(W)
    own_rows, model_width = tokens.shape[1], tokens.shape[2]
    head_size = query_gain.shape[0]
    head_count = model_width // head_size
    score_scale = head_size ** (-0.5)
    score_shift = 3.0 * math.sqrt(head_size)
    split_tokens = head_count % (wide_count * narrow_count) != 0
    tp, dp = ((N,), (C, W)) if split_tokens else (PLANE, (C,))
    tp_count, dp_count = axes_size(tp), axes_size(dp)
    tp_index = lax.axis_index(tp)
    masks = [0, 1, 4, 5, 2, 3, 6, 7]
    order = (tp_index ^ jnp.array(masks, jnp.int32)).astype(jnp.int32)
    group_rows = own_rows * tp_count
    local_heads = head_count // tp_count
    head_width = local_heads * head_size
    weight_rows = query_weight.shape[0]
    hidden_rows, hidden_width = down_weight.shape[0], gate_weight.shape[1]
    local_hidden = hidden_width // tp_count

    text_rows, caption_rows = text_weight.shape[0], captions.shape[1]
    slot_count = caption_rows * narrow_count
    slot_part = slot_count // tp_count

    def gather_rows(rows):
        return lax.all_gather(rows, dp, axis=0, tiled=True)

    def scatter_rows(grads):
        return lax.psum_scatter(grads, dp, scatter_dimension=0, tiled=True)

    row_stack = gather_rows(jnp.concatenate([output_weight, text_weight], axis=0))
    row_stack = row_stack.reshape(dp_count, weight_rows + text_rows, model_width)

    cond_float = conditioning.astype(F32)
    cond_act = jax.nn.silu(cond_float)
    cond_rows = jnp.stack([pick(cond_act, clip_index ^ at) for at in range(clip_count)])
    weight_float = modulation_weight.astype(F32)
    partial_mod = jnp.dot(cond_rows, weight_float, precision=HIGHEST, preferred_element_type=F32)
    clip_mod = partner_sum([partial_mod[at] for at in range(clip_count)], (C,))

    head_parts_in = split_heads((textkey_weight, textvalue_weight, query_weight, key_weight, value_weight), tp_count)
    place_rows = jnp.stack([positions[0] // 64, positions[0] % 64]).astype(BF16)
    place_rows = jnp.pad(place_rows, ((0, 30), (0, model_width - own_rows)))
    bundle = jnp.concatenate([tokens[0], cotangent[0], place_rows], axis=0)
    head_parts_got, bundle = tie(turn(head_parts_in, tp), bundle)
    pieces, clip_mod = spread(bundle, tp, masks, clip_mod)
    hidden_in = split_groups((gate_weight, up_weight), tp_count, dp_count, hidden_rows)
    own_mod = small_sum(clip_mod, PLANE) + modulation_bias
    pieces[3], hidden_in, own_mod = tie(pieces[3], hidden_in, own_mod)
    shift_attn, scale_attn, gate_attn, shift_feed, scale_feed, gate_feed = jnp.split(own_mod, 6)
    hidden_parts = turn(hidden_in, tp)
    head_slice = gather_rows(head_parts_got.reshape(tp_count * weight_rows, 5 * head_width))
    text_slice, qkv_slice = head_slice[:, : 2 * head_width], head_slice[:, 2 * head_width :]

    caption_sent = take_columns(captions[0], tp_index ^ jnp.arange(narrow_count), narrow_count, dp_count, tp_count, text_rows)
    caption_got = [swap(part, (N,), at) if at else part for at, part in enumerate(caption_sent)]
    narrow_order = (lax.axis_index(N) ^ jnp.arange(narrow_count, dtype=jnp.int32)).astype(jnp.int32)
    caption_columns = place([part[None] for part in caption_got], narrow_order).reshape(slot_count, -1)

    mod_in, dfeed, tails = modulate(
        pieces, attention_gain * (1.0 + scale_attn), shift_attn, gate_feed, own_rows, own_rows
    )
    hidden_parts, mod_in = tie(hidden_parts, mod_in)
    feed_rows = [hidden_parts.reshape(tp_count * weight_rows, 2 * local_hidden), down_weight]
    feed_stack = gather_rows(jnp.concatenate([stack_columns(rows) for rows in feed_rows], axis=0))
    feed_stack = feed_stack.reshape(dp_count, -1, BLOCK)
    position_all = (tails[:, 0].astype(F32) * 64.0 + tails[:, 1].astype(F32)).reshape(group_rows)
    cosine, sine = rope_tables(position_all, head_size, 2 * head_size)
    head_gain = jnp.concatenate([jnp.tile(query_gain, local_heads), jnp.tile(key_gain, local_heads)])

    output_rows = row_stack[:, :weight_rows].reshape(dp_count * weight_rows, model_width)
    text_own_rows = row_stack[:, weight_rows:].reshape(-1, model_width)
    text_parts = dot(caption_columns, text_own_rows).astype(BF16).reshape(tp_count, slot_part, model_width)
    text_turned = turn(text_parts, tp)
    output_pieces = [
        piece.reshape(dp_count, weight_rows, model_width) for piece in spread(output_rows, tp, masks)
    ]
    output_full = place(output_pieces, order).reshape(model_width, model_width)

    qkv_raw = dot(mod_in, qkv_slice)
    text_turned, qkv_raw = tie(text_turned, qkv_raw)
    text_own = jnp.sum(text_turned.astype(F32), axis=0).astype(BF16)
    text_proj = turn_spread(text_own, tp).reshape(slot_count, model_width)
    heads, value_own = prepare(qkv_raw, cosine, sine, head_gain, head_size)
    if split_tokens:
        keys_all, key_base = lax.all_gather(heads[:, head_width:], W, axis=0, tiled=True), 0
        values_all = lax.all_gather(value_own, W, axis=0, tiled=True)
    else:
        keys_all, values_all, key_base = heads, value_own, head_width
    own_out, denom = attend(heads, keys_all, key_base, values_all, head_size)
    keep = (jnp.arange(slot_count) < caption_lengths[clip_index]).astype(F32)
    text_raw = dot(text_proj, text_slice)
    text_key, text_value = prepare_text(text_raw, textkey_gain, head_width)
    text_gate = pick(jnp.tanh(cross_gate).reshape(tp_count, local_heads), tp_index)
    gate_lanes = jnp.repeat(text_gate, head_size)
    mixed, cross_out, text_denom = attend_text(
        order, heads, text_key, text_value, keep, gate_lanes, own_out, head_size
    )

    token_float = tokens[0].astype(F32)
    inv_attn = inverse_rms(token_float)
    hat_attn = token_float * inv_attn
    normed_attn = hat_attn * attention_gain
    mixed_own = turn(mixed, tp).reshape(model_width, own_rows)
    attn_out = dot(mixed_own, output_full, 0, 0)
    resid = token_float + gate_attn * attn_out
    inv_feed = inverse_rms(resid)
    hat_feed = resid * inv_feed
    normed_feed = hat_feed * feedforward_gain
    mod_own = (normed_feed * (1.0 + scale_feed) + shift_feed).astype(BF16)

    mod_ff, inner, dhidden, hidden_slice, down_slice = feed(
        spread(mod_own, tp, masks), feed_stack, local_hidden, dfeed
    )
    dmod_sum = Collect(*halves_product(dhidden, hidden_slice, 1, tp_count), tp, masks)
    dmod_sum.keep, mod_ff, dhidden = tie(dmod_sum.keep, mod_ff, dhidden)
    dmod_sum.first()
    dhidden_grads = dot(mod_ff, dhidden, 0, 0).astype(BF16)
    (dhidden_grads,) = dmod_sum.tie_second(dhidden_grads)
    ddown_grads = dot(inner, dfeed, 0, 0).astype(BF16)
    dmod_ff, ddown_grads = dmod_sum.tie_end(ddown_grads)
    dhidden_rows = scatter_rows(dhidden_grads)
    down_rows = scatter_rows(ddown_grads)

    dout = cotangent[0].astype(F32)
    dshift_feed = jnp.sum(dmod_ff, axis=0)
    dscale_feed = jnp.sum(dmod_ff * normed_feed, axis=0)
    dfeed_gain, dresid_norm = norm_backward(
        hat_feed, inv_feed, feedforward_gain, dmod_ff * (1.0 + scale_feed)
    )
    dresid = dout + dresid_norm
    dgate_attn = jnp.sum(dresid * attn_out, axis=0)
    dattn = (gate_attn * dresid).astype(BF16)

    dmixed_own = dot(output_full, dattn, 1, 1).astype(BF16)
    dmixed_own, inner, mixed_own = tie(dmixed_own, inner, mixed_own)
    dmixed = turn(dmixed_own.reshape(tp_count, head_width, own_rows), tp)
    late_keep, late_send = late_parts(
        inner, down_slice, mixed_own.reshape(dp_count, tp_count, weight_rows, own_rows), dattn, order
    )
    dmixed, late_send = tie(dmixed, late_send)
    late_sum = Collect(late_keep, late_send, tp, masks)
    (dmixed,) = late_sum.tie_first(dmixed)
    late_sum.left[1], dmixed = tie(late_sum.left[1], dmixed)
    saved = (own_out, denom, cross_out, text_denom)
    dquery, dkey, dvalue, dtext_key, dtext_value, dgate_lanes = attend_back(
        order, heads, saved, dmixed, keys_all, key_base, values_all, text_key, text_value, keep, gate_lanes, head_size
    )
    dhidden_rows, dquery = tie(dhidden_rows, dquery)
    dhidden_parts = turn(dhidden_rows.reshape(tp_count, weight_rows, 2 * local_hidden), tp)
    (dquery,) = late_sum.tie_second(dquery)
    if split_tokens:
        dkey = lax.psum_scatter(dkey.astype(BF16), W, scatter_dimension=0, tiled=True)
        dvalue = lax.psum_scatter(dvalue.astype(BF16), W, scatter_dimension=0, tiled=True)
        dtext_key, dtext_value = lax.psum((dtext_key, dtext_value), W)
    dcross_gate = jnp.sum(dgate_lanes.reshape(local_heads, head_size), axis=1) * (1.0 - text_gate * text_gate)
    dqkv, dhead_gain, dtext_heads, dtkey_gain = finish(
        qkv_raw, dquery, dkey, dvalue, cosine, sine, head_gain, text_raw, dtext_key, dtext_value, textkey_gain
    )
    shared = 1.0 / wide_count if split_tokens else 1.0
    dhead_grads = head_grads(text_proj, dtext_heads, mod_in, dqkv, shared)
    dhead_grads, dqkv, dtext_heads, dhidden_parts = tie(dhead_grads, dqkv, dtext_heads, dhidden_parts)
    dhead_rows = scatter_rows(dhead_grads)

    dtext_parts = dot(dtext_heads, text_slice, 1, 1).astype(BF16).reshape(tp_count, slot_part, model_width)
    dtext_parts, dqkv = tie(dtext_parts, dqkv)
    dtext_turned = turn(dtext_parts, tp)
    middle = group_rows // 2
    shape = (tp_count // 2, own_rows, model_width)
    din_send = dot(dqkv[middle:], qkv_slice, 1, 1).astype(BF16).reshape(shape)
    din_send, dqkv = tie(din_send, dqkv)
    din_sum = Collect(dot(dqkv[:middle], qkv_slice, 1, 1).astype(BF16).reshape(shape), din_send, tp, masks)
    din_sum.first()
    dtext_turned, din_sum.left[1] = tie(dtext_turned, din_sum.left[1])
    dtext_own = jnp.sum(dtext_turned.astype(F32), axis=0).astype(BF16)
    late_own, dtext_own = late_sum.tie_end(dtext_own)
    dtext_all = turn_spread(dtext_own, tp).reshape(slot_count, model_width)
    feed_out, dout_group = late_own[:own_rows], late_own[own_rows:].astype(BF16)
    block_output = resid + gate_feed * feed_out
    dgate_feed = jnp.sum(dout * feed_out, axis=0)
    (dgate_feed,) = din_sum.tie_second(dgate_feed)
    dtext_grads = (dot(caption_columns, dtext_all, 0, 0) * shared).astype(BF16)
    dcaption = dot(dtext_all, text_own_rows, 1, 1).astype(BF16)
    dmod_in, dtext_grads, dcaption, down_rows = din_sum.tie_end(dtext_grads, dcaption, down_rows)
    dtext_rows = scatter_rows(dtext_grads)
    downweight_grad = down_rows.astype(F32)

    dshift_attn = jnp.sum(dmod_in, axis=0)
    dscale_attn = jnp.sum(dmod_in * normed_attn, axis=0)
    dattn_gain, dtokens_norm = norm_backward(
        hat_attn, inv_attn, attention_gain, dmod_in * (1.0 + scale_attn)
    )
    tokens_grad = dresid + dtokens_norm
    block_output = resid + gate_feed * feed_out
    dgate_feed = jnp.sum(dout * feed_out, axis=0)
    head_range = jnp.arange(head_count) - tp_index * local_heads
    dgate_rows = jnp.sum(
        jnp.where(head_range[:, None] == jnp.arange(local_heads)[None, :], dcross_gate[None, :], 0.0), axis=1
    )
    dgains = jnp.sum(dhead_gain.reshape(2, local_heads, head_size), axis=1)
    pad = -head_count % head_size
    small = jnp.concatenate(
        [
            dshift_attn,
            dscale_attn,
            dgate_attn,
            dshift_feed,
            dscale_feed,
            dgate_feed,
            dattn_gain,
            dfeed_gain,
            dgains[0],
            dgains[1],
            dtkey_gain[0] * shared,
            dgate_rows,
            jnp.zeros((pad,), F32),
        ]
    )
    dcaption = dcaption.reshape(narrow_count, caption_rows, -1)
    if not split_tokens:
        narrow_index = lax.axis_index(N)
        own_parts = [pick(dcaption, narrow_index ^ at) for at in range(narrow_count)]
        dcaption = jnp.stack([swap(part, (N,), at) if at else part for at, part in enumerate(own_parts)])
    plane_small, dcaption, dhead_rows = tie(small_sum(small, PLANE), dcaption, dhead_rows)
    dhead_parts = turn(dhead_rows.reshape(tp_count, weight_rows, 5 * head_width), tp)
    clip_small = jnp.stack(partner_spread(plane_small, (C,)))
    dout_group = dout_group.reshape(dp_count, weight_rows, model_width)
    if split_tokens:
        outweight_grad = lax.psum_scatter(dout_group, dp, scatter_dimension=0, tiled=False).astype(F32)
    else:
        outs = [pick(dout_group, clip_index ^ at) for at in range(dp_count)]
        outs = [outs[0]] + [swap(outs[at], dp, at) for at in range(1, dp_count)]
        *outs, clip_small = tie(*outs, clip_small)
        outweight_grad = functools.reduce(jnp.add, [out.astype(F32) for out in outs])
    mod_width = 6 * model_width
    dmod_all = clip_small[:, :mod_width]
    gains = jnp.sum(clip_small[:, mod_width:], axis=0)
    attngain_grad, feedgain_grad = gains[:model_width], gains[model_width : 2 * model_width]
    rest = gains[2 * model_width :]
    querygain_grad, keygain_grad, textgain_grad = (
        rest[:head_size],
        rest[head_size : 2 * head_size],
        rest[2 * head_size : 3 * head_size],
    )
    crossgate_grad = rest[3 * head_size : 3 * head_size + head_count]
    modweight_grad = jnp.dot(cond_rows.T, dmod_all, precision=HIGHEST, preferred_element_type=F32)
    dcond_rows = jnp.dot(dmod_all, weight_float.T, precision=HIGHEST, preferred_element_type=F32)
    dcond_act = jnp.stack([pick(dcond_rows, clip_index ^ at) for at in range(clip_count)])
    sigmoid_cond = jax.nn.sigmoid(cond_float)
    conditioning_grad = dcond_act * sigmoid_cond * (1.0 + cond_float * (1.0 - sigmoid_cond))
    modbias_grad = jnp.sum(dmod_all, axis=0)

    if split_tokens:
        captions_grad = join_groups(turn(dcaption, tp), dp_count, text_rows, 1)[0]
    else:
        far_parts = swap(dcaption, (W,), 2)
        wide_parts = [dcaption, far_parts, swap(dcaption, (W,), 1), swap(far_parts, (W,), 1)]
        wide_order = wide_index ^ jnp.array([0, 2, 1, 3], jnp.int32)
        captions_grad = join_captions(wide_parts, wide_order.astype(jnp.int32), narrow_order, dp_count, wide_count)

    gateweight_grad, upweight_grad = join_groups(dhidden_parts, dp_count, hidden_rows, 2)
    head_results = join_heads(dhead_parts, head_width)
    textvalue_grad, dtext_rows = tie(head_results[1], dtext_rows)
    textkey_grad, _, queryweight_grad, keyweight_grad, valueweight_grad = head_results
    textweight_grad = dtext_rows.astype(F32)
    return (
        block_output[None],
        tokens_grad[None],
        captions_grad[None],
        conditioning_grad,
        modweight_grad,
        modbias_grad,
        attngain_grad,
        queryweight_grad,
        keyweight_grad,
        valueweight_grad,
        querygain_grad,
        keygain_grad,
        textweight_grad,
        textkey_grad,
        textvalue_grad,
        textgain_grad,
        crossgate_grad,
        outweight_grad,
        feedgain_grad,
        gateweight_grad,
        upweight_grad,
        downweight_grad,
    )


def solution(mesh):
    rows, whole = P(ALL, None), P()
    tokens, captions = P(C, PLANE, None), P(C, N, None)
    columns = P(None, ALL)
    return jax.shard_map(
        on_device,
        mesh=mesh,
        in_specs=(
            tokens,
            P(C, PLANE),
            captions,
            whole,
            columns,
            rows,
            whole,
            whole,
            rows,
            rows,
            rows,
            whole,
            whole,
            rows,
            rows,
            rows,
            whole,
            whole,
            rows,
            whole,
            rows,
            rows,
            rows,
            tokens,
        ),
        out_specs=(
            tokens,
            tokens,
            captions,
            columns,
            rows,
            whole,
            whole,
            rows,
            rows,
            rows,
            whole,
            whole,
            rows,
            rows,
            rows,
            whole,
            whole,
            rows,
            whole,
            rows,
            rows,
            rows,
        ),
        check_vma=False,
    )
```

```python
import functools
import math

import jax
import jax.numpy as jnp
import numpy as np
from jax import lax
from jax.experimental import pallas as pl
from jax.experimental.pallas import tpu as pltpu
from jax.sharding import PartitionSpec as P

EPSILON = 1e-06
ROPE_BASE = 10000.0
BLOCK = 512
C, W, N = "clip", "wide", "narrow"
ALL = (C, W, N)
PLANE = (W, N)
BF16, F32 = jnp.bfloat16, jnp.float32
HIGHEST = lax.Precision.HIGHEST


def dot(left, right, left_dim=1, right_dim=0):
    return lax.dot_general(
        left, right, (((left_dim,), (right_dim,)), ((), ())), preferred_element_type=F32
    )


def inverse_rms(values):
    return lax.rsqrt(jnp.mean(values * values, axis=-1, keepdims=True) + EPSILON)


def norm_backward(normed, inv_scale, gain, upstream):
    gain_grad = jnp.sum((upstream * normed).reshape(-1, normed.shape[-1]), axis=0)
    scaled = upstream * gain
    values_grad = inv_scale * (scaled - normed * jnp.mean(scaled * normed, axis=-1, keepdims=True))
    return (gain_grad, values_grad)


def rope_tables(positions, head_size, width):
    half_size = head_size // 2
    frequency = jnp.exp(-math.log(ROPE_BASE) * 2.0 * jnp.arange(half_size, dtype=F32) / head_size)
    angles = positions.astype(F32)[:, None] * jnp.tile(frequency, width // half_size)[None, :]
    sign = jnp.where(jnp.arange(width) % head_size < half_size, -1.0, 1.0)
    return (jnp.cos(angles), jnp.sin(angles) * sign[None, :])


def exact_dot(left, right):
    high = left.astype(BF16)
    low = (left - high.astype(F32)).astype(BF16)
    return dot(high, right) + dot(low, right)


def head_means(width, size):
    at = np.arange(width)
    return jnp.asarray((at[:, None] // size == at[None, :] // size) / size, BF16)


def half_swaps(width, size):
    at = np.arange(width)
    other = np.where(at % size < size // 2, at + size // 2, at - size // 2)
    return jnp.asarray(at[:, None] == other[None, :], BF16)


def widen(table, width):
    return jnp.concatenate([table] * (width // table.shape[1]), axis=1)


def full_spec(shape):
    return pl.BlockSpec(shape, lambda *_: (0,) * len(shape))


def row_spec(rows, width):
    return pl.BlockSpec((rows, width), lambda i, *_: (i, 0))


def struct(shape, dtype):
    return jax.ShapeDtypeStruct(shape, dtype)


def head_parts(width, size):
    return [slice(at, at + size) for at in range(0, width, size)]


def prepare_body(raw_ref, cos_ref, sin_ref, gain_ref, means_ref, swaps_ref, out_ref, value_ref):
    width = out_ref.shape[1]
    raw = raw_ref[:, :width]
    inv = lax.rsqrt(exact_dot(raw * raw, means_ref[...]) + EPSILON)
    normed = raw * inv * gain_ref[...]
    swapped = exact_dot(normed, swaps_ref[...])
    cosine, sine = widen(cos_ref[...], width), widen(sin_ref[...], width)
    out_ref[...] = (normed * cosine + swapped * sine).astype(BF16)
    value_ref[...] = raw_ref[:, width:].astype(BF16)


def prepare(raw, cosine, sine, gain, size):
    rows, width = raw.shape[0], gain.shape[0]
    block = math.gcd(rows, 512)
    return pl.pallas_call(
        prepare_body,
        grid=(rows // block,),
        in_specs=[
            row_spec(block, raw.shape[1]),
            row_spec(block, cosine.shape[1]),
            row_spec(block, cosine.shape[1]),
            full_spec((1, width)),
            full_spec((width, width)),
            full_spec((width, width)),
        ],
        out_specs=[row_spec(block, width), row_spec(block, raw.shape[1] - width)],
        out_shape=[struct((rows, width), BF16), struct((rows, raw.shape[1] - width), BF16)],
        name="prepare",
    )(raw, cosine, sine, gain[None], head_means(width, size), half_swaps(width, size))


def prepare_text_body(raw_ref, gain_ref, key_ref, value_ref):
    width, size = key_ref.shape[1], gain_ref.shape[1]
    raw, gain = raw_ref[...], gain_ref[...]
    heads = [raw[:, part] for part in head_parts(width, size)]
    heads = [head * inverse_rms(head) * gain for head in heads]
    key_ref[...] = jnp.concatenate(heads, axis=1).astype(BF16)
    value_ref[...] = raw[:, width:].astype(BF16)


def prepare_text(raw, gain, width):
    return pl.pallas_call(
        prepare_text_body, out_shape=[struct((raw.shape[0], width), BF16)] * 2, name="prepare_text"
    )(raw, gain[None])


def weights_of(left, right, factor, offset):
    scores = lax.dot_general(left, right, (((1,), (1,)), ((), ())), preferred_element_type=F32)
    return jnp.exp2(scores * factor - offset)


def attend_body(query_ref, key_ref, value_ref, out_ref, denom_ref, *, size, base, factor, offset):
    rows, width = out_ref.shape
    outs, denoms = [], []
    for part in head_parts(width, size):
        keys = key_ref[:, base + part.start : base + part.stop]
        wts = weights_of(query_ref[:, part], keys, factor, offset)
        denom = jnp.sum(wts, axis=1, keepdims=True)
        outs.append(dot(wts.astype(BF16), value_ref[:, part]) / denom)
        denoms.append(jnp.broadcast_to(denom, (rows, size)))
    out_ref[...] = jnp.concatenate(outs, axis=1)
    denom_ref[...] = jnp.concatenate(denoms, axis=1)


def score_constants(size):
    return {"factor": size**-0.5 / math.log(2.0), "offset": 3.0 * size**0.5 / math.log(2.0)}


def attend(query, keys, base, values, size):
    rows, width = query.shape[0], values.shape[1]
    block = math.gcd(rows, 512)
    return pl.pallas_call(
        functools.partial(attend_body, size=size, base=base, **score_constants(size)),
        grid=(rows // block,),
        in_specs=[row_spec(block, query.shape[1]), full_spec(keys.shape), full_spec(values.shape)],
        out_specs=[row_spec(block, width)] * 2,
        out_shape=[struct((rows, width), F32)] * 2,
        name="attend",
    )(query, keys, values)


def attend_text_body(
    order_ref,
    query_ref,
    key_ref,
    value_ref,
    keep_ref,
    gate_ref,
    own_ref,
    mixed_ref,
    cross_ref,
    denom_ref,
    *,
    size,
    factor,
    offset,
):
    rows, width = cross_ref.shape
    part_rows = mixed_ref.shape[2]
    keep = keep_ref[...]
    outs, denoms = [], []
    for part in head_parts(width, size):
        wts = weights_of(query_ref[:, part], key_ref[:, part], factor, offset) * keep
        denom = jnp.sum(wts, axis=1, keepdims=True)
        outs.append(dot(wts.astype(BF16), value_ref[:, part]) / denom)
        denoms.append(jnp.broadcast_to(denom, (rows, size)))
    cross = jnp.concatenate(outs, axis=1)
    cross_ref[...], denom_ref[...] = cross, jnp.concatenate(denoms, axis=1)
    mixed = (own_ref[...] + gate_ref[...] * cross).astype(BF16)
    first = pl.program_id(0) * (rows // part_rows)
    for index in range(rows // part_rows):
        mixed_ref[order_ref[first + index]] = mixed[index * part_rows : (index + 1) * part_rows].T


def attend_text(order, query, text_key, text_value, keep, gate, own, size):
    rows, width = own.shape
    slots, count = text_key.shape[0], order.shape[0]
    part_rows = rows // count
    block = part_rows * math.gcd(count, max(1, 512 // part_rows))
    return pl.pallas_call(
        functools.partial(attend_text_body, size=size, **score_constants(size)),
        grid_spec=pltpu.PrefetchScalarGridSpec(
            num_scalar_prefetch=1,
            grid=(rows // block,),
            in_specs=[
                row_spec(block, query.shape[1]),
                full_spec((slots, width)),
                full_spec((slots, width)),
                full_spec((1, slots)),
                full_spec((1, width)),
                row_spec(block, width),
            ],
            out_specs=[full_spec((count, width, part_rows))] + [row_spec(block, width)] * 2,
        ),
        out_shape=[struct((count, width, part_rows), BF16)] + [struct((rows, width), F32)] * 2,
        name="attend_text",
    )(order, query, text_key, text_value, keep[None], gate[None], own)


def attend_back_body(
    order_ref,
    query_ref,
    own_ref,
    denom_ref,
    cross_ref,
    text_denom_ref,
    dmixed_ref,
    key_ref,
    value_ref,
    text_key_ref,
    text_value_ref,
    keep_ref,
    gate_ref,
    dquery_ref,
    dkey_ref,
    dvalue_ref,
    dtext_key_ref,
    dtext_value_ref,
    dgate_ref,
    *,
    size,
    base,
    factor,
    offset,
):
    rows, width = own_ref.shape
    part_rows = dmixed_ref.shape[2]
    step = pl.program_id(0)
    first = step * (rows // part_rows)
    dmixed = jnp.concatenate(
        [dmixed_ref[order_ref[first + index]].astype(F32).T for index in range(rows // part_rows)], axis=0
    )
    own, cross = own_ref[...], cross_ref[...]
    inv, text_inv = 1.0 / denom_ref[...], 1.0 / text_denom_ref[...]

    @pl.when(step == 0)
    def _():
        for ref in (dkey_ref, dvalue_ref, dtext_key_ref, dtext_value_ref, dgate_ref):
            ref[...] = jnp.zeros_like(ref)

    dgate_ref[...] += jnp.sum(dmixed * cross, axis=0, keepdims=True)
    dcross = dmixed * gate_ref[...]
    numer, text_numer = (dmixed * inv).astype(BF16), (dcross * text_inv).astype(BF16)
    level, text_level = -(dmixed * own * inv), -(dcross * cross * text_inv)
    keep = jnp.broadcast_to(keep_ref[...], (128, keep_ref.shape[1])).T[:, :1]
    scale = size**-0.5

    def back(query, keys, values, dnumer, levels, mask):
        column = jnp.sum(levels, axis=1, keepdims=True)
        level_row = jnp.broadcast_to(column, (rows, 128)).T[:1]
        wts = weights_of(keys, query, factor, offset)
        if mask is not None:
            wts = wts * mask
        dwts = lax.dot_general(values, dnumer, (((1,), (1,)), ((), ())), preferred_element_type=F32)
        dscores = (wts * (dwts + level_row)).astype(BF16)
        return dot(keys.T, dscores), dot(dscores, query) * scale, dot(wts.astype(BF16), dnumer)

    results = []
    for part in head_parts(width, size):
        query, keys = query_ref[:, part], key_ref[:, base + part.start : base + part.stop]
        dquery, dkey, dvalue = back(query, keys, value_ref[:, part], numer[:, part], level[:, part], None)
        text = back(
            query, text_key_ref[:, part], text_value_ref[:, part], text_numer[:, part], text_level[:, part], keep
        )
        results.append((((dquery + text[0]) * scale).T, dkey, dvalue, text[1], text[2]))
    dquery, dkey, dvalue, dtext_key, dtext_value = (
        jnp.concatenate(heads, axis=1) for heads in zip(*results)
    )
    dquery_ref[...] = dquery
    dkey_ref[...] += dkey
    dvalue_ref[...] += dvalue
    dtext_key_ref[...] += dtext_key
    dtext_value_ref[...] += dtext_value


def attend_back(order, query, saved, dmixed, keys, base, values, text_key, text_value, keep, gate, size):
    rows, width = saved[0].shape
    slots = text_key.shape[0]
    part_rows = rows // order.shape[0]
    block = part_rows * math.gcd(order.shape[0], max(1, 512 // part_rows))
    return pl.pallas_call(
        functools.partial(attend_back_body, size=size, base=base, **score_constants(size)),
        grid_spec=pltpu.PrefetchScalarGridSpec(
            num_scalar_prefetch=1,
            grid=(rows // block,),
            in_specs=[row_spec(block, query.shape[1])]
            + [row_spec(block, width)] * 4
            + [full_spec(x.shape) for x in (dmixed, keys, values, text_key, text_value)]
            + [full_spec((1, slots)), full_spec((1, width))],
            out_specs=[row_spec(block, width)]
            + [full_spec(x.shape) for x in (values, values, text_value, text_value)]
            + [full_spec((1, width))],
        ),
        out_shape=[struct((rows, width), F32)]
        + [struct(x.shape, F32) for x in (values, values, text_value, text_value)]
        + [struct((1, width), F32)],
        name="attend_back",
    )(order, query, *saved, dmixed, keys, values, text_key, text_value, keep[None], gate[None])


def norm_heads_back(raw, upstream, gain, size):
    gain_grad, grads = 0.0, []
    for part in head_parts(raw.shape[1], size):
        head, grad = raw[:, part], upstream[part.start // size]
        inv = inverse_rms(head)
        hat = head * inv
        gain_grad = gain_grad + jnp.sum(grad * hat, axis=0, keepdims=True)
        scaled = grad * gain
        grads.append(inv * (scaled - hat * jnp.mean(scaled * hat, axis=1, keepdims=True)))
    return gain_grad, jnp.concatenate(grads, axis=1)


def finish_body(
    raw_ref,
    dquery_ref,
    dkey_ref,
    dvalue_ref,
    cos_ref,
    sin_ref,
    gain_ref,
    means_ref,
    swaps_ref,
    text_raw_ref,
    dtext_key_ref,
    dtext_value_ref,
    text_gain_ref,
    out_ref,
    dgain_ref,
    dtext_ref,
    dtext_gain_ref,
):
    width = gain_ref.shape[1]

    @pl.when(pl.program_id(0) == 0)
    def _():
        dgain_ref[...] = jnp.zeros_like(dgain_ref)
        text_width, size = dtext_key_ref.shape[1], text_gain_ref.shape[1]
        upstream = [dtext_key_ref[:, part] for part in head_parts(text_width, size)]
        dtext_gain_ref[...], grads = norm_heads_back(
            text_raw_ref[:, :text_width], upstream, text_gain_ref[...], size
        )
        dtext_ref[...] = jnp.concatenate([grads.astype(BF16), dtext_value_ref[...].astype(BF16)], axis=1)

    raw, means = raw_ref[:, :width], means_ref[...]
    inv = lax.rsqrt(exact_dot(raw * raw, means) + EPSILON)
    hat = raw * inv
    grad = jnp.concatenate([dquery_ref[...], dkey_ref[...].astype(F32)], axis=1)
    swapped = exact_dot(grad, swaps_ref[...])
    grad = grad * widen(cos_ref[...], width) - swapped * widen(sin_ref[...], width)
    dgain_ref[...] += jnp.sum(grad * hat, axis=0, keepdims=True)
    scaled = grad * gain_ref[...]
    out = inv * (scaled - hat * exact_dot(scaled * hat, means))
    out_ref[...] = jnp.concatenate([out.astype(BF16), dvalue_ref[...].astype(BF16)], axis=1)


def finish(raw, dquery, dkey, dvalue, cosine, sine, gain, text_raw, dtext_key, dtext_value, text_gain):
    rows, width, size = raw.shape[0], gain.shape[0], text_gain.shape[0]
    block = math.gcd(rows, 512)
    return pl.pallas_call(
        finish_body,
        grid=(rows // block,),
        in_specs=[row_spec(block, raw.shape[1])]
        + [row_spec(block, width // 2)] * 3
        + [row_spec(block, cosine.shape[1])] * 2
        + [full_spec((1, width)), full_spec((width, width)), full_spec((width, width))]
        + [full_spec(x.shape) for x in (text_raw, dtext_key, dtext_value)]
        + [full_spec((1, size))],
        out_specs=[
            row_spec(block, raw.shape[1]),
            full_spec((1, width)),
            full_spec(text_raw.shape),
            full_spec((1, size)),
        ],
        out_shape=[
            struct(raw.shape, BF16),
            struct((1, width), F32),
            struct(text_raw.shape, BF16),
            struct((1, size), F32),
        ],
        name="finish",
    )(
        raw,
        dquery,
        dkey,
        dvalue,
        cosine,
        sine,
        gain[None],
        head_means(width, size),
        half_swaps(width, size),
        text_raw,
        dtext_key,
        dtext_value,
        text_gain[None],
    )


def join_body(parts_ref, *outs, width):
    for index, out_ref in enumerate(outs):
        for turn_index in range(parts_ref.shape[0]):
            at = turn_index * width
            out_ref[:, at : at + width] = parts_ref[turn_index, :, index * width : (index + 1) * width].astype(F32)


def join_heads(parts, width):
    count, rows, total = parts.shape
    return pl.pallas_call(
        functools.partial(join_body, width=width),
        out_shape=[struct((rows, count * width), F32)] * (total // width),
        name="join_heads",
    )(parts)


def join_groups_body(parts_ref, *outs, groups, width):
    count = parts_ref.shape[0]
    for index, out_ref in enumerate(outs):
        for group in range(groups):
            for turn_index in range(count):
                at = (group * count + turn_index) * width
                source = (index * groups + group) * width
                out_ref[:, at : at + width] = parts_ref[turn_index, :, source : source + width].astype(F32)


def join_groups(parts, groups, width, kinds):
    count, rows, _ = parts.shape
    return pl.pallas_call(
        functools.partial(join_groups_body, groups=groups, width=width),
        out_shape=[struct((rows, groups * count * width), F32)] * kinds,
        name="join_groups",
    )(parts)


def join_captions_body(wide_ref, narrow_ref, *refs, groups, wides):
    *pieces, out_ref = refs
    inner, _, total = pieces[0].shape
    width = total // groups
    for wide, piece in enumerate(pieces):
        for narrow in range(inner):
            for group in range(groups):
                device = wide_ref[wide] * inner + narrow_ref[narrow]
                to = pl.multiple_of((group * wides * inner + device) * width, width)
                part = piece[narrow, :, group * width : (group + 1) * width]
                out_ref[:, pl.ds(to, width)] = part.astype(F32)


def join_captions(pieces, wide_order, narrow_order, groups, wides):
    inner, rows, total = pieces[0].shape
    return pl.pallas_call(
        functools.partial(join_captions_body, groups=groups, wides=wides),
        grid_spec=pltpu.PrefetchScalarGridSpec(
            num_scalar_prefetch=2,
            grid=(1,),
            in_specs=[full_spec(pieces[0].shape)] * len(pieces),
            out_specs=full_spec((rows, len(pieces) * inner * total)),
        ),
        out_shape=struct((rows, len(pieces) * inner * total), F32),
        name="join_captions",
    )(wide_order, narrow_order, *pieces)


def to_float_body(in_ref, out_ref):
    out_ref[...] = in_ref[...].astype(F32)


def to_float(values):
    rows, width = values.shape
    block = math.gcd(rows, 64)
    return pl.pallas_call(
        to_float_body,
        grid=(rows // block,),
        in_specs=[row_spec(block, width)],
        out_specs=row_spec(block, width),
        out_shape=struct((rows, width), F32),
        name="to_float",
    )(values)


def split_heads_body(*refs, width):
    *ins, out_ref = refs
    for index, in_ref in enumerate(ins):
        for device in range(out_ref.shape[0]):
            at = device * width
            out_ref[device, :, index * width : (index + 1) * width] = in_ref[:, at : at + width]


def split_heads(weights, count):
    rows, columns = weights[0].shape
    width = columns // count
    return pl.pallas_call(
        functools.partial(split_heads_body, width=width),
        out_shape=struct((count, rows, len(weights) * width), BF16),
        name="split_heads",
    )(*weights)


def split_groups_body(*refs, groups, width):
    *ins, out_ref = refs
    count = out_ref.shape[0]
    for index, in_ref in enumerate(ins):
        for group in range(groups):
            for device in range(count):
                at, to = (group * count + device) * width, (index * groups + group) * width
                out_ref[device, :, to : to + width] = in_ref[:, at : at + width]


def split_groups(weights, count, groups, width):
    rows = weights[0].shape[0]
    return pl.pallas_call(
        functools.partial(split_groups_body, groups=groups, width=width),
        out_shape=struct((count, rows, len(weights) * groups * width), BF16),
        name="split_groups",
    )(*weights)


def take_columns_body(order_ref, in_ref, *outs, groups, count, width):
    for index, out_ref in enumerate(outs):
        for group in range(groups):
            at = pl.multiple_of((group * count + order_ref[index]) * width, width)
            out_ref[:, group * width : (group + 1) * width] = in_ref[:, pl.ds(at, width)]


def take_columns(values, order, takers, groups, count, width):
    rows = values.shape[0]
    if width % 128:
        split = values.reshape(rows, groups, count, width)
        return [pick(split, order[at], 2).reshape(rows, groups * width) for at in range(takers)]
    return pl.pallas_call(
        functools.partial(take_columns_body, groups=groups, count=count, width=width),
        grid_spec=pltpu.PrefetchScalarGridSpec(
            num_scalar_prefetch=1,
            grid=(1,),
            in_specs=[full_spec(values.shape)],
            out_specs=[full_spec((rows, groups * width))] * takers,
        ),
        out_shape=[struct((rows, groups * width), values.dtype)] * takers,
        name="take_columns",
    )(order, values)


def head_grads_body(text_ref, dtext_ref, mod_ref, dqkv_ref, out_ref, *, factor):
    text = dot(text_ref[...], dtext_ref[...], 0, 0) * factor
    out_ref[:, : text.shape[1]] = text.astype(BF16)
    out_ref[:, text.shape[1] :] = dot(mod_ref[...], dqkv_ref[...], 0, 0).astype(BF16)


def head_grads(text, dtext, mod, dqkv, factor):
    width, total = text.shape[1], dtext.shape[1] + dqkv.shape[1]
    block = math.gcd(width, 768)
    return pl.pallas_call(
        functools.partial(head_grads_body, factor=factor),
        grid=(width // block,),
        in_specs=[
            pl.BlockSpec((text.shape[0], block), lambda i: (0, i)),
            full_spec(dtext.shape),
            pl.BlockSpec((mod.shape[0], block), lambda i: (0, i)),
            full_spec(dqkv.shape),
        ],
        out_specs=row_spec(block, total),
        out_shape=struct((width, total), BF16),
        name="head_grads",
    )(text, dtext, mod, dqkv)


def feed_body(*refs, count, steps):
    pieces = refs[:count]
    stack_ref, dfeed_ref, mod_ref, inner_ref, dhidden_ref, weight_ref, down_ref, buffer, sems = refs[count:]
    step, per = pl.program_id(0), count // steps
    rows, hidden = pieces[0].shape[0], inner_ref.shape[1]

    def fetch(at):
        for index in range(per):
            pltpu.make_async_copy(
                pieces[at * per + index], buffer.at[at % 2, pl.ds(index * rows, rows)], sems.at[at % 2, index]
            ).start()

    @pl.when(step == 0)
    def _():
        fetch(0)
        groups = stack_ref.shape[0]
        rows_in, rows_down = weight_ref.shape[0] // groups, down_ref.shape[0] // groups
        for group in range(groups):
            at = 0
            for ref, size in ((weight_ref, rows_in), (down_ref, rows_down)):
                for column in range(0, ref.shape[1], BLOCK):
                    ref[group * size : (group + 1) * size, column : column + BLOCK] = stack_ref[group, at : at + size]
                    at += size

    for at in range(steps - 1):

        @pl.when(step == at)
        def _(at=at):
            fetch(at + 1)

    slot = step % 2
    for index in range(per):
        pltpu.make_async_copy(
            pieces[0], buffer.at[slot, pl.ds(index * rows, rows)], sems.at[slot, index]
        ).wait()
    mod = buffer[slot]
    mod_ref[...] = mod
    gate = dot(mod, weight_ref[:, :hidden])
    up = dot(mod, weight_ref[:, hidden:])
    sigmoid = 1.0 / (1.0 + jnp.exp(-gate))
    silu = gate * sigmoid
    inner = (silu * up).astype(BF16)
    inner_ref[...] = inner
    dinner = dot(dfeed_ref[...], down_ref[...], 1, 1)
    dhidden_ref[:, :hidden] = (dinner * up * (sigmoid * (1.0 + gate * (1.0 - sigmoid)))).astype(BF16)
    dhidden_ref[:, hidden:] = (dinner * silu).astype(BF16)


def stack_columns(values):
    rows, width = values.shape
    return values.reshape(rows, width // BLOCK, BLOCK).transpose(1, 0, 2).reshape(-1, BLOCK)


def feed(pieces, stack, hidden, dfeed):
    count = len(pieces)
    rows, width = pieces[0].shape
    steps = count // 2
    block = rows * 2
    return pl.pallas_call(
        functools.partial(feed_body, count=count, steps=steps),
        grid=(steps,),
        in_specs=[pl.BlockSpec(memory_space=pl.ANY)] * count
        + [full_spec(stack.shape), row_spec(block, width)],
        out_specs=[
            row_spec(block, width),
            row_spec(block, hidden),
            row_spec(block, 2 * hidden),
            full_spec((width, 2 * hidden)),
            full_spec((hidden, width)),
        ],
        out_shape=[
            struct((count * rows, width), BF16),
            struct((count * rows, hidden), BF16),
            struct((count * rows, 2 * hidden), BF16),
            struct((width, 2 * hidden), BF16),
            struct((hidden, width), BF16),
        ],
        scratch_shapes=[pltpu.VMEM((2, block, width), BF16), pltpu.SemaphoreType.DMA((2, 2))],
        name="feed",
    )(*pieces, stack, dfeed)


def place_body(order_ref, *refs):
    *pieces, out_ref = refs
    for at, piece in enumerate(pieces):
        out_ref[:, order_ref[at]] = piece[...]


def place(pieces, order):
    groups, rows, columns = pieces[0].shape
    return pl.pallas_call(
        place_body,
        grid_spec=pltpu.PrefetchScalarGridSpec(
            num_scalar_prefetch=1,
            grid=(groups,),
            in_specs=[pl.BlockSpec((1, rows, columns), lambda i, *_: (i, 0, 0))] * len(pieces),
            out_specs=pl.BlockSpec((1, len(pieces), rows, columns), lambda i, *_: (i, 0, 0, 0)),
        ),
        out_shape=struct((groups, len(pieces), rows, columns), pieces[0].dtype),
        name="place",
    )(order, *pieces)


def modulate_body(*refs, count, own_rows):
    pieces = refs[:count]
    scale_ref, shift_ref, gate_ref, mod_ref, dfeed_ref, tail_ref, buffer, sems = refs[count:]
    step = pl.program_id(0)

    @pl.when(step == 0)
    def _():
        for at, piece in enumerate(pieces):
            pltpu.make_async_copy(piece, buffer.at[at], sems.at[at]).start()

    pltpu.make_async_copy(pieces[0], buffer.at[step], sems.at[step]).wait()
    tokens = buffer[step, :own_rows].astype(F32)
    mod_ref[...] = (tokens * inverse_rms(tokens) * scale_ref[...] + shift_ref[...]).astype(BF16)
    dfeed_ref[...] = (buffer[step, own_rows : 2 * own_rows].astype(F32) * gate_ref[...]).astype(BF16)
    tail_ref[0] = buffer[step, 2 * own_rows :, : tail_ref.shape[2]]


def modulate(pieces, scale, shift, gate, own_rows, tail_width):
    count = len(pieces)
    rows, width = pieces[0].shape
    tail = (1, rows - 2 * own_rows, tail_width)
    return pl.pallas_call(
        functools.partial(modulate_body, count=count, own_rows=own_rows),
        grid=(count,),
        in_specs=[pl.BlockSpec(memory_space=pl.ANY)] * count + [full_spec((1, width))] * 3,
        out_specs=[row_spec(own_rows, width)] * 2 + [pl.BlockSpec(tail, lambda i: (i, 0, 0))],
        out_shape=[struct((count * own_rows, width), BF16)] * 2 + [struct((count,) + tail[1:], BF16)],
        scratch_shapes=[pltpu.VMEM((count, rows, width), BF16), pltpu.SemaphoreType.DMA((count,))],
        name="modulate",
    )(*pieces, scale[None], shift[None], gate[None])


def late_body(order_ref, inner_ref, down_ref, first_ref, second_ref, dattn_ref, keep_ref, send_ref):
    groups, _, rows, tokens = first_ref.shape
    part_rows = inner_ref.shape[0] // 2
    feed = dot(inner_ref[...], down_ref[...]).astype(BF16)
    kept = pl.program_id(0) >= pl.num_programs(0) // 2
    for index, left_ref in enumerate((first_ref, second_ref)):
        outer = dot(left_ref[...].reshape(groups * rows, tokens), dattn_ref[...]).astype(BF16)
        part = feed[index * part_rows : (index + 1) * part_rows]

        @pl.when(kept)
        def _(index=index, outer=outer, part=part):
            keep_ref[index, :part_rows] = part
            keep_ref[index, part_rows:] = outer

        @pl.when(jnp.logical_not(kept))
        def _(index=index, outer=outer, part=part):
            send_ref[index, :part_rows] = part
            send_ref[index, part_rows:] = outer


def late_parts(inner, down, mixed, dattn, order):
    groups, count, rows, tokens = mixed.shape
    columns, half = down.shape[1], count // 2
    block = 2 * (inner.shape[0] // count)
    shape = (half, block // 2 + groups * rows, columns)

    def left(which):
        return pl.BlockSpec(
            (groups, 1, rows, tokens), lambda i, order_ref: (0, order_ref[(2 * i + which + half) % count], 0, 0)
        )

    return pl.pallas_call(
        late_body,
        grid_spec=pltpu.PrefetchScalarGridSpec(
            num_scalar_prefetch=1,
            grid=(half,),
            in_specs=[
                pl.BlockSpec((block, inner.shape[1]), lambda i, order_ref: ((i + half // 2) % half, 0)),
                full_spec(down.shape),
                left(0),
                left(1),
                full_spec(dattn.shape),
            ],
            out_specs=[
                pl.BlockSpec((2,) + shape[1:], lambda i, order_ref: (jnp.maximum(i - half // 2, 0), 0, 0)),
                pl.BlockSpec((2,) + shape[1:], lambda i, order_ref: (jnp.minimum(i, half // 2 - 1), 0, 0)),
            ],
        ),
        out_shape=[struct(shape, BF16)] * 2,
        name="late_parts",
    )(order, inner, down, mixed, mixed, dattn)


def axes_size(axes):
    return math.prod(lax.axis_size(axis) for axis in axes)


def swap(x, axes, mask):
    return lax.ppermute(x, axes, [(i, i ^ mask) for i in range(axes_size(axes))])


def pick(x, index, axis=0):
    return lax.dynamic_index_in_dim(x, index, axis, keepdims=False)


def spread(x, axes, masks, hold=None):
    first, second, fast = masks[1], masks[2], masks[4]
    half = x.shape[0] // 2
    one = swap(x, axes, first)
    two = swap(x, axes, second)
    if hold is not None:
        one, two, hold = tie(one, two, hold)
    far = jnp.concatenate([swap(two[:half], axes, first), swap(one[half:], axes, second)], axis=0)
    near = [x, one, two, far]
    pieces = near + [swap(piece, axes, fast) for piece in near]
    return pieces if hold is None else (pieces, hold)


class Collect:
    def __init__(self, keep, send, axes, masks):
        self.axes, self.masks, self.keep = axes, masks, keep
        self.got = swap(send, axes, masks[4])

    def exchange(self, x, index):
        return swap(x.astype(BF16), self.axes, self.masks[index])

    def part(self, slots, columns):
        return self.keep[slots, :, columns].astype(F32) + self.got[slots, :, columns].astype(F32)

    def first(self):
        half = self.keep.shape[2] // 2
        left, right = slice(0, half), slice(half, 2 * half)
        self.left_got = self.exchange(self.part(slice(1, 4, 2), left), 1)
        self.right_got = self.exchange(self.part(slice(2, 4), right), 2)
        self.left = [self.part(0, left), self.part(2, left)]
        self.right = [self.part(0, right), self.part(1, right)]

    def second(self):
        left_got, right_got = self.left_got.astype(F32), self.right_got.astype(F32)
        self.left_end = self.exchange(self.left[1] + left_got[1], 2)
        self.right_end = self.exchange(self.right[1] + right_got[1], 1)

    def end(self):
        left = self.left[0] + self.left_got[0].astype(F32) + self.left_end.astype(F32)
        right = self.right[0] + self.right_got[0].astype(F32) + self.right_end.astype(F32)
        return jnp.concatenate([left, right], axis=1)

    def tie_first(self, *others):
        self.got, *rest = tie(self.got, *others)
        self.first()
        return rest

    def tie_second(self, *others):
        self.left_got, self.right_got, *rest = tie(self.left_got, self.right_got, *others)
        self.second()
        return rest

    def tie_end(self, *others):
        self.left_end, self.right_end, *rest = tie(self.left_end, self.right_end, *others)
        return [self.end()] + rest


def tie(*values):
    return lax.optimization_barrier(values)


def halves_product(left, right, right_dim, count):
    middle = left.shape[0] // 2
    shape = (count // 2, left.shape[0] // count, right.shape[1 - right_dim])
    send = dot(left[middle:], right, 1, right_dim).astype(BF16).reshape(shape)
    send, first = tie(send, left[:middle])
    return dot(first, right, 1, right_dim).astype(BF16).reshape(shape), send


def small_sum(x, axes):
    count = axes_size(axes)
    if count > 8 or count & (count - 1):
        return lax.psum(x, axes)
    total = x
    for mask in range(1, count):
        total = total + swap(x, axes, mask)
    return total


def partner_sum(parts, axes):
    total = parts[0].astype(F32)
    for mask in range(1, len(parts)):
        total = total + swap(parts[mask], axes, mask).astype(F32)
    return total


def partner_spread(x, axes):
    return [swap(x, axes, mask) if mask else x for mask in range(axes_size(axes))]


def turn_spread(x, axes):
    return turn(jnp.broadcast_to(x, (axes_size(axes),) + x.shape), axes)


def turn_sum(parts, axes):
    return jnp.sum(turn(parts, axes).astype(F32), axis=0)


def turn(x, axes):
    return lax.all_to_all(x, axes, split_axis=0, concat_axis=0, tiled=False)


def on_device(
    tokens,
    positions,
    captions,
    caption_lengths,
    conditioning,
    modulation_weight,
    modulation_bias,
    attention_gain,
    query_weight,
    key_weight,
    value_weight,
    query_gain,
    key_gain,
    text_weight,
    textkey_weight,
    textvalue_weight,
    textkey_gain,
    cross_gate,
    output_weight,
    feedforward_gain,
    gate_weight,
    up_weight,
    down_weight,
    cotangent,
):
    wide_count, narrow_count = lax.axis_size(W), lax.axis_size(N)
    clip_count = lax.axis_size(C)
    clip_index, wide_index = lax.axis_index(C), lax.axis_index(W)
    own_rows, model_width = tokens.shape[1], tokens.shape[2]
    head_size = query_gain.shape[0]
    head_count = model_width // head_size
    score_scale = head_size ** (-0.5)
    score_shift = 3.0 * math.sqrt(head_size)
    split_tokens = head_count % (wide_count * narrow_count) != 0
    tp, dp = ((N,), (C, W)) if split_tokens else (PLANE, (C,))
    tp_count, dp_count = axes_size(tp), axes_size(dp)
    tp_index = lax.axis_index(tp)
    masks = [0, 1, 4, 5, 2, 3, 6, 7]
    order = (tp_index ^ jnp.array(masks, jnp.int32)).astype(jnp.int32)
    group_rows = own_rows * tp_count
    local_heads = head_count // tp_count
    head_width = local_heads * head_size
    weight_rows = query_weight.shape[0]
    hidden_rows, hidden_width = down_weight.shape[0], gate_weight.shape[1]
    local_hidden = hidden_width // tp_count

    text_rows, caption_rows = text_weight.shape[0], captions.shape[1]
    slot_count = caption_rows * narrow_count
    slot_part = slot_count // tp_count

    def gather_rows(rows):
        return lax.all_gather(rows, dp, axis=0, tiled=True)

    def scatter_rows(grads):
        return lax.psum_scatter(grads, dp, scatter_dimension=0, tiled=True)

    row_stack = gather_rows(jnp.concatenate([output_weight, text_weight], axis=0))
    row_stack = row_stack.reshape(dp_count, weight_rows + text_rows, model_width)

    cond_float = conditioning.astype(F32)
    cond_act = jax.nn.silu(cond_float)
    cond_rows = jnp.stack([pick(cond_act, clip_index ^ at) for at in range(clip_count)])
    weight_float = modulation_weight.astype(F32)
    partial_mod = jnp.dot(cond_rows, weight_float, precision=HIGHEST, preferred_element_type=F32)
    clip_mod = partner_sum([partial_mod[at] for at in range(clip_count)], (C,))

    head_parts_in = split_heads((textkey_weight, textvalue_weight, query_weight, key_weight, value_weight), tp_count)
    place_rows = jnp.stack([positions[0] // 64, positions[0] % 64]).astype(BF16)
    place_rows = jnp.pad(place_rows, ((0, 30), (0, model_width - own_rows)))
    bundle = jnp.concatenate([tokens[0], cotangent[0], place_rows], axis=0)
    head_parts_got, bundle = tie(turn(head_parts_in, tp), bundle)
    pieces, clip_mod = spread(bundle, tp, masks, clip_mod)
    hidden_in = split_groups((gate_weight, up_weight), tp_count, dp_count, hidden_rows)
    own_mod = small_sum(clip_mod, PLANE) + modulation_bias
    pieces[3], hidden_in, own_mod = tie(pieces[3], hidden_in, own_mod)
    shift_attn, scale_attn, gate_attn, shift_feed, scale_feed, gate_feed = jnp.split(own_mod, 6)
    hidden_parts = turn(hidden_in, tp)
    head_slice = gather_rows(head_parts_got.reshape(tp_count * weight_rows, 5 * head_width))
    text_slice, qkv_slice = head_slice[:, : 2 * head_width], head_slice[:, 2 * head_width :]

    caption_sent = take_columns(captions[0], tp_index ^ jnp.arange(narrow_count), narrow_count, dp_count, tp_count, text_rows)
    caption_got = [swap(part, (N,), at) if at else part for at, part in enumerate(caption_sent)]
    narrow_order = (lax.axis_index(N) ^ jnp.arange(narrow_count, dtype=jnp.int32)).astype(jnp.int32)
    caption_columns = place([part[None] for part in caption_got], narrow_order).reshape(slot_count, -1)

    mod_in, dfeed, tails = modulate(
        pieces, attention_gain * (1.0 + scale_attn), shift_attn, gate_feed, own_rows, own_rows
    )
    hidden_parts, mod_in = tie(hidden_parts, mod_in)
    feed_rows = [hidden_parts.reshape(tp_count * weight_rows, 2 * local_hidden), down_weight]
    feed_stack = gather_rows(jnp.concatenate([stack_columns(rows) for rows in feed_rows], axis=0))
    feed_stack = feed_stack.reshape(dp_count, -1, BLOCK)
    position_all = (tails[:, 0].astype(F32) * 64.0 + tails[:, 1].astype(F32)).reshape(group_rows)
    cosine, sine = rope_tables(position_all, head_size, 2 * head_size)
    head_gain = jnp.concatenate([jnp.tile(query_gain, local_heads), jnp.tile(key_gain, local_heads)])

    output_rows = row_stack[:, :weight_rows].reshape(dp_count * weight_rows, model_width)
    text_own_rows = row_stack[:, weight_rows:].reshape(-1, model_width)
    text_parts = dot(caption_columns, text_own_rows).astype(BF16).reshape(tp_count, slot_part, model_width)
    text_turned = turn(text_parts, tp)
    output_pieces = [
        piece.reshape(dp_count, weight_rows, model_width) for piece in spread(output_rows, tp, masks)
    ]
    output_full = place(output_pieces, order).reshape(model_width, model_width)

    qkv_raw = dot(mod_in, qkv_slice)
    text_turned, qkv_raw = tie(text_turned, qkv_raw)
    text_own = jnp.sum(text_turned.astype(F32), axis=0).astype(BF16)
    text_proj = turn_spread(text_own, tp).reshape(slot_count, model_width)
    heads, value_own = prepare(qkv_raw, cosine, sine, head_gain, head_size)
    if split_tokens:
        keys_all, key_base = lax.all_gather(heads[:, head_width:], W, axis=0, tiled=True), 0
        values_all = lax.all_gather(value_own, W, axis=0, tiled=True)
    else:
        keys_all, values_all, key_base = heads, value_own, head_width
    own_out, denom = attend(heads, keys_all, key_base, values_all, head_size)
    keep = (jnp.arange(slot_count) < caption_lengths[clip_index]).astype(F32)
    text_raw = dot(text_proj, text_slice)
    text_key, text_value = prepare_text(text_raw, textkey_gain, head_width)
    text_gate = pick(jnp.tanh(cross_gate).reshape(tp_count, local_heads), tp_index)
    gate_lanes = jnp.repeat(text_gate, head_size)
    mixed, cross_out, text_denom = attend_text(
        order, heads, text_key, text_value, keep, gate_lanes, own_out, head_size
    )

    token_float = tokens[0].astype(F32)
    inv_attn = inverse_rms(token_float)
    hat_attn = token_float * inv_attn
    normed_attn = hat_attn * attention_gain
    mixed_own = turn(mixed, tp).reshape(model_width, own_rows)
    attn_out = dot(mixed_own, output_full, 0, 0)
    resid = token_float + gate_attn * attn_out
    inv_feed = inverse_rms(resid)
    hat_feed = resid * inv_feed
    normed_feed = hat_feed * feedforward_gain
    mod_own = (normed_feed * (1.0 + scale_feed) + shift_feed).astype(BF16)

    mod_ff, inner, dhidden, hidden_slice, down_slice = feed(
        spread(mod_own, tp, masks), feed_stack, local_hidden, dfeed
    )
    dmod_sum = Collect(*halves_product(dhidden, hidden_slice, 1, tp_count), tp, masks)
    dmod_sum.keep, mod_ff, dhidden = tie(dmod_sum.keep, mod_ff, dhidden)
    dmod_sum.first()
    dhidden_grads = dot(mod_ff, dhidden, 0, 0).astype(BF16)
    (dhidden_grads,) = dmod_sum.tie_second(dhidden_grads)
    ddown_grads = dot(inner, dfeed, 0, 0).astype(BF16)
    dmod_ff, ddown_grads = dmod_sum.tie_end(ddown_grads)
    dhidden_rows = scatter_rows(dhidden_grads)
    down_rows = scatter_rows(ddown_grads)

    dout = cotangent[0].astype(F32)
    dshift_feed = jnp.sum(dmod_ff, axis=0)
    dscale_feed = jnp.sum(dmod_ff * normed_feed, axis=0)
    dfeed_gain, dresid_norm = norm_backward(
        hat_feed, inv_feed, feedforward_gain, dmod_ff * (1.0 + scale_feed)
    )
    dresid = dout + dresid_norm
    dgate_attn = jnp.sum(dresid * attn_out, axis=0)
    dattn = (gate_attn * dresid).astype(BF16)

    dmixed_own = dot(output_full, dattn, 1, 1).astype(BF16)
    dmixed_own, inner, mixed_own = tie(dmixed_own, inner, mixed_own)
    dmixed = turn(dmixed_own.reshape(tp_count, head_width, own_rows), tp)
    late_keep, late_send = late_parts(
        inner, down_slice, mixed_own.reshape(dp_count, tp_count, weight_rows, own_rows), dattn, order
    )
    dmixed, late_send = tie(dmixed, late_send)
    late_sum = Collect(late_keep, late_send, tp, masks)
    (dmixed,) = late_sum.tie_first(dmixed)
    late_sum.left[1], dmixed = tie(late_sum.left[1], dmixed)
    saved = (own_out, denom, cross_out, text_denom)
    dquery, dkey, dvalue, dtext_key, dtext_value, dgate_lanes = attend_back(
        order, heads, saved, dmixed, keys_all, key_base, values_all, text_key, text_value, keep, gate_lanes, head_size
    )
    dhidden_rows, dquery = tie(dhidden_rows, dquery)
    dhidden_parts = turn(dhidden_rows.reshape(tp_count, weight_rows, 2 * local_hidden), tp)
    (dquery,) = late_sum.tie_second(dquery)
    if split_tokens:
        dkey = lax.psum_scatter(dkey.astype(BF16), W, scatter_dimension=0, tiled=True)
        dvalue = lax.psum_scatter(dvalue.astype(BF16), W, scatter_dimension=0, tiled=True)
        dtext_key, dtext_value = lax.psum((dtext_key, dtext_value), W)
    dcross_gate = jnp.sum(dgate_lanes.reshape(local_heads, head_size), axis=1) * (1.0 - text_gate * text_gate)
    dqkv, dhead_gain, dtext_heads, dtkey_gain = finish(
        qkv_raw, dquery, dkey, dvalue, cosine, sine, head_gain, text_raw, dtext_key, dtext_value, textkey_gain
    )
    shared = 1.0 / wide_count if split_tokens else 1.0
    dhead_grads = head_grads(text_proj, dtext_heads, mod_in, dqkv, shared)
    dhead_grads, dqkv, dtext_heads, dhidden_parts = tie(dhead_grads, dqkv, dtext_heads, dhidden_parts)
    dhead_rows = scatter_rows(dhead_grads)

    dtext_parts = dot(dtext_heads, text_slice, 1, 1).astype(BF16).reshape(tp_count, slot_part, model_width)
    dtext_parts, dqkv = tie(dtext_parts, dqkv)
    dtext_turned = turn(dtext_parts, tp)
    middle = group_rows // 2
    shape = (tp_count // 2, own_rows, model_width)
    din_send = dot(dqkv[middle:], qkv_slice, 1, 1).astype(BF16).reshape(shape)
    din_send, dqkv = tie(din_send, dqkv)
    din_sum = Collect(dot(dqkv[:middle], qkv_slice, 1, 1).astype(BF16).reshape(shape), din_send, tp, masks)
    din_sum.first()
    dtext_turned, din_sum.left[1] = tie(dtext_turned, din_sum.left[1])
    dtext_own = jnp.sum(dtext_turned.astype(F32), axis=0).astype(BF16)
    late_own, dtext_own = late_sum.tie_end(dtext_own)
    dtext_all = turn_spread(dtext_own, tp).reshape(slot_count, model_width)
    feed_out, dout_group = late_own[:own_rows], late_own[own_rows:].astype(BF16)
    block_output = resid + gate_feed * feed_out
    dgate_feed = jnp.sum(dout * feed_out, axis=0)
    (dgate_feed,) = din_sum.tie_second(dgate_feed)
    dtext_grads = (dot(caption_columns, dtext_all, 0, 0) * shared).astype(BF16)
    dcaption = dot(dtext_all, text_own_rows, 1, 1).astype(BF16)
    dmod_in, dtext_grads, dcaption, down_rows = din_sum.tie_end(dtext_grads, dcaption, down_rows)
    dtext_rows = scatter_rows(dtext_grads)
    downweight_grad = to_float(down_rows)

    dshift_attn = jnp.sum(dmod_in, axis=0)
    dscale_attn = jnp.sum(dmod_in * normed_attn, axis=0)
    dattn_gain, dtokens_norm = norm_backward(
        hat_attn, inv_attn, attention_gain, dmod_in * (1.0 + scale_attn)
    )
    tokens_grad = dresid + dtokens_norm
    block_output = resid + gate_feed * feed_out
    dgate_feed = jnp.sum(dout * feed_out, axis=0)
    head_range = jnp.arange(head_count) - tp_index * local_heads
    dgate_rows = jnp.sum(
        jnp.where(head_range[:, None] == jnp.arange(local_heads)[None, :], dcross_gate[None, :], 0.0), axis=1
    )
    dgains = jnp.sum(dhead_gain.reshape(2, local_heads, head_size), axis=1)
    pad = -head_count % head_size
    small = jnp.concatenate(
        [
            dshift_attn,
            dscale_attn,
            dgate_attn,
            dshift_feed,
            dscale_feed,
            dgate_feed,
            dattn_gain,
            dfeed_gain,
            dgains[0],
            dgains[1],
            dtkey_gain[0] * shared,
            dgate_rows,
            jnp.zeros((pad,), F32),
        ]
    )
    dcaption = dcaption.reshape(narrow_count, caption_rows, -1)
    if not split_tokens:
        narrow_index = lax.axis_index(N)
        own_parts = [pick(dcaption, narrow_index ^ at) for at in range(narrow_count)]
        dcaption = jnp.stack([swap(part, (N,), at) if at else part for at, part in enumerate(own_parts)])
    plane_small, dcaption, dhead_rows = tie(small_sum(small, PLANE), dcaption, dhead_rows)
    dhead_parts = turn(dhead_rows.reshape(tp_count, weight_rows, 5 * head_width), tp)
    clip_small = jnp.stack(partner_spread(plane_small, (C,)))
    dout_group = dout_group.reshape(dp_count, weight_rows, model_width)
    if split_tokens:
        outweight_grad = lax.psum_scatter(dout_group, dp, scatter_dimension=0, tiled=False).astype(F32)
    else:
        outs = [pick(dout_group, clip_index ^ at) for at in range(dp_count)]
        outs = [outs[0]] + [swap(outs[at], dp, at) for at in range(1, dp_count)]
        *outs, clip_small = tie(*outs, clip_small)
        outweight_grad = functools.reduce(jnp.add, [out.astype(F32) for out in outs])
    mod_width = 6 * model_width
    dmod_all = clip_small[:, :mod_width]
    gains = jnp.sum(clip_small[:, mod_width:], axis=0)
    attngain_grad, feedgain_grad = gains[:model_width], gains[model_width : 2 * model_width]
    rest = gains[2 * model_width :]
    querygain_grad, keygain_grad, textgain_grad = (
        rest[:head_size],
        rest[head_size : 2 * head_size],
        rest[2 * head_size : 3 * head_size],
    )
    crossgate_grad = rest[3 * head_size : 3 * head_size + head_count]
    modweight_grad = jnp.dot(cond_rows.T, dmod_all, precision=HIGHEST, preferred_element_type=F32)
    dcond_rows = jnp.dot(dmod_all, weight_float.T, precision=HIGHEST, preferred_element_type=F32)
    dcond_act = jnp.stack([pick(dcond_rows, clip_index ^ at) for at in range(clip_count)])
    sigmoid_cond = jax.nn.sigmoid(cond_float)
    conditioning_grad = dcond_act * sigmoid_cond * (1.0 + cond_float * (1.0 - sigmoid_cond))
    modbias_grad = jnp.sum(dmod_all, axis=0)

    if split_tokens:
        captions_grad = join_groups(turn(dcaption, tp), dp_count, text_rows, 1)[0]
    else:
        far_parts = swap(dcaption, (W,), 2)
        wide_parts = [dcaption, far_parts, swap(dcaption, (W,), 1), swap(far_parts, (W,), 1)]
        wide_order = wide_index ^ jnp.array([0, 2, 1, 3], jnp.int32)
        captions_grad = join_captions(wide_parts, wide_order.astype(jnp.int32), narrow_order, dp_count, wide_count)

    gateweight_grad, upweight_grad = join_groups(dhidden_parts, dp_count, hidden_rows, 2)
    head_results = join_heads(dhead_parts, head_width)
    textvalue_grad, dtext_rows = tie(head_results[1], dtext_rows)
    textkey_grad, _, queryweight_grad, keyweight_grad, valueweight_grad = head_results
    textweight_grad = to_float(dtext_rows)
    return (
        block_output[None],
        tokens_grad[None],
        captions_grad[None],
        conditioning_grad,
        modweight_grad,
        modbias_grad,
        attngain_grad,
        queryweight_grad,
        keyweight_grad,
        valueweight_grad,
        querygain_grad,
        keygain_grad,
        textweight_grad,
        textkey_grad,
        textvalue_grad,
        textgain_grad,
        crossgate_grad,
        outweight_grad,
        feedgain_grad,
        gateweight_grad,
        upweight_grad,
        downweight_grad,
    )


def solution(mesh):
    rows, whole = P(ALL, None), P()
    tokens, captions = P(C, PLANE, None), P(C, N, None)
    columns = P(None, ALL)
    return jax.shard_map(
        on_device,
        mesh=mesh,
        in_specs=(
            tokens,
            P(C, PLANE),
            captions,
            whole,
            columns,
            rows,
            whole,
            whole,
            rows,
            rows,
            rows,
            whole,
            whole,
            rows,
            rows,
            rows,
            whole,
            whole,
            rows,
            whole,
            rows,
            rows,
            rows,
            tokens,
        ),
        out_specs=(
            tokens,
            tokens,
            captions,
            columns,
            rows,
            whole,
            whole,
            rows,
            rows,
            rows,
            whole,
            whole,
            rows,
            rows,
            rows,
            whole,
            whole,
            rows,
            whole,
            rows,
            rows,
            rows,
        ),
        check_vma=False,
    )
```
